128 devices in a mesh: table: 8 (over y, core), ray: 16 (over x, z).
Axes of the slice: x: 4, y: 4, z: 4, core: 2. Of those that a mesh axis runs over, the one named last changes fastest.
Arguments:
- table: float32 [2, 8192, 4, 512], P(None, ('table', 'ray')), may hold values from -6 to 6
- moment1: float32 [2, 8192, 4, 512], P(None, ('table', 'ray')), may hold values from -2 to 2
- moment2: float32 [2, 8192, 4, 512], P(None, ('table', 'ray')), may hold values from 0.01 to 1
- block_ids: int32 [8, 2, 128, 4], replicated, may hold values from 0 to 63, as said below
- sample_slot: int32 [2, 65536], P(None, ('table', 'ray')), may hold values from 0 to 511, as said below
- corners: int32 [2, 8, 65536], P(None, None, ('table', 'ray')), may hold values from 0 to 511
- fractions: float32 [2, 3, 65536], P(None, None, ('table', 'ray')), may hold values from 0 to 1
- feat_cot: float32 [2, 4, 65536], P(None, None, ('table', 'ray')), may hold values from -24 to 24
- weight_in: float32 [64, 8], replicated, may hold values from -2 to 2
- weight_out: float32 [16, 64], replicated, may hold values from -0.75 to 0.75
Outputs:
- table_new: float32 [2, 8192, 4, 512], P(None, ('table', 'ray'))
- moment1_new: float32 [2, 8192, 4, 512], P(None, ('table', 'ray'))
- moment2_new: float32 [2, 8192, 4, 512], P(None, ('table', 'ray'))
- mlp_out: float32 [16, 65536], P(None, ('table', 'ray'))
The draws below stay inside these ranges and needn't reach their ends.
Inputs may be any that keep to these rules, and one draw needn't show every extreme that they name: `block_ids`: for every group, level and owner the 4 listed blocks are distinct local block numbers of that owner. `sample_slot`: each device's 512 samples of a level come in 16 runs of 512 // 16 in order; the samples of run i read only blocks of owners o with o % 16 == i.
All inputs are finite; a program needn't handle non-finite values.
Results may differ from the reference program's by a relative error of at most 0.000075.
Values sent between devices are 32-bit elements; how exact they have to be, the bound alone decides.
No kernel may reach another device: no remote copies, remote signals or barrier semaphores. Data moves between devices by JAX's collectives and lax.ppermute only.
A program may use at most 64 MiB of HBM per device.

```python
import math
import jax
import jax.numpy as jnp
from jax import lax

LEV = 2
BLK = 512
SLOTS = 4
S_DEV = 512
HID = 64
OUT = 16
NBLOCKS = 8192
BLKS_DEV = 64
SAMPLES = 65536
FEAT_IN = 8
N_TABLE = 8
N_RAY = 16
DEVICES = 128


def draw_block_ids(key, part):
    scores = jax.random.randint(key, (N_TABLE, LEV, DEVICES, BLKS_DEV), 0, 1 << 20, dtype=jnp.int32)
    scores = scores * BLKS_DEV + jnp.arange(BLKS_DEV, dtype=jnp.int32)
    picked = lax.top_k(scores, SLOTS)[1]
    return picked.astype(jnp.int32)


def draw_sample_slot(key, part):
    key_table = jax.random.fold_in(key, 11)
    key_slot = jax.random.fold_in(key, 23)
    table_pick = jax.random.randint(key_table, (LEV, SAMPLES), 0, N_TABLE, dtype=jnp.int32)
    slot_pick = jax.random.randint(key_slot, (LEV, SAMPLES), 0, SLOTS, dtype=jnp.int32)
    position = jnp.arange(SAMPLES, dtype=jnp.int32)[None, :]
    ray_pick = position % S_DEV // (S_DEV // N_RAY)
    first = position == 0
    last = position == SAMPLES - 1
    table_pick = jnp.where(first, 0, jnp.where(last, N_TABLE - 1, table_pick))
    slot_pick = jnp.where(first, 0, jnp.where(last, SLOTS - 1, slot_pick))
    result = (table_pick * N_RAY + ray_pick) * SLOTS + slot_pick
    return result.astype(jnp.int32)


def place_ends(values, own_key, smallest, largest):
    extent = values.shape
    index_at = [jax.random.randint(jax.random.fold_in(own_key, axis), (), 0, extent[axis]) for axis in range(len(extent))]
    values = values.at[tuple(index_at)].set(smallest)
    longest = extent.index(max(extent))
    index_at[longest] = (index_at[longest] + 1) % extent[longest]
    return values.at[tuple(index_at)].set(largest)


def steps_of(key, shape, pieces, smallest, largest):
    factor_of = 1.0
    for dim, shards_of in pieces:
        draws = jax.random.uniform(jax.random.fold_in(jax.random.fold_in(key, 6), dim), (shards_of,), jnp.float32, smallest / len(pieces), largest / len(pieces))
        factor_of = factor_of * jnp.repeat(jnp.exp(draws), shape[dim] // shards_of).reshape((-1,) + (1,) * (len(shape) - 1 - dim))
    return factor_of


def noise(stream_key, shape, scale, reach, pieces=(), kind=jnp.bfloat16):
    values = scale * jax.random.normal(stream_key, shape, jnp.float32)
    if pieces:
        values = values * steps_of(stream_key, shape, pieces, -0.22, 0.18)
    return jnp.clip(values, -reach, reach).astype(kind)


def setup_inputs(seed: int = 0) -> dict:
    key_of = jax.random.split(jax.random.key(seed), 11)
    return {
        "table": noise(key_of[0], (LEV, NBLOCKS, 4, BLK), 1.0, 6.0, ((1, 128),), jnp.float32),
        "moment1": noise(key_of[1], (LEV, NBLOCKS, 4, BLK), 0.3, 2.0, ((1, 128),), jnp.float32),
        "moment2": jnp.clip(jnp.exp(math.log(1.0) - 4.6051702 * jax.random.uniform(key_of[2], (LEV, NBLOCKS, 4, BLK), jnp.float32) ** steps_of(key_of[2], (LEV, NBLOCKS, 4, BLK), ((1, 128),), -0.2, 0.2)), 0.01, 1.0),
        "block_ids": draw_block_ids(jax.random.fold_in(key_of[10], 71), 0),
        "sample_slot": draw_sample_slot(jax.random.fold_in(key_of[10], 71), 0),
        "corners": place_ends(jax.random.randint(key_of[5], (LEV, 8, SAMPLES), 0, BLK), jax.random.fold_in(key_of[5], 1), 0, BLK - 1).astype(jnp.int32),
        "fractions": jnp.clip(1.0 * jax.random.uniform(key_of[6], (LEV, 3, SAMPLES), jnp.float32) ** steps_of(key_of[6], (LEV, 3, SAMPLES), ((2, 128),), -0.2, 0.2), 0.0, 1.0),
        "feat_cot": noise(key_of[7], (LEV, 4, SAMPLES), 4.0, 24.0, ((2, 128),), jnp.float32),
        "weight_in": noise(key_of[8], (HID, FEAT_IN), FEAT_IN ** -0.5, 2.0, (), jnp.float32),
        "weight_out": noise(key_of[9], (OUT, HID), HID ** -0.5, 0.75, (), jnp.float32),
    }


def hat_weights(fractions):
    columns = []
    for corner in range(8):
        weight = jnp.ones_like(fractions[:, 0, :])
        for dimension in range(3):
            if corner >> dimension & 1:
                weight = weight * fractions[:, dimension, :]
            else:
                weight = weight * (1.0 - fractions[:, dimension, :])
        columns.append(weight)
    return jnp.stack(columns, axis=1)

def reference(table, moment1, moment2, block_ids, sample_slot, corners, fractions, feat_cot, weight_in, weight_out):
    group_of = jnp.arange(SAMPLES, dtype=jnp.int32) // (S_DEV * N_RAY)
    owner = sample_slot // SLOTS
    within = sample_slot % SLOTS
    level_index = jnp.arange(LEV, dtype=jnp.int32)[:, None]
    local_block = block_ids[group_of[None, :], level_index, owner, within]
    global_block = owner * BLKS_DEV + local_block
    feature_index = jnp.arange(4, dtype=jnp.int32)[None, None, :, None]
    flat_index = (global_block[:, None, None, :] * 4 + feature_index) * BLK + corners[:, :, None, :]
    weights = hat_weights(fractions)
    contrib = weights[:, :, None, :] * feat_cot[:, None, :, :]
    level_full = jnp.arange(LEV, dtype=jnp.int32)[:, None, None, None]
    gradient = jnp.zeros((LEV, NBLOCKS * 4 * BLK), table.dtype).at[level_full, flat_index].add(contrib)
    gradient = gradient.reshape(table.shape)
    first_new = 0.9 * moment1 + 0.1 * gradient
    second_new = 0.99 * moment2 + 0.01 * gradient * gradient
    table_new = table - 0.01 * first_new / (jnp.sqrt(second_new) + 1e-15)
    values = table_new.reshape(LEV, -1)[level_full, flat_index]
    encoded = lax.optimization_barrier(jnp.sum(weights[:, :, None, :] * values, axis=1)).reshape(4 * LEV, SAMPLES)
    hidden = jax.nn.relu(jnp.dot(weight_in, encoded, precision=lax.Precision.HIGHEST))
    mlp_out = jnp.dot(weight_out, hidden, precision=lax.Precision.HIGHEST)
    return (table_new, first_new, second_new, mlp_out)
```

```python
import jax
import jax.numpy as jnp
from jax import lax
from jax.experimental import pallas as pl
from jax.experimental.pallas import tpu as pltpu
from jax.sharding import PartitionSpec as P

beta_one = 0.9
beta_two = 0.99
learn_rate = 0.01
adam_eps = 1e-15

LANES = 128
RUN = 32
VMEM_LIMIT = 48 << 20


def block_transpose(pieces):
    group = lax.broadcasted_iota(jnp.int32, pieces[0].shape, 1) // RUN
    results = []
    for q in range(4):
        value = pieces[q]
        for p in range(4):
            if p != q:
                moved = pltpu.roll(pieces[p], (RUN * (p - q)) % LANES, 1)
                value = jnp.where(group == p, moved, value)
        results.append(value)
    return results


def split_two(value):
    high = value.astype(jnp.bfloat16)
    low = (value - high.astype(jnp.float32)).astype(jnp.bfloat16)
    return high, low


def pack_kernel(slot_ref, corners_ref, fractions_ref, cot_ref, out_ref):
    groups = [corners_ref[0].astype(jnp.float32), corners_ref[1].astype(jnp.float32)]
    for level in range(2):
        rows = [slot_ref[level : level + 1, :].astype(jnp.float32)]
        rows += [fractions_ref[d, level : level + 1, :] for d in range(3)]
        rows += [cot_ref[level]]
        groups.append(jnp.concatenate(rows, axis=0))
    for v in range(4):
        lanes = slice(v * LANES, (v + 1) * LANES)
        for p, value in enumerate(block_transpose([g[:, lanes] for g in groups])):
            out_ref[4 * v + p] = value


def grad_kernel(recv_ref, part_ref, high_ref, low_ref, cand_ref, corner_s, aux_s):
    for v in range(4):
        lanes = slice(v * LANES, (v + 1) * LANES)
        rows = block_transpose([recv_ref[4 * v + p] for p in range(4)])
        for level in range(2):
            corner_s[level, :, lanes] = rows[level].astype(jnp.int32)
            aux_s[level, :, lanes] = rows[2 + level]
    for level in range(2):
        aux = aux_s[level]
        sub = lax.broadcasted_iota(jnp.int32, (8, 512), 0)
        hat = None
        for d in range(3):
            f = jnp.broadcast_to(aux[1 + d : 2 + d], (8, 512))
            factor = jnp.where((sub >> d) & 1 == 1, f, 1.0 - f)
            hat = factor if hat is None else hat * factor
        slot = aux[0:1].astype(jnp.int32)
        cand = (slot // 64) * 4 + slot % 4
        cand_ref[level : level + 1, :] = cand
        for v in range(4):
            lanes = slice(v * LANES, (v + 1) * LANES)
            corner = corner_s[level, :, lanes]
            hat_v = hat[:, lanes]
            corner_b = [jnp.broadcast_to(corner[c : c + 1], (16, LANES)) for c in range(8)]
            hat_b = [jnp.broadcast_to(hat_v[c : c + 1], (16, LANES)) for c in range(8)]
            base = lax.broadcasted_iota(jnp.int32, (16, LANES), 0)

            def tile(step, carry):
                start = pl.multiple_of(step * 16, 16)
                entry = base + start
                total = jnp.where(corner_b[0] == entry, hat_b[0], 0.0)
                for c in range(1, 8):
                    total = total + jnp.where(corner_b[c] == entry, hat_b[c], 0.0)
                high, low = split_two(total)
                high_ref[level, pl.ds(start, 16), lanes] = high
                low_ref[level, pl.ds(start, 16), lanes] = low
                return carry

            lax.fori_loop(0, 32, tile, 0, unroll=4)
        cot = jnp.concatenate([aux[4:8]] * 32, axis=0)
        row = lax.broadcasted_iota(jnp.int32, (128, 512), 0) // 4
        scaled = jnp.where(cand == row, cot, 0.0)
        s_high, s_low = split_two(scaled)
        high = high_ref[level]
        contract = (((1,), (1,)), ((), ()))
        both = lax.dot_general(
            jnp.concatenate([s_high, s_low], axis=0), high, contract, preferred_element_type=jnp.float32
        )
        rest = lax.dot_general(s_high, low_ref[level], contract, preferred_element_type=jnp.float32)
        part = both[:128] + both[128:] + rest
        for t in range(8):
            part_ref[t, level] = part[16 * t : 16 * t + 16]


def adam_kernel(ids_ref, recv_ref, table_ref, m1_ref, m2_ref, tnew_ref, m1new_ref, m2new_ref, pick_ref, grad_s, *, ray):
    owner = lax.axis_index("table") * ray + lax.axis_index("ray")
    sub = lax.broadcasted_iota(jnp.int32, (8, LANES), 0) < 4
    grad_s[...] = jnp.zeros_like(grad_s)
    for g in range(8):
        for level in range(2):
            for pair in range(2):
                a = [recv_ref[g, level, 8 * pair : 8 * pair + 8, c * LANES : (c + 1) * LANES] for c in range(4)]
                for half in range(2):
                    row = (g * 2 + level) * 4 + 2 * pair + half
                    block = level * 64 + ids_ref[row, owner]
                    for k in range(2):
                        x, y = a[2 * k], a[2 * k + 1]
                        if half == 0:
                            value = jnp.where(sub, x, pltpu.roll(y, 4, 0))
                        else:
                            value = jnp.where(sub, pltpu.roll(x, 4, 0), y)
                        grad_s[block, 8 * k : 8 * k + 8, :] += value

    def update(step, carry):
        at = pl.ds(step * 4, 4)
        grad = grad_s[at]
        first = beta_one * m1_ref[at] + (1.0 - beta_one) * grad
        second = beta_two * m2_ref[at] + (1.0 - beta_two) * grad * grad
        m1new_ref[at] = first
        m2new_ref[at] = second
        tnew_ref[at] = table_ref[at] - learn_rate * first / (jnp.sqrt(second) + adam_eps)
        return carry

    lax.fori_loop(0, 32, update, 0)
    for g in range(8):
        for level in range(2):
            for pair in range(2):
                row = (g * 2 + level) * 4 + 2 * pair
                one = level * 64 + ids_ref[row, owner]
                two = level * 64 + ids_ref[row + 1, owner]
                for k in range(2):
                    x = tnew_ref[one, 8 * k : 8 * k + 8, :]
                    y = tnew_ref[two, 8 * k : 8 * k + 8, :]
                    pick_ref[g, level, 8 * pair : 8 * pair + 8, 2 * k * LANES : (2 * k + 1) * LANES] = jnp.where(
                        sub, x, pltpu.roll(y, 4, 0)
                    )
                    pick_ref[g, level, 8 * pair : 8 * pair + 8, (2 * k + 1) * LANES : (2 * k + 2) * LANES] = jnp.where(
                        sub, pltpu.roll(x, 4, 0), y
                    )


def lookup_kernel(recv_ref, high_ref, low_ref, cand_ref, win_ref, wout_ref, out_ref):
    rows = []
    for level in range(2):
        blocks = recv_ref[:, level].reshape(128, 512)
        b_high, b_low = split_two(blocks)
        both = jnp.dot(
            jnp.concatenate([b_high, b_low], axis=0), high_ref[level], preferred_element_type=jnp.float32
        )
        rest = jnp.dot(b_high, low_ref[level], preferred_element_type=jnp.float32)
        looked = both[:128] + both[128:] + rest
        row = lax.broadcasted_iota(jnp.int32, (128, 512), 0) // 4
        kept = jnp.where(cand_ref[level : level + 1, :] == row, looked, 0.0)
        folded = jnp.sum(kept.reshape(16, 8, 512), axis=0)
        rows.append(folded[:4] + folded[4:])
    encoded = jnp.concatenate(rows, axis=0)
    hidden = jnp.maximum(
        lax.dot_general(
            win_ref[...], encoded, (((0,), (0,)), ((), ())),
            precision=lax.Precision.HIGHEST, preferred_element_type=jnp.float32,
        ),
        0.0,
    )
    out = jnp.dot(wout_ref[...], hidden, precision=lax.Precision.HIGHEST, preferred_element_type=jnp.float32)
    low_lanes = lax.broadcasted_iota(jnp.int32, (8, LANES), 1) < RUN
    for v in range(4):
        upper = out[:8, v * LANES : (v + 1) * LANES]
        lower = out[8:, v * LANES : (v + 1) * LANES]
        for p in range(4):
            x = pltpu.roll(upper, (-RUN * p) % LANES, 1) if p else upper
            y = pltpu.roll(lower, (RUN - RUN * p) % LANES, 1) if p != 1 else lower
            out_ref[4 * v + p] = jnp.where(low_lanes, x, y)


def unpack_kernel(recv_ref, out_ref):
    group = lax.broadcasted_iota(jnp.int32, (8, LANES), 1) // RUN
    for v in range(4):
        upper = lower = None
        for p in range(4):
            piece = recv_ref[4 * v + p]
            x = pltpu.roll(piece, RUN * p, 1) if p else piece
            y = pltpu.roll(piece, (RUN * p - RUN) % LANES, 1) if p != 1 else piece
            upper = x if upper is None else jnp.where(group == p, x, upper)
            lower = y if lower is None else jnp.where(group == p, y, lower)
        out_ref[:8, v * LANES : (v + 1) * LANES] = upper
        out_ref[8:, v * LANES : (v + 1) * LANES] = lower


def call(kernel, outs, scratch=(), in_specs=None):
    vmem = pl.BlockSpec(memory_space=pltpu.VMEM)
    shapes = [jax.ShapeDtypeStruct(s, d) for s, d in outs]
    single = len(shapes) == 1
    extra = {} if in_specs is None else {"in_specs": in_specs}
    return pl.pallas_call(
        kernel,
        out_shape=shapes[0] if single else shapes,
        out_specs=vmem if single else [vmem] * len(shapes),
        scratch_shapes=list(scratch),
        compiler_params=pltpu.CompilerParams(vmem_limit_bytes=VMEM_LIMIT),
        **extra,
    )


def exchange(value, axis):
    return lax.all_to_all(value, axis, split_axis=0, concat_axis=0, tiled=True)


def rows_of(array):
    levels, blocks = array.shape[:2]
    return array.reshape(levels, blocks, 4, 4, LANES).transpose(0, 1, 3, 2, 4).reshape(levels * blocks, 16, LANES)


def rows_back(array, shape):
    levels, blocks = shape[:2]
    return array.reshape(levels, blocks, 4, 4, LANES).transpose(0, 1, 3, 2, 4).reshape(shape)


def on_device(
    table,
    moment1,
    moment2,
    block_ids,
    sample_slot,
    corners,
    fractions,
    feat_cot,
    weight_in,
    weight_out,
):
    f32, bf16, i32 = jnp.float32, jnp.bfloat16, jnp.int32
    ray = lax.axis_size("ray")
    packed = call(pack_kernel, [((16, 8, LANES), f32)])(
        sample_slot, corners, fractions.transpose(1, 0, 2), feat_cot
    )
    samples = exchange(packed, "ray")
    part, high, low, cand = call(
        grad_kernel,
        [((8, 2, 16, 512), f32), ((2, 512, 512), bf16), ((2, 512, 512), bf16), ((2, 512), i32)],
        [pltpu.VMEM((2, 8, 512), i32), pltpu.VMEM((2, 8, 512), f32)],
    )(samples)
    received = exchange(part, "table")
    ids = block_ids.transpose(0, 1, 3, 2).reshape(64, 128)
    vmem = pl.BlockSpec(memory_space=pltpu.VMEM)
    rows = (128, 16, LANES)

    def adam(*refs):
        adam_kernel(*refs, ray=ray)

    tnew, m1new, m2new, picked = call(
        adam,
        [(rows, f32), (rows, f32), (rows, f32), ((8, 2, 16, 512), f32)],
        [pltpu.VMEM(rows, f32)],
        [pl.BlockSpec(memory_space=pltpu.SMEM)] + [vmem] * 4,
    )(ids, received, rows_of(table), rows_of(moment1), rows_of(moment2))
    returned = exchange(picked, "table")
    sent = call(lookup_kernel, [((16, 8, LANES), f32)])(
        returned, high, low, cand, weight_in.T, weight_out
    )
    back = exchange(sent, "ray")
    mlp_out = call(unpack_kernel, [((16, 512), f32)])(back)
    shape = table.shape
    return (rows_back(tnew, shape), rows_back(m1new, shape), rows_back(m2new, shape), mlp_out)


def solution(mesh):
    in_specs = (
        P(None, ("table", "ray"), None, None),
        P(None, ("table", "ray"), None, None),
        P(None, ("table", "ray"), None, None),
        P(),
        P(None, ("table", "ray")),
        P(None, None, ("table", "ray")),
        P(None, None, ("table", "ray")),
        P(None, None, ("table", "ray")),
        P(),
        P(),
    )
    out_specs = (
        P(None, ("table", "ray"), None, None),
        P(None, ("table", "ray"), None, None),
        P(None, ("table", "ray"), None, None),
        P(None, ("table", "ray")),
    )
    return jax.shard_map(
        on_device, mesh=mesh, in_specs=in_specs, out_specs=out_specs, check_vma=False
    )
```

```python
import jax
import jax.numpy as jnp
from jax import lax
from jax.experimental import pallas as pl
from jax.experimental.pallas import tpu as pltpu
from jax.sharding import PartitionSpec as P

beta_one = 0.9
beta_two = 0.99
learn_rate = 0.01
adam_eps = 1e-15

LANES = 128
RUN = 32
VMEM_LIMIT = 24 << 20


def block_transpose(pieces):
    group = lax.broadcasted_iota(jnp.int32, pieces[0].shape, 1) // RUN
    results = []
    for q in range(4):
        value = pieces[q]
        for p in range(4):
            if p != q:
                moved = pltpu.roll(pieces[p], (RUN * (p - q)) % LANES, 1)
                value = jnp.where(group == p, moved, value)
        results.append(value)
    return results


def split_two(value):
    high = value.astype(jnp.bfloat16)
    low = (value - high.astype(jnp.float32)).astype(jnp.bfloat16)
    return high, low


def pack_kernel(slot_hbm, corners_hbm, fractions_hbm, cot_hbm, out_ref, slot_ref, corners_ref, fractions_ref, cot_ref, sems):
    sources = (slot_hbm, corners_hbm, fractions_hbm, cot_hbm)
    targets = (slot_ref, corners_ref, fractions_ref, cot_ref)
    copies = [pltpu.make_async_copy(x, y, sems.at[n]) for n, (x, y) in enumerate(zip(sources, targets))]
    for copy in copies:
        copy.start()
    for copy in copies:
        copy.wait()
    groups = [corners_ref[0].astype(jnp.float32), corners_ref[1].astype(jnp.float32)]
    for level in range(2):
        rows = [slot_ref[level : level + 1, :].astype(jnp.float32)]
        rows += [fractions_ref[d, level : level + 1, :] for d in range(3)]
        rows += [cot_ref[level]]
        groups.append(jnp.concatenate(rows, axis=0))
    for v in range(4):
        lanes = slice(v * LANES, (v + 1) * LANES)
        for p, value in enumerate(block_transpose([g[:, lanes] for g in groups])):
            out_ref[4 * v + p] = value


def grad_kernel(
    recv_ref, table_hbm, m1_hbm, m2_hbm, win_hbm, wout_hbm,
    part_ref, high_ref, low_ref, cand_ref, table_ref, m1_ref, m2_ref, win_ref, wout_ref, corner_s, aux_s, sems,
):
    sources = (table_hbm, m1_hbm, m2_hbm, win_hbm, wout_hbm)
    targets = (table_ref, m1_ref, m2_ref, win_ref, wout_ref)
    copies = [pltpu.make_async_copy(x, y, sems.at[n]) for n, (x, y) in enumerate(zip(sources, targets))]
    for copy in copies:
        copy.start()
    for v in range(4):
        lanes = slice(v * LANES, (v + 1) * LANES)
        rows = block_transpose([recv_ref[4 * v + p] for p in range(4)])
        for level in range(2):
            corner_s[level, :, lanes] = rows[level].astype(jnp.int32)
            aux_s[level, :, lanes] = rows[2 + level]
    for level in range(2):
        aux = aux_s[level]
        sub = lax.broadcasted_iota(jnp.int32, (8, 512), 0)
        hat = None
        for d in range(3):
            f = jnp.broadcast_to(aux[1 + d : 2 + d], (8, 512))
            factor = jnp.where((sub >> d) & 1 == 1, f, 1.0 - f)
            hat = factor if hat is None else hat * factor
        slot = aux[0:1].astype(jnp.int32)
        cand = (slot // 64) * 4 + slot % 4
        cand_ref[level : level + 1, :] = cand
        for v in range(4):
            lanes = slice(v * LANES, (v + 1) * LANES)
            corner = corner_s[level, :, lanes]
            hat_v = hat[:, lanes]
            corner_b = [jnp.broadcast_to(corner[c : c + 1], (16, LANES)) for c in range(8)]
            hat_b = [jnp.broadcast_to(hat_v[c : c + 1], (16, LANES)) for c in range(8)]
            base = lax.broadcasted_iota(jnp.int32, (16, LANES), 0)

            def tile(step, carry):
                start = pl.multiple_of(step * 16, 16)
                entry = base + start
                total = jnp.where(corner_b[0] == entry, hat_b[0], 0.0)
                for c in range(1, 8):
                    total = total + jnp.where(corner_b[c] == entry, hat_b[c], 0.0)
                high, low = split_two(total)
                high_ref[level, pl.ds(start, 16), lanes] = high
                low_ref[level, pl.ds(start, 16), lanes] = low
                return carry

            lax.fori_loop(0, 32, tile, 0, unroll=4)
        cot = jnp.concatenate([aux[4:8]] * 32, axis=0)
        row = lax.broadcasted_iota(jnp.int32, (128, 512), 0) // 4
        scaled = jnp.where(cand == row, cot, 0.0)
        s_high, s_low = split_two(scaled)
        high = high_ref[level]
        contract = (((1,), (1,)), ((), ()))
        both = lax.dot_general(
            jnp.concatenate([s_high, s_low], axis=0), high, contract, preferred_element_type=jnp.float32
        )
        rest = lax.dot_general(s_high, low_ref[level], contract, preferred_element_type=jnp.float32)
        part = both[:128] + both[128:] + rest
        for t in range(8):
            part_ref[t, level] = part[16 * t : 16 * t + 16]
    for copy in copies:
        copy.wait()


def moments(grad, m1, m2):
    first = beta_one * m1 + (1.0 - beta_one) * grad
    second = beta_two * m2 + (1.0 - beta_two) * grad * grad
    return first, second


def stepped(table, first, second):
    return table - learn_rate * first / (jnp.sqrt(second) + adam_eps)


def listed_kernel(ids_ref, recv_ref, table_ref, m1_ref, m2_ref, pick_ref, grad_ref, *, ray):
    owner = lax.axis_index("table") * ray + lax.axis_index("ray")
    sub = lax.broadcasted_iota(jnp.int32, (8, LANES), 0) < 4
    grad_ref[...] = jnp.zeros_like(grad_ref)
    blocks = {}
    for g in range(8):
        for level in range(2):
            for slot in range(4):
                blocks[g, level, slot] = level * 64 + ids_ref[(g * 2 + level) * 4 + slot, owner]
    for g in range(8):
        for level in range(2):
            for pair in range(2):
                rows = slice(8 * pair, 8 * pair + 8)
                a = [recv_ref[g, level, rows, c * LANES : (c + 1) * LANES] for c in range(4)]
                for half in range(2):
                    block = blocks[g, level, 2 * pair + half]
                    for k in range(2):
                        x, y = a[2 * k], a[2 * k + 1]
                        if half == 0:
                            value = jnp.where(sub, x, pltpu.roll(y, 4, 0))
                        else:
                            value = jnp.where(sub, pltpu.roll(x, 4, 0), y)
                        grad_ref[block, 8 * k : 8 * k + 8, :] += value

    def new_rows(block, k):
        rows = slice(8 * k, 8 * k + 8)
        first, second = moments(grad_ref[block, rows], m1_ref[block, rows], m2_ref[block, rows])
        return stepped(table_ref[block, rows], first, second)

    for g in range(8):
        for level in range(2):
            for pair in range(2):
                rows = slice(8 * pair, 8 * pair + 8)
                for k in range(2):
                    x = new_rows(blocks[g, level, 2 * pair], k)
                    y = new_rows(blocks[g, level, 2 * pair + 1], k)
                    left = slice(2 * k * LANES, (2 * k + 1) * LANES)
                    right = slice((2 * k + 1) * LANES, (2 * k + 2) * LANES)
                    pick_ref[g, level, rows, left] = jnp.where(sub, x, pltpu.roll(y, 4, 0))
                    pick_ref[g, level, rows, right] = jnp.where(sub, pltpu.roll(x, 4, 0), y)


def dense_kernel(grad_ref, table_ref, m1_ref, m2_ref, tnew_ref, m1new_ref, m2new_ref):
    first, second = moments(grad_ref[...], m1_ref[...], m2_ref[...])
    m1new_ref[...] = first
    m2new_ref[...] = second
    tnew_ref[...] = stepped(table_ref[...], first, second)


def lookup_kernel(recv_ref, high_ref, low_ref, cand_ref, win_ref, wout_ref, out_ref):
    rows = []
    for level in range(2):
        blocks = recv_ref[:, level].reshape(128, 512)
        b_high, b_low = split_two(blocks)
        both = jnp.dot(
            jnp.concatenate([b_high, b_low], axis=0), high_ref[level], preferred_element_type=jnp.float32
        )
        rest = jnp.dot(b_high, low_ref[level], preferred_element_type=jnp.float32)
        looked = both[:128] + both[128:] + rest
        row = lax.broadcasted_iota(jnp.int32, (128, 512), 0) // 4
        kept = jnp.where(cand_ref[level : level + 1, :] == row, looked, 0.0)
        folded = jnp.sum(kept.reshape(16, 8, 512), axis=0)
        rows.append(folded[:4] + folded[4:])
    encoded = jnp.concatenate(rows, axis=0)
    hidden = jnp.maximum(
        lax.dot_general(
            win_ref[...], encoded, (((0,), (0,)), ((), ())),
            precision=lax.Precision.HIGHEST, preferred_element_type=jnp.float32,
        ),
        0.0,
    )
    out = jnp.dot(wout_ref[...], hidden, precision=lax.Precision.HIGHEST, preferred_element_type=jnp.float32)
    low_lanes = lax.broadcasted_iota(jnp.int32, (8, LANES), 1) < RUN
    for v in range(4):
        upper = out[:8, v * LANES : (v + 1) * LANES]
        lower = out[8:, v * LANES : (v + 1) * LANES]
        for p in range(4):
            x = pltpu.roll(upper, (-RUN * p) % LANES, 1) if p else upper
            y = pltpu.roll(lower, (RUN - RUN * p) % LANES, 1) if p != 1 else lower
            out_ref[4 * v + p] = jnp.where(low_lanes, x, y)


def unpack_kernel(recv_ref, out_ref):
    group = lax.broadcasted_iota(jnp.int32, (8, LANES), 1) // RUN
    for v in range(4):
        upper = lower = None
        for p in range(4):
            piece = recv_ref[4 * v + p]
            x = pltpu.roll(piece, RUN * p, 1) if p else piece
            y = pltpu.roll(piece, (RUN * p - RUN) % LANES, 1) if p != 1 else piece
            upper = x if upper is None else jnp.where(group == p, x, upper)
            lower = y if lower is None else jnp.where(group == p, y, lower)
        out_ref[:8, v * LANES : (v + 1) * LANES] = upper
        out_ref[8:, v * LANES : (v + 1) * LANES] = lower


def call(kernel, outs, scratch=(), in_specs=None, **extra):
    vmem = pl.BlockSpec(memory_space=pltpu.VMEM)
    shapes = [jax.ShapeDtypeStruct(s, d) for s, d in outs]
    single = len(shapes) == 1
    if in_specs is not None:
        extra["in_specs"] = in_specs
    return pl.pallas_call(
        kernel,
        out_shape=shapes[0] if single else shapes,
        out_specs=vmem if single else [vmem] * len(shapes),
        scratch_shapes=list(scratch),
        compiler_params=pltpu.CompilerParams(vmem_limit_bytes=VMEM_LIMIT),
        **extra,
    )


def in_hbm(*arrays):
    return [pltpu.with_memory_space_constraint(array, pltpu.HBM) for array in arrays]


def exchange(value, axis):
    return lax.all_to_all(value, axis, split_axis=0, concat_axis=0, tiled=True)


def rows_of(array):
    levels, blocks = array.shape[:2]
    return array.reshape(levels, blocks, 4, 4, LANES).transpose(0, 1, 3, 2, 4).reshape(levels * blocks, 16, LANES)


def rows_back(array, shape):
    levels, blocks = shape[:2]
    return array.reshape(levels, blocks, 4, 4, LANES).transpose(0, 1, 3, 2, 4).reshape(shape)


def on_device(
    table,
    moment1,
    moment2,
    block_ids,
    sample_slot,
    corners,
    fractions,
    feat_cot,
    weight_in,
    weight_out,
):
    f32, bf16, i32 = jnp.float32, jnp.bfloat16, jnp.int32
    ray = lax.axis_size("ray")
    vmem = pl.BlockSpec(memory_space=pltpu.VMEM)
    hbm = pl.BlockSpec(memory_space=pltpu.HBM)
    packed = call(
        pack_kernel,
        [((16, 8, LANES), f32)],
        [
            pltpu.VMEM((2, 512), i32),
            pltpu.VMEM((2, 8, 512), i32),
            pltpu.VMEM((3, 2, 512), f32),
            pltpu.VMEM((2, 4, 512), f32),
            pltpu.SemaphoreType.DMA((4,)),
        ],
        [hbm] * 4,
    )(*in_hbm(sample_slot, corners, fractions.transpose(1, 0, 2), feat_cot))
    samples = exchange(packed, "ray")
    rows = (128, 16, LANES)
    part, high, low, cand, table_v, m1_v, m2_v, win_v, wout_v = call(
        grad_kernel,
        [
            ((8, 2, 16, 512), f32),
            ((2, 512, 512), bf16),
            ((2, 512, 512), bf16),
            ((2, 512), i32),
            (rows, f32),
            (rows, f32),
            (rows, f32),
            ((8, 64), f32),
            ((16, 64), f32),
        ],
        [pltpu.VMEM((2, 8, 512), i32), pltpu.VMEM((2, 8, 512), f32), pltpu.SemaphoreType.DMA((5,))],
        [vmem] + [hbm] * 5,
    )(samples, *in_hbm(rows_of(table), rows_of(moment1), rows_of(moment2), weight_in.T, weight_out))
    received = exchange(part, "table")
    ids = block_ids.transpose(0, 1, 3, 2).reshape(64, 128)

    def listed(*refs):
        listed_kernel(*refs, ray=ray)

    picked, grad = call(
        listed,
        [((8, 2, 16, 512), f32), (rows, f32)],
        (),
        [pl.BlockSpec(memory_space=pltpu.SMEM)] + [vmem] * 4,
    )(*in_hbm(ids), received, table_v, m1_v, m2_v)
    returned = exchange(picked, "table")
    step = pl.BlockSpec((16, 16, LANES), lambda i: (i, 0, 0))
    tnew, m1new, m2new = pl.pallas_call(
        dense_kernel,
        grid=(8,),
        in_specs=[step] * 4,
        out_specs=[step] * 3,
        out_shape=[jax.ShapeDtypeStruct(rows, f32)] * 3,
        compiler_params=pltpu.CompilerParams(vmem_limit_bytes=VMEM_LIMIT),
        cost_estimate=pl.CostEstimate(flops=20 << 20, bytes_accessed=7 << 20, transcendentals=0),
    )(grad, *in_hbm(rows_of(table), rows_of(moment1), rows_of(moment2)))
    sent = call(lookup_kernel, [((16, 8, LANES), f32)])(returned, high, low, cand, win_v, wout_v)
    back = exchange(sent, "ray")
    mlp_out = call(unpack_kernel, [((16, 512), f32)])(back)
    shape = table.shape
    return (rows_back(tnew, shape), rows_back(m1new, shape), rows_back(m2new, shape), mlp_out)


def solution(mesh):
    in_specs = (
        P(None, ("table", "ray"), None, None),
        P(None, ("table", "ray"), None, None),
        P(None, ("table", "ray"), None, None),
        P(),
        P(None, ("table", "ray")),
        P(None, None, ("table", "ray")),
        P(None, None, ("table", "ray")),
        P(None, None, ("table", "ray")),
        P(),
        P(),
    )
    out_specs = (
        P(None, ("table", "ray"), None, None),
        P(None, ("table", "ray"), None, None),
        P(None, ("table", "ray"), None, None),
        P(None, ("table", "ray")),
    )
    return jax.shard_map(
        on_device, mesh=mesh, in_specs=in_specs, out_specs=out_specs, check_vma=False
    )
```

```python
import jax
import jax.numpy as jnp
from jax import lax
from jax.experimental import pallas as pl
from jax.experimental.pallas import tpu as pltpu
from jax.sharding import PartitionSpec as P

beta_one = 0.9
beta_two = 0.99
learn_rate = 0.01
adam_eps = 1e-15

LANES = 128
RUN = 32
VMEM_LIMIT = 40 << 20
f32, bf16, i32 = jnp.float32, jnp.bfloat16, jnp.int32


def iota(shape, axis):
    return lax.broadcasted_iota(i32, shape, axis)


def lane_blocks(pieces):
    group = iota(pieces[0].shape, 1) // RUN
    results = []
    for q in range(4):
        value = pieces[q]
        for p in range(4):
            if p != q:
                moved = pltpu.roll(pieces[p], (RUN * (p - q)) % LANES, 1)
                value = jnp.where(group == p, moved, value)
        results.append(value)
    return results


def tile_blocks(value):
    shift = (iota((8, LANES), 0) // 2 - iota((8, LANES), 1) // RUN) & 3
    result = value
    for d in range(1, 4):
        moved = pltpu.roll(pltpu.roll(value, 2 * d, 0), LANES - RUN * d, 1)
        result = jnp.where(shift == d, moved, result)
    return result


def start_all(sources, targets, sems):
    copies = [pltpu.make_async_copy(x, y, sems.at[n]) for n, (x, y) in enumerate(zip(sources, targets))]
    for copy in copies:
        copy.start()
    return copies


def wait_all(copies):
    for copy in copies:
        copy.wait()


def pack_kernel(slot_hbm, corners_hbm, fractions_hbm, cot_hbm, out_ref, slot_ref, corners_ref, fractions_ref, cot_ref, sems):
    wait_all(
        start_all(
            (slot_hbm, corners_hbm, fractions_hbm, cot_hbm), (slot_ref, corners_ref, fractions_ref, cot_ref), sems
        )
    )
    groups = [corners_ref[0].astype(f32), corners_ref[1].astype(f32)]
    for level in range(2):
        rows = [slot_ref[level : level + 1, :].astype(f32)]
        rows += [fractions_ref[d, level : level + 1, :] for d in range(3)]
        rows += [cot_ref[level]]
        groups.append(jnp.concatenate(rows, axis=0))
    for v in range(4):
        lanes = slice(v * LANES, (v + 1) * LANES)
        for p, value in enumerate(lane_blocks([g[:, lanes] for g in groups])):
            for t in range(8):
                out_ref[16 * t + 4 * v + p] = value


def gather_lanes(value, index):
    return jnp.take_along_axis(value, index, axis=1, mode="promise_in_bounds")


def owner_kernel(
    ids_ref, recv_ref, table_hbm, m1_hbm, m2_hbm, win_hbm, wout_hbm,
    tnew_hbm, m1new_hbm, m2new_hbm, out_ref, win_ref, wout_ref,
    table_ref, m1_ref, m2_ref, grad_ref, corner_ref, aux_ref, back_ref, slots_ref, hot_ref, hat_ref, key_ref,
    found_ref, result_ref, sems,
):
    loads = start_all(
        (table_hbm, m1_hbm, m2_hbm, win_hbm, wout_hbm), (table_ref, m1_ref, m2_ref, win_ref, wout_ref), sems
    )
    mine = lax.axis_index("table")
    owner = mine * lax.axis_size("ray") + lax.axis_index("ray")
    sub = iota((8, LANES), 0)
    parity = sub // 4
    lane16 = iota((16, LANES), 1)

    grad_ref[...] = jnp.zeros_like(grad_ref)
    result_ref[...] = jnp.zeros_like(result_ref)

    def unpack(t, carry):
        for v in range(4):
            rows = lane_blocks([recv_ref[t * 16 + 4 * v + p] for p in range(4)])
            corner_ref[t, v] = rows[0]
            corner_ref[8 + t, v] = rows[1]
            aux_ref[t, v] = rows[2]
            aux_ref[8 + t, v] = rows[3]
        return carry

    lax.fori_loop(0, 8, unpack, 0, unroll=2)

    first_slot = (mine * 64).astype(f32)
    hits = []
    for v in range(4):
        slot = jnp.concatenate([aux_ref[lt, v, 0:1, :] for lt in range(16)], axis=0)
        hits.append(jnp.where((slot >= first_slot) & (slot < first_slot + 64.0), 1.0, 0.0))
    row, column = iota((LANES, 2 * LANES), 0), iota((LANES, 2 * LANES), 1)
    upper = jnp.where(row <= column, 1.0, 0.0).astype(bf16)
    counts = jnp.dot(jnp.concatenate(hits, axis=0).astype(bf16), upper, preferred_element_type=f32).astype(i32)
    through = [counts[16 * v : 16 * v + 16, :LANES] for v in range(4)]
    totals = [counts[16 * v : 16 * v + 16, LANES:] for v in range(4)]
    before = [jnp.zeros_like(totals[0])]
    for v in range(4):
        before.append(before[v] + totals[v])
    passes = (jnp.max(before[4]) + (LANES - 1)) // LANES

    def locate(step):
        for v in range(4):
            rank = before[v] + through[v] - 1 - step * LANES
            inside = (hits[v] > 0.5) & (rank >= 0) & (rank < LANES)
            slots_ref[v] = jnp.where(inside, rank, -1)
            wanted = lane16 + step * LANES - before[v]
            place = jnp.zeros_like(wanted)
            for jump in (64, 32, 16, 8, 4, 2, 1):
                probe = gather_lanes(through[v], place + (jump - 1))
                place = jnp.where(probe <= wanted, place + jump, place)
            back_ref[v] = jnp.where((wanted >= 0) & (wanted < totals[v]), place, -1)

    def compact(lt):
        corner = jnp.zeros((8, LANES), f32)
        aux = jnp.zeros((8, LANES), f32)
        for v in range(4):
            place = jnp.broadcast_to(back_ref[v, pl.ds(lt, 1), :], (8, LANES))
            index = jnp.maximum(place, 0)
            corner = jnp.where(place >= 0, gather_lanes(corner_ref[lt, v], index), corner)
            aux = jnp.where(place >= 0, gather_lanes(aux_ref[lt, v], index), aux)
        hat = None
        for d in range(3):
            f = jnp.broadcast_to(aux[1 + d : 2 + d], (8, LANES))
            factor = jnp.where((sub >> d) & 1 == 1, f, 1.0 - f)
            hat = factor if hat is None else hat * factor
        entry = corner.astype(i32)
        key = (aux[0:1].astype(i32) & 3) * 2 + ((entry >> 7) & 1)
        column = (entry & 127) | ((entry >> 8) << 7)
        hat_ref[lt] = hat
        key_ref[lt] = key
        entries = iota((256, LANES), 0)
        for c in range(8):
            hot = jnp.where(column[c : c + 1] == entries, 1.0, 0.0).astype(bf16)
            hot_ref[lt, :, c * LANES : (c + 1) * LANES] = hot
        return aux, hat, key

    def block_of(lt, slot):
        level, group = lt // 8, lt % 8
        return level * 64 + ids_ref[(group * 2 + level) * 4 + slot, owner]

    def accumulate(lt, carry):
        aux, hat, key = compact(lt)
        cot = jnp.where(sub < 4, pltpu.roll(aux, 4, 0), aux)
        columns = []
        for c in range(8):
            value = cot * hat[c : c + 1]
            high = value.astype(bf16).astype(f32)
            low = value - high
            masks = [jnp.broadcast_to(key[c : c + 1], (8, LANES)) == parity + 2 * i for i in range(4)]
            pieces = [jnp.where(m, high, 0.0) for m in masks] + [jnp.where(m, low, 0.0) for m in masks]
            columns.append(jnp.concatenate(pieces, axis=0).astype(bf16))
        both = lax.dot_general(
            jnp.concatenate(columns, axis=1), hot_ref[lt], (((1,), (1,)), ((), ())), preferred_element_type=f32
        )
        part = both[:32] + both[32:]
        for slot in range(4):
            block = block_of(lt, slot)
            for half in range(2):
                grad_ref[block, 8 * half : 8 * half + 8, :] += part[
                    8 * slot : 8 * slot + 8, half * LANES : (half + 1) * LANES
                ]
        return carry

    def gather_pass(step, carry):
        locate(step)
        lax.fori_loop(0, 16, accumulate, 0, unroll=2)
        return carry

    lax.fori_loop(0, passes, gather_pass, 0)
    wait_all(loads)

    def update(step, carry):
        at = pl.ds(step * 4, 4)
        grad = grad_ref[at]
        first = beta_one * m1_ref[at] + (1.0 - beta_one) * grad
        second = beta_two * m2_ref[at] + (1.0 - beta_two) * grad * grad
        m1_ref[at] = first
        m2_ref[at] = second
        table_ref[at] = table_ref[at] - learn_rate * first / (jnp.sqrt(second) + adam_eps)
        return carry

    lax.fori_loop(0, 32, update, 0)
    stores = start_all((table_ref, m1_ref, m2_ref), (tnew_hbm, m1new_hbm, m2new_hbm), sems)

    def look(lt, carry):
        blocks = [table_ref[block_of(lt, slot)] for slot in range(4)]
        rows = jnp.concatenate([jnp.concatenate([b[:8], b[8:]], axis=1) for b in blocks], axis=0)
        high = rows.astype(bf16)
        low = (rows - high.astype(f32)).astype(bf16)
        both = jnp.dot(jnp.concatenate([high, low], axis=0), hot_ref[lt], preferred_element_type=f32)
        seen = both[:32] + both[32:]
        hat, key = hat_ref[lt], key_ref[lt]
        total = jnp.zeros((8, LANES), f32)
        for c in range(8):
            own = jnp.broadcast_to(key[c : c + 1], (8, LANES))
            picked = jnp.zeros((8, LANES), f32)
            for i in range(4):
                picked = jnp.where(own == parity + 2 * i, seen[8 * i : 8 * i + 8, c * LANES : (c + 1) * LANES], picked)
            total = total + jnp.where((own & 1) == parity, picked, 0.0) * hat[c : c + 1]
        found_ref[lt] = total + pltpu.roll(total, 4, 0)
        return carry

    def spread(t, carry):
        value = jnp.where(sub < 4, found_ref[t], found_ref[8 + t])
        for v in range(4):
            zero = jnp.broadcast_to(slots_ref[v, pl.ds(t, 1), :], (8, LANES))
            one = jnp.broadcast_to(slots_ref[v, pl.ds(8 + t, 1), :], (8, LANES))
            place = jnp.where(sub < 4, zero, one)
            taken = gather_lanes(value, jnp.maximum(place, 0))
            result_ref[t * 4 + v] += jnp.where(place >= 0, taken, 0.0)
        return carry

    def look_pass(step, carry):
        @pl.when(passes > 1)
        def _():
            locate(step)

            def again(lt, inner):
                compact(lt)
                return inner

            lax.fori_loop(0, 16, again, 0)

        lax.fori_loop(0, 16, look, 0, unroll=2)
        lax.fori_loop(0, 8, spread, 0, unroll=2)
        return carry

    lax.fori_loop(0, passes, look_pass, 0)
    for m in range(32):
        out_ref[m] = tile_blocks(result_ref[m])
    wait_all(stores)


def network_kernel(recv_ref, win_ref, wout_ref, out_ref):
    columns = []
    for v in range(4):
        total = recv_ref[v]
        for t in range(1, 8):
            total = total + recv_ref[4 * t + v]
        columns.append(tile_blocks(total))
    encoded = jnp.concatenate(columns, axis=1)
    hidden = jnp.maximum(
        lax.dot_general(
            win_ref[...], encoded, (((0,), (0,)), ((), ())),
            precision=lax.Precision.HIGHEST, preferred_element_type=f32,
        ),
        0.0,
    )
    out_ref[...] = jnp.dot(wout_ref[...], hidden, precision=lax.Precision.HIGHEST, preferred_element_type=f32)


VMEM = pl.BlockSpec(memory_space=pltpu.VMEM)
HBM = pl.BlockSpec(memory_space=pltpu.HBM)
SMEM = pl.BlockSpec(memory_space=pltpu.SMEM)


def call(kernel, outs, in_specs, scratch=(), out_specs=None, **extra):
    return pl.pallas_call(
        kernel,
        out_shape=[jax.ShapeDtypeStruct(s, d) for s, d in outs],
        in_specs=in_specs,
        out_specs=[VMEM] * len(outs) if out_specs is None else out_specs,
        scratch_shapes=list(scratch),
        compiler_params=pltpu.CompilerParams(vmem_limit_bytes=VMEM_LIMIT),
        **extra,
    )


def in_hbm(*arrays):
    return [pltpu.with_memory_space_constraint(array, pltpu.HBM) for array in arrays]


def exchange(value):
    return lax.all_to_all(value, ("table", "ray"), split_axis=0, concat_axis=0, tiled=True)


def rows_of(array):
    levels, blocks = array.shape[:2]
    return array.reshape(levels, blocks, 4, 4, LANES).transpose(0, 1, 3, 2, 4).reshape(levels * blocks, 16, LANES)


def rows_back(array, shape):
    levels, blocks = shape[:2]
    return array.reshape(levels, blocks, 4, 4, LANES).transpose(0, 1, 3, 2, 4).reshape(shape)


def on_device(
    table,
    moment1,
    moment2,
    block_ids,
    sample_slot,
    corners,
    fractions,
    feat_cot,
    weight_in,
    weight_out,
):
    (packed,) = call(
        pack_kernel,
        [((128, 8, LANES), f32)],
        [HBM] * 4,
        [
            pltpu.VMEM((2, 512), i32),
            pltpu.VMEM((2, 8, 512), i32),
            pltpu.VMEM((3, 2, 512), f32),
            pltpu.VMEM((2, 4, 512), f32),
            pltpu.SemaphoreType.DMA((4,)),
        ],
    )(*in_hbm(sample_slot, corners, fractions.transpose(1, 0, 2), feat_cot))
    samples = exchange(packed)
    rows = (128, 16, LANES)
    ids = block_ids.transpose(0, 1, 3, 2).reshape(64, 128)
    tnew, m1new, m2new, found, win, wout = call(
        owner_kernel,
        [(rows, f32), (rows, f32), (rows, f32), ((32, 8, LANES), f32), ((8, 64), f32), ((16, 64), f32)],
        [SMEM, VMEM] + [HBM] * 5,
        [
            pltpu.VMEM(rows, f32),
            pltpu.VMEM(rows, f32),
            pltpu.VMEM(rows, f32),
            pltpu.VMEM(rows, f32),
            pltpu.VMEM((16, 4, 8, LANES), f32),
            pltpu.VMEM((16, 4, 8, LANES), f32),
            pltpu.VMEM((4, 16, LANES), i32),
            pltpu.VMEM((4, 16, LANES), i32),
            pltpu.VMEM((16, 256, 8 * LANES), bf16),
            pltpu.VMEM((16, 8, LANES), f32),
            pltpu.VMEM((16, 8, LANES), i32),
            pltpu.VMEM((16, 8, LANES), f32),
            pltpu.VMEM((32, 8, LANES), f32),
            pltpu.SemaphoreType.DMA((5,)),
        ],
        [HBM] * 3 + [VMEM] * 3,
    )(
        *in_hbm(ids),
        samples,
        *in_hbm(rows_of(table), rows_of(moment1), rows_of(moment2), weight_in.T, weight_out),
    )
    back = exchange(found.reshape(128, 2, LANES)).reshape(32, 8, LANES)
    (mlp_out,) = call(network_kernel, [((16, 512), f32)], [VMEM] * 3)(back, win, wout)
    shape = table.shape
    return (rows_back(tnew, shape), rows_back(m1new, shape), rows_back(m2new, shape), mlp_out)


def solution(mesh):
    in_specs = (
        P(None, ("table", "ray"), None, None),
        P(None, ("table", "ray"), None, None),
        P(None, ("table", "ray"), None, None),
        P(),
        P(None, ("table", "ray")),
        P(None, None, ("table", "ray")),
        P(None, None, ("table", "ray")),
        P(None, None, ("table", "ray")),
        P(),
        P(),
    )
    out_specs = (
        P(None, ("table", "ray"), None, None),
        P(None, ("table", "ray"), None, None),
        P(None, ("table", "ray"), None, None),
        P(None, ("table", "ray")),
    )
    return jax.shard_map(
        on_device, mesh=mesh, in_specs=in_specs, out_specs=out_specs, check_vma=False
    )
```

```python
import jax
import jax.numpy as jnp
from jax import lax
from jax.experimental import pallas as pl
from jax.experimental.pallas import tpu as pltpu
from jax.sharding import PartitionSpec as P

beta_one = 0.9
beta_two = 0.99
learn_rate = 0.01
adam_eps = 1e-15

LANES = 128
RUN = 32
VMEM_LIMIT = 40 << 20
f32, bf16, i32 = jnp.float32, jnp.bfloat16, jnp.int32


def iota(shape, axis):
    return lax.broadcasted_iota(i32, shape, axis)


def lane_blocks(pieces):
    lane = iota(pieces[0].shape, 1)
    for width in (2 * RUN, RUN):
        low = (lane & width) == 0
        step = width // RUN
        results = list(pieces)
        for one in range(4):
            if not one & step:
                x, y = pieces[one], pieces[one + step]
                results[one] = jnp.where(low, x, pltpu.roll(y, width, 1))
                results[one + step] = jnp.where(low, pltpu.roll(x, LANES - width, 1), y)
        pieces = results
    return pieces


def tile_blocks(value):
    shift = (iota((8, LANES), 0) // 2 - iota((8, LANES), 1) // RUN) & 3
    result = value
    for d in range(1, 4):
        moved = pltpu.roll(pltpu.roll(value, 2 * d, 0), LANES - RUN * d, 1)
        result = jnp.where(shift == d, moved, result)
    return result


def start_all(sources, targets, sems):
    copies = [pltpu.make_async_copy(x, y, sems.at[n]) for n, (x, y) in enumerate(zip(sources, targets))]
    for copy in copies:
        copy.start()
    return copies


def wait_all(copies):
    for copy in copies:
        copy.wait()


def pack_kernel(slot_hbm, corners_hbm, fractions_hbm, cot_hbm, out_ref, slot_ref, corners_ref, fractions_ref, cot_ref, sems):
    wait_all(
        start_all(
            (slot_hbm, corners_hbm, fractions_hbm, cot_hbm), (slot_ref, corners_ref, fractions_ref, cot_ref), sems
        )
    )
    groups = [corners_ref[0].astype(f32), corners_ref[1].astype(f32)]
    for level in range(2):
        rows = [slot_ref[level : level + 1, :].astype(f32)]
        rows += [fractions_ref[d, level : level + 1, :] for d in range(3)]
        rows += [cot_ref[level]]
        groups.append(jnp.concatenate(rows, axis=0))
    for v in range(4):
        lanes = slice(v * LANES, (v + 1) * LANES)
        for p, value in enumerate(lane_blocks([g[:, lanes] for g in groups])):
            for t in range(8):
                out_ref[16 * t + 4 * v + p] = value


def gather_lanes(value, index):
    return jnp.take_along_axis(value, index, axis=1, mode="promise_in_bounds")


def owner_kernel(
    ids_ref, recv_ref, table_hbm, m1_hbm, m2_hbm, win_hbm, wout_hbm,
    tnew_hbm, m1new_hbm, m2new_hbm, out_ref, win_ref, wout_ref,
    table_ref, m1_ref, m2_ref, grad_ref, corner_ref, aux_ref, back_ref, slots_ref, hat_ref, key_ref, column_ref, cot_ref,
    found_ref, result_ref, sems,
):
    loads = start_all(
        (table_hbm, m1_hbm, m2_hbm, win_hbm, wout_hbm), (table_ref, m1_ref, m2_ref, win_ref, wout_ref), sems
    )
    mine = lax.axis_index("table")
    owner = mine * lax.axis_size("ray") + lax.axis_index("ray")
    sub = iota((8, LANES), 0)
    parity = sub // 4
    lane16 = iota((16, LANES), 1)

    grad_ref[...] = jnp.zeros_like(grad_ref)
    result_ref[...] = jnp.zeros_like(result_ref)

    def unpack(t, carry):
        for v in range(4):
            rows = lane_blocks([recv_ref[t * 16 + 4 * v + p] for p in range(4)])
            corner_ref[t, v] = rows[0]
            corner_ref[8 + t, v] = rows[1]
            aux_ref[t, v] = rows[2]
            aux_ref[8 + t, v] = rows[3]
        return carry

    lax.fori_loop(0, 8, unpack, 0, unroll=8)

    first_slot = (mine * 64).astype(f32)
    hits = []
    for v in range(4):
        slot = jnp.concatenate([aux_ref[lt, v, 0:1, :] for lt in range(16)], axis=0)
        hits.append(jnp.where((slot >= first_slot) & (slot < first_slot + 64.0), 1.0, 0.0))
    row, column = iota((LANES, 2 * LANES), 0), iota((LANES, 2 * LANES), 1)
    upper = jnp.where(row <= column, 1.0, 0.0).astype(bf16)
    counts = jnp.dot(jnp.concatenate(hits, axis=0).astype(bf16), upper, preferred_element_type=f32).astype(i32)
    through = [counts[16 * v : 16 * v + 16, :LANES] for v in range(4)]
    totals = [counts[16 * v : 16 * v + 16, LANES:] for v in range(4)]
    before = [jnp.zeros_like(totals[0])]
    for v in range(4):
        before.append(before[v] + totals[v])
    passes = (jnp.max(before[4]) + (LANES - 1)) // LANES

    def locate(step):
        for v in range(4):
            rank = before[v] + through[v] - 1 - step * LANES
            inside = (hits[v] > 0.5) & (rank >= 0) & (rank < LANES)
            slots_ref[v] = jnp.where(inside, rank, -1)
            wanted = lane16 + step * LANES - before[v]
            place = jnp.zeros_like(wanted)
            for jump in (64, 32, 16, 8, 4, 2, 1):
                probe = gather_lanes(through[v], place + (jump - 1))
                place = jnp.where(probe <= wanted, place + jump, place)
            back_ref[v] = jnp.where((wanted >= 0) & (wanted < totals[v]), place, -1)

    entries = [(iota((16, LANES), 0) + 16 * i).astype(f32).astype(bf16) for i in range(8)]
    owns = [((iota((16, LANES), 0) & 7) // 4 + 2 * i).astype(f32).astype(bf16) for i in range(8)]
    one = jnp.ones((16, LANES), bf16)
    none = jnp.zeros((16, LANES), bf16)

    def compact(lt, carry):
        corner = jnp.zeros((8, LANES), f32)
        aux = jnp.zeros((8, LANES), f32)
        for v in range(4):
            place = jnp.broadcast_to(back_ref[v, pl.ds(lt, 1), :], (8, LANES))
            index = jnp.maximum(place, 0)
            corner = jnp.where(place >= 0, gather_lanes(corner_ref[lt, v], index), corner)
            aux = jnp.where(place >= 0, gather_lanes(aux_ref[lt, v], index), aux)
        hat = None
        for d in range(3):
            f = jnp.broadcast_to(aux[1 + d : 2 + d], (8, LANES))
            factor = jnp.where((sub >> d) & 1 == 1, f, 1.0 - f)
            hat = factor if hat is None else hat * factor
        entry = corner.astype(i32)
        hat_ref[lt] = hat
        key_ref[lt] = ((aux[0:1].astype(i32) & 3) * 4 + (entry >> 7)).astype(f32)
        column_ref[lt] = (entry & 127).astype(f32)
        cot_ref[lt] = jnp.where(sub < 4, pltpu.roll(aux, 4, 0), aux)
        return carry

    def hot_rows(lt):
        pieces = []
        for c in range(8):
            wanted = jnp.broadcast_to(column_ref[lt, c : c + 1, :], (16, LANES)).astype(bf16)
            pieces.append(jnp.concatenate([jnp.where(wanted == entries[i], one, none) for i in range(8)], axis=0))
        return jnp.concatenate(pieces, axis=1)

    def block_of(lt, slot):
        level, group = lt // 8, lt % 8
        return level * 64 + ids_ref[(group * 2 + level) * 4 + slot, owner]

    def accumulate(lt, carry):
        cot = cot_ref[lt]
        columns = []
        for c in range(8):
            value = cot * hat_ref[lt, c : c + 1, :]
            high = value.astype(bf16).astype(f32)
            both = jnp.concatenate([high, value - high], axis=0).astype(bf16)
            key = jnp.broadcast_to(key_ref[lt, c : c + 1, :], (16, LANES)).astype(bf16)
            columns.append(jnp.concatenate([jnp.where(key == owns[i], both, none) for i in range(8)], axis=0))
        sums = lax.dot_general(
            jnp.concatenate(columns, axis=1), hot_rows(lt), (((1,), (1,)), ((), ())), preferred_element_type=f32
        )
        for slot in range(4):
            block = block_of(lt, slot)
            for half in range(2):
                at = 32 * slot + 16 * half
                grad_ref[block, 8 * half : 8 * half + 8, :] += sums[at : at + 8] + sums[at + 8 : at + 16]
        return carry

    def gather_pass(step, carry):
        locate(step)
        lax.fori_loop(0, 16, compact, 0, unroll=4)
        lax.fori_loop(0, 16, accumulate, 0, unroll=4)
        return carry

    lax.fori_loop(0, passes, gather_pass, 0)
    wait_all(loads)

    def update(step, carry):
        at = pl.ds(step * 4, 4)
        grad = grad_ref[at]
        first = beta_one * m1_ref[at] + (1.0 - beta_one) * grad
        second = beta_two * m2_ref[at] + (1.0 - beta_two) * grad * grad
        m1_ref[at] = first
        m2_ref[at] = second
        table_ref[at] = table_ref[at] - learn_rate * first / (jnp.sqrt(second) + adam_eps)
        return carry

    lax.fori_loop(0, 32, update, 0)
    stores = start_all((table_ref, m1_ref, m2_ref), (tnew_hbm, m1new_hbm, m2new_hbm), sems)

    def look(lt, carry):
        rows = jnp.concatenate([table_ref[block_of(lt, slot)] for slot in range(4)], axis=0)
        high = rows.astype(bf16)
        low = (rows - high.astype(f32)).astype(bf16)
        hot = hot_rows(lt)
        seen = jnp.dot(
            jnp.concatenate([high, low], axis=1), jnp.concatenate([hot, hot], axis=0), preferred_element_type=f32
        )
        total = jnp.zeros((8, LANES), f32)
        for c in range(8):
            own = jnp.broadcast_to(key_ref[lt, c : c + 1, :], (8, LANES))
            picked = jnp.zeros((8, LANES), f32)
            for i in range(8):
                mask = own == (parity + 2 * i).astype(f32)
                picked = jnp.where(mask, seen[8 * i : 8 * i + 8, c * LANES : (c + 1) * LANES], picked)
            total = total + picked * hat_ref[lt, c : c + 1, :]
        found_ref[lt] = total + pltpu.roll(total, 4, 0)
        return carry

    def spread(t, carry):
        value = jnp.where(sub < 4, found_ref[t], found_ref[8 + t])
        for v in range(4):
            zero = jnp.broadcast_to(slots_ref[v, pl.ds(t, 1), :], (8, LANES))
            one = jnp.broadcast_to(slots_ref[v, pl.ds(8 + t, 1), :], (8, LANES))
            place = jnp.where(sub < 4, zero, one)
            taken = gather_lanes(value, jnp.maximum(place, 0))
            result_ref[t * 4 + v] += jnp.where(place >= 0, taken, 0.0)
        return carry

    def look_pass(step, carry):
        @pl.when(passes > 1)
        def _():
            locate(step)
            lax.fori_loop(0, 16, compact, 0)

        lax.fori_loop(0, 16, look, 0, unroll=4)
        lax.fori_loop(0, 8, spread, 0, unroll=2)
        return carry

    lax.fori_loop(0, passes, look_pass, 0)
    for m in range(32):
        out_ref[m] = tile_blocks(result_ref[m])
    wait_all(stores)


def network_kernel(recv_ref, win_ref, wout_ref, out_ref):
    columns = []
    for v in range(4):
        total = recv_ref[v]
        for t in range(1, 8):
            total = total + recv_ref[4 * t + v]
        columns.append(tile_blocks(total))
    encoded = jnp.concatenate(columns, axis=1)
    hidden = jnp.maximum(
        lax.dot_general(
            win_ref[...], encoded, (((0,), (0,)), ((), ())),
            precision=lax.Precision.HIGHEST, preferred_element_type=f32,
        ),
        0.0,
    )
    out_ref[...] = jnp.dot(wout_ref[...], hidden, precision=lax.Precision.HIGHEST, preferred_element_type=f32)


VMEM = pl.BlockSpec(memory_space=pltpu.VMEM)
HBM = pl.BlockSpec(memory_space=pltpu.HBM)
SMEM = pl.BlockSpec(memory_space=pltpu.SMEM)


def call(kernel, outs, in_specs, scratch=(), out_specs=None, **extra):
    return pl.pallas_call(
        kernel,
        out_shape=[jax.ShapeDtypeStruct(s, d) for s, d in outs],
        in_specs=in_specs,
        out_specs=[VMEM] * len(outs) if out_specs is None else out_specs,
        scratch_shapes=list(scratch),
        compiler_params=pltpu.CompilerParams(vmem_limit_bytes=VMEM_LIMIT),
        **extra,
    )


def in_hbm(*arrays):
    return [pltpu.with_memory_space_constraint(array, pltpu.HBM) for array in arrays]


def exchange(value):
    return lax.all_to_all(value, ("table", "ray"), split_axis=0, concat_axis=0, tiled=True)


def rows_of(array):
    levels, blocks = array.shape[:2]
    return array.reshape(levels, blocks, 4, 4, LANES).transpose(0, 1, 3, 2, 4).reshape(levels * blocks, 16, LANES)


def rows_back(array, shape):
    levels, blocks = shape[:2]
    return array.reshape(levels, blocks, 4, 4, LANES).transpose(0, 1, 3, 2, 4).reshape(shape)


def on_device(
    table,
    moment1,
    moment2,
    block_ids,
    sample_slot,
    corners,
    fractions,
    feat_cot,
    weight_in,
    weight_out,
):
    (packed,) = call(
        pack_kernel,
        [((128, 8, LANES), f32)],
        [HBM] * 4,
        [
            pltpu.VMEM((2, 512), i32),
            pltpu.VMEM((2, 8, 512), i32),
            pltpu.VMEM((3, 2, 512), f32),
            pltpu.VMEM((2, 4, 512), f32),
            pltpu.SemaphoreType.DMA((4,)),
        ],
    )(*in_hbm(sample_slot, corners, fractions.transpose(1, 0, 2), feat_cot))
    samples = exchange(packed)
    rows = (128, 16, LANES)
    ids = block_ids.transpose(0, 1, 3, 2).reshape(64, 128)
    tnew, m1new, m2new, found, win, wout = call(
        owner_kernel,
        [(rows, f32), (rows, f32), (rows, f32), ((32, 8, LANES), f32), ((8, 64), f32), ((16, 64), f32)],
        [SMEM, VMEM] + [HBM] * 5,
        [
            pltpu.VMEM(rows, f32),
            pltpu.VMEM(rows, f32),
            pltpu.VMEM(rows, f32),
            pltpu.VMEM(rows, f32),
            pltpu.VMEM((16, 4, 8, LANES), f32),
            pltpu.VMEM((16, 4, 8, LANES), f32),
            pltpu.VMEM((4, 16, LANES), i32),
            pltpu.VMEM((4, 16, LANES), i32),
            pltpu.VMEM((16, 8, LANES), f32),
            pltpu.VMEM((16, 8, LANES), f32),
            pltpu.VMEM((16, 8, LANES), f32),
            pltpu.VMEM((16, 8, LANES), f32),
            pltpu.VMEM((16, 8, LANES), f32),
            pltpu.VMEM((32, 8, LANES), f32),
            pltpu.SemaphoreType.DMA((5,)),
        ],
        [HBM] * 3 + [VMEM] * 3,
    )(
        *in_hbm(ids),
        samples,
        *in_hbm(rows_of(table), rows_of(moment1), rows_of(moment2), weight_in.T, weight_out),
    )
    back = exchange(found.reshape(128, 2, LANES)).reshape(32, 8, LANES)
    (mlp_out,) = call(network_kernel, [((16, 512), f32)], [VMEM] * 3)(back, win, wout)
    shape = table.shape
    return (rows_back(tnew, shape), rows_back(m1new, shape), rows_back(m2new, shape), mlp_out)


def solution(mesh):
    in_specs = (
        P(None, ("table", "ray"), None, None),
        P(None, ("table", "ray"), None, None),
        P(None, ("table", "ray"), None, None),
        P(),
        P(None, ("table", "ray")),
        P(None, None, ("table", "ray")),
        P(None, None, ("table", "ray")),
        P(None, None, ("table", "ray")),
        P(),
        P(),
    )
    out_specs = (
        P(None, ("table", "ray"), None, None),
        P(None, ("table", "ray"), None, None),
        P(None, ("table", "ray"), None, None),
        P(None, ("table", "ray")),
    )
    return jax.shard_map(
        on_device, mesh=mesh, in_specs=in_specs, out_specs=out_specs, check_vma=False
    )
```

```python
import jax
import jax.numpy as jnp
from jax import lax
from jax.experimental import pallas as pl
from jax.experimental.pallas import tpu as pltpu
from jax.sharding import PartitionSpec as P

beta_one = 0.9
beta_two = 0.99
learn_rate = 0.01
adam_eps = 1e-15

LANES = 128
RUN = 32
VMEM_LIMIT = 16 << 20
f32, bf16, i32 = jnp.float32, jnp.bfloat16, jnp.int32


def iota(shape, axis):
    return lax.broadcasted_iota(i32, shape, axis)


def lane_blocks(pieces):
    lane = iota(pieces[0].shape, 1)
    for width in (2 * RUN, RUN):
        low = (lane & width) == 0
        step = width // RUN
        results = list(pieces)
        for one in range(4):
            if not one & step:
                x, y = pieces[one], pieces[one + step]
                results[one] = jnp.where(low, x, pltpu.roll(y, width, 1))
                results[one + step] = jnp.where(low, pltpu.roll(x, LANES - width, 1), y)
        pieces = results
    return pieces


def tile_blocks(value):
    shift = (iota((8, LANES), 0) // 2 - iota((8, LANES), 1) // RUN) & 3
    result = value
    for d in range(1, 4):
        moved = pltpu.roll(pltpu.roll(value, 2 * d, 0), LANES - RUN * d, 1)
        result = jnp.where(shift == d, moved, result)
    return result


def start_all(sources, targets, sems):
    copies = [pltpu.make_async_copy(x, y, sems.at[n]) for n, (x, y) in enumerate(zip(sources, targets))]
    for copy in copies:
        copy.start()
    return copies


def wait_all(copies):
    for copy in copies:
        copy.wait()


def pack_kernel(slot_hbm, corners_hbm, fractions_hbm, cot_hbm, out_ref, slot_ref, corners_ref, fractions_ref, cot_ref, sems):
    wait_all(
        start_all(
            (slot_hbm, corners_hbm, fractions_hbm, cot_hbm), (slot_ref, corners_ref, fractions_ref, cot_ref), sems
        )
    )
    groups = [corners_ref[0].astype(f32), corners_ref[1].astype(f32)]
    for level in range(2):
        rows = [slot_ref[level : level + 1, :].astype(f32)]
        rows += [fractions_ref[d, level : level + 1, :] for d in range(3)]
        rows += [cot_ref[level]]
        groups.append(jnp.concatenate(rows, axis=0))
    for v in range(4):
        lanes = slice(v * LANES, (v + 1) * LANES)
        for p, value in enumerate(lane_blocks([g[:, lanes] for g in groups])):
            for t in range(8):
                out_ref[16 * t + 4 * v + p] = value


def gather_lanes(value, index):
    return jnp.take_along_axis(value, index, axis=1, mode="promise_in_bounds")


def owner_kernel(
    ids_ref, recv_ref, table_ref, m1_hbm, m2_hbm,
    tnew_ref, m1new_ref, m2new_ref, out_ref,
    grad_ref, corner_ref, aux_ref, back_ref, slots_ref, hat_ref, key_ref, column_ref, cot_ref,
    found_ref, result_ref, sems,
):
    loads = start_all((m1_hbm, m2_hbm), (m1new_ref, m2new_ref), sems)
    mine = lax.axis_index("table")
    owner = mine * lax.axis_size("ray") + lax.axis_index("ray")
    sub = iota((8, LANES), 0)
    parity = sub // 4
    lane16 = iota((16, LANES), 1)

    grad_ref[...] = jnp.zeros_like(grad_ref)
    result_ref[...] = jnp.zeros_like(result_ref)

    def unpack(t, carry):
        for v in range(4):
            rows = lane_blocks([recv_ref[t * 16 + 4 * v + p] for p in range(4)])
            corner_ref[t, v] = rows[0]
            corner_ref[8 + t, v] = rows[1]
            aux_ref[t, v] = rows[2]
            aux_ref[8 + t, v] = rows[3]
        return carry

    lax.fori_loop(0, 8, unpack, 0, unroll=8)

    first_slot = (mine * 64).astype(f32)
    hits = []
    for v in range(4):
        slot = jnp.concatenate([aux_ref[lt, v, 0:1, :] for lt in range(16)], axis=0)
        hits.append(jnp.where((slot >= first_slot) & (slot < first_slot + 64.0), 1.0, 0.0))
    row, column = iota((LANES, 2 * LANES), 0), iota((LANES, 2 * LANES), 1)
    upper = jnp.where(row <= column, 1.0, 0.0).astype(bf16)
    counts = jnp.dot(jnp.concatenate(hits, axis=0).astype(bf16), upper, preferred_element_type=f32).astype(i32)
    through = [counts[16 * v : 16 * v + 16, :LANES] for v in range(4)]
    totals = [counts[16 * v : 16 * v + 16, LANES:] for v in range(4)]
    before = [jnp.zeros_like(totals[0])]
    for v in range(4):
        before.append(before[v] + totals[v])
    passes = (jnp.max(before[4]) + (LANES - 1)) // LANES

    def locate(step):
        for v in range(4):
            rank = before[v] + through[v] - 1 - step * LANES
            inside = (hits[v] > 0.5) & (rank >= 0) & (rank < LANES)
            slots_ref[v] = jnp.where(inside, rank, -1)
            wanted = lane16 + step * LANES - before[v]
            place = jnp.zeros_like(wanted)
            for jump in (64, 32, 16, 8, 4, 2, 1):
                probe = gather_lanes(through[v], place + (jump - 1))
                place = jnp.where(probe <= wanted, place + jump, place)
            back_ref[v] = jnp.where((wanted >= 0) & (wanted < totals[v]), place, -1)

    entries = [(iota((16, LANES), 0) + 16 * i).astype(f32).astype(bf16) for i in range(8)]
    owns = [((iota((16, LANES), 0) & 7) // 4 + 2 * i).astype(f32).astype(bf16) for i in range(8)]
    one = jnp.ones((16, LANES), bf16)
    none = jnp.zeros((16, LANES), bf16)

    def compact(lt, carry):
        corner = jnp.zeros((8, LANES), f32)
        aux = jnp.zeros((8, LANES), f32)
        for v in range(4):
            place = jnp.broadcast_to(back_ref[v, pl.ds(lt, 1), :], (8, LANES))
            index = jnp.maximum(place, 0)
            corner = jnp.where(place >= 0, gather_lanes(corner_ref[lt, v], index), corner)
            aux = jnp.where(place >= 0, gather_lanes(aux_ref[lt, v], index), aux)
        hat = None
        for d in range(3):
            f = jnp.broadcast_to(aux[1 + d : 2 + d], (8, LANES))
            factor = jnp.where((sub >> d) & 1 == 1, f, 1.0 - f)
            hat = factor if hat is None else hat * factor
        entry = corner.astype(i32)
        hat_ref[lt] = hat
        key_ref[lt] = ((aux[0:1].astype(i32) & 3) * 4 + (entry >> 7)).astype(f32)
        column_ref[lt] = (entry & 127).astype(f32)
        cot_ref[lt] = jnp.where(sub < 4, pltpu.roll(aux, 4, 0), aux)
        return carry

    def hot_rows(lt):
        pieces = []
        for c in range(8):
            wanted = jnp.broadcast_to(column_ref[lt, c : c + 1, :], (16, LANES)).astype(bf16)
            pieces.append(jnp.concatenate([jnp.where(wanted == entries[i], one, none) for i in range(8)], axis=0))
        return jnp.concatenate(pieces, axis=1)

    def block_of(lt, slot):
        level, group = lt // 8, lt % 8
        return level * 64 + ids_ref[(group * 2 + level) * 4 + slot, owner]

    def accumulate(lt, carry):
        cot = cot_ref[lt]
        columns = []
        for c in range(8):
            value = cot * hat_ref[lt, c : c + 1, :]
            high = value.astype(bf16).astype(f32)
            both = jnp.concatenate([high, value - high], axis=0).astype(bf16)
            key = jnp.broadcast_to(key_ref[lt, c : c + 1, :], (16, LANES)).astype(bf16)
            columns.append(jnp.concatenate([jnp.where(key == owns[i], both, none) for i in range(8)], axis=0))
        sums = lax.dot_general(
            jnp.concatenate(columns, axis=1), hot_rows(lt), (((1,), (1,)), ((), ())), preferred_element_type=f32
        )
        for slot in range(4):
            block = block_of(lt, slot)
            for half in range(2):
                at = 32 * slot + 16 * half
                grad_ref[block, 8 * half : 8 * half + 8, :] += sums[at : at + 8] + sums[at + 8 : at + 16]
        return carry

    def gather_pass(step, carry):
        locate(step)
        lax.fori_loop(0, 16, compact, 0, unroll=4)
        lax.fori_loop(0, 16, accumulate, 0, unroll=4)
        return carry

    lax.fori_loop(0, passes, gather_pass, 0)

    wait_all(loads)

    def update(step, carry):
        at = pl.ds(step * 4, 4)
        grad = grad_ref[at]
        first = beta_one * m1new_ref[at] + (1.0 - beta_one) * grad
        second = beta_two * m2new_ref[at] + (1.0 - beta_two) * grad * grad
        m1new_ref[at] = first
        m2new_ref[at] = second
        tnew_ref[at] = table_ref[at] - learn_rate * first / (jnp.sqrt(second) + adam_eps)
        return carry

    lax.fori_loop(0, 32, update, 0)

    def look(lt, carry):
        rows = jnp.concatenate([tnew_ref[block_of(lt, slot)] for slot in range(4)], axis=0)
        high = rows.astype(bf16)
        low = (rows - high.astype(f32)).astype(bf16)
        hot = hot_rows(lt)
        seen = jnp.dot(
            jnp.concatenate([high, low], axis=1), jnp.concatenate([hot, hot], axis=0), preferred_element_type=f32
        )
        total = jnp.zeros((8, LANES), f32)
        for c in range(8):
            own = jnp.broadcast_to(key_ref[lt, c : c + 1, :], (8, LANES))
            picked = jnp.zeros((8, LANES), f32)
            for i in range(8):
                mask = own == (parity + 2 * i).astype(f32)
                picked = jnp.where(mask, seen[8 * i : 8 * i + 8, c * LANES : (c + 1) * LANES], picked)
            total = total + picked * hat_ref[lt, c : c + 1, :]
        found_ref[lt] = total + pltpu.roll(total, 4, 0)
        return carry

    def spread(t, carry):
        value = jnp.where(sub < 4, found_ref[t], found_ref[8 + t])
        for v in range(4):
            zero = jnp.broadcast_to(slots_ref[v, pl.ds(t, 1), :], (8, LANES))
            one = jnp.broadcast_to(slots_ref[v, pl.ds(8 + t, 1), :], (8, LANES))
            place = jnp.where(sub < 4, zero, one)
            taken = gather_lanes(value, jnp.maximum(place, 0))
            result_ref[t * 4 + v] += jnp.where(place >= 0, taken, 0.0)
        return carry

    def look_pass(step, carry):
        @pl.when(passes > 1)
        def _():
            locate(step)
            lax.fori_loop(0, 16, compact, 0)

        lax.fori_loop(0, 16, look, 0, unroll=4)
        lax.fori_loop(0, 8, spread, 0, unroll=2)
        return carry

    lax.fori_loop(0, passes, look_pass, 0)
    for m in range(32):
        out_ref[m] = tile_blocks(result_ref[m])


def network_kernel(recv_ref, win_ref, wout_ref, out_ref):
    columns = []
    for v in range(4):
        total = recv_ref[v]
        for t in range(1, 8):
            total = total + recv_ref[4 * t + v]
        columns.append(tile_blocks(total))
    encoded = jnp.concatenate(columns, axis=1)
    hidden = jnp.maximum(
        lax.dot_general(
            win_ref[...], encoded, (((0,), (0,)), ((), ())),
            precision=lax.Precision.HIGHEST, preferred_element_type=f32,
        ),
        0.0,
    )
    out_ref[...] = jnp.dot(wout_ref[...], hidden, precision=lax.Precision.HIGHEST, preferred_element_type=f32)


VMEM = pl.BlockSpec(memory_space=pltpu.VMEM)
HBM = pl.BlockSpec(memory_space=pltpu.HBM)
SMEM = pl.BlockSpec(memory_space=pltpu.SMEM)


def call(kernel, outs, in_specs, scratch=(), out_specs=None, **extra):
    return pl.pallas_call(
        kernel,
        out_shape=[jax.ShapeDtypeStruct(*o) if isinstance(o, tuple) else o for o in outs],
        in_specs=in_specs,
        out_specs=[VMEM] * len(outs) if out_specs is None else out_specs,
        scratch_shapes=list(scratch),
        compiler_params=pltpu.CompilerParams(vmem_limit_bytes=VMEM_LIMIT),
        **extra,
    )


def in_hbm(*arrays):
    return [pltpu.with_memory_space_constraint(array, pltpu.HBM) for array in arrays]


def exchange(value):
    return lax.all_to_all(value, ("table", "ray"), split_axis=0, concat_axis=0, tiled=True)


def rows_of(array):
    levels, blocks = array.shape[:2]
    return array.reshape(levels, blocks, 4, 4, LANES).transpose(0, 1, 3, 2, 4).reshape(levels * blocks, 16, LANES)


def rows_back(array, shape):
    levels, blocks = shape[:2]
    return array.reshape(levels, blocks, 4, 4, LANES).transpose(0, 1, 3, 2, 4).reshape(shape)


def on_device(
    table,
    moment1,
    moment2,
    block_ids,
    sample_slot,
    corners,
    fractions,
    feat_cot,
    weight_in,
    weight_out,
):
    (packed,) = call(
        pack_kernel,
        [((128, 8, LANES), f32)],
        [HBM] * 4,
        [
            pltpu.VMEM((2, 512), i32),
            pltpu.VMEM((2, 8, 512), i32),
            pltpu.VMEM((3, 2, 512), f32),
            pltpu.VMEM((2, 4, 512), f32),
            pltpu.SemaphoreType.DMA((4,)),
        ],
    )(*in_hbm(sample_slot, corners, fractions.transpose(1, 0, 2), feat_cot))
    samples = exchange(packed)
    rows = (128, 16, LANES)
    ids = block_ids.transpose(0, 1, 3, 2).reshape(64, 128)
    tnew, m1new, m2new, found = call(
        owner_kernel,
        [pltpu.VMEM(rows, f32)] * 3 + [((32, 8, LANES), f32)],
        [SMEM, VMEM, VMEM, HBM, HBM],
        [
            pltpu.VMEM(rows, f32),
            pltpu.VMEM((16, 4, 8, LANES), f32),
            pltpu.VMEM((16, 4, 8, LANES), f32),
            pltpu.VMEM((4, 16, LANES), i32),
            pltpu.VMEM((4, 16, LANES), i32),
            pltpu.VMEM((16, 8, LANES), f32),
            pltpu.VMEM((16, 8, LANES), f32),
            pltpu.VMEM((16, 8, LANES), f32),
            pltpu.VMEM((16, 8, LANES), f32),
            pltpu.VMEM((16, 8, LANES), f32),
            pltpu.VMEM((32, 8, LANES), f32),
            pltpu.SemaphoreType.DMA((2,)),
        ],
    )(*in_hbm(ids), samples, rows_of(table), *in_hbm(rows_of(moment1), rows_of(moment2)))
    back = exchange(found.reshape(128, 2, LANES)).reshape(32, 8, LANES)
    (mlp_out,) = call(network_kernel, [((16, 512), f32)], [VMEM] * 3)(back, weight_in.T, weight_out)
    shape = table.shape
    return (rows_back(tnew, shape), rows_back(m1new, shape), rows_back(m2new, shape), mlp_out)


def solution(mesh):
    in_specs = (
        P(None, ("table", "ray"), None, None),
        P(None, ("table", "ray"), None, None),
        P(None, ("table", "ray"), None, None),
        P(),
        P(None, ("table", "ray")),
        P(None, None, ("table", "ray")),
        P(None, None, ("table", "ray")),
        P(None, None, ("table", "ray")),
        P(),
        P(),
    )
    out_specs = (
        P(None, ("table", "ray"), None, None),
        P(None, ("table", "ray"), None, None),
        P(None, ("table", "ray"), None, None),
        P(None, ("table", "ray")),
    )
    return jax.shard_map(
        on_device, mesh=mesh, in_specs=in_specs, out_specs=out_specs, check_vma=False
    )
```

```python
import jax
import jax.numpy as jnp
from jax import lax
from jax.experimental import pallas as pl
from jax.experimental.pallas import tpu as pltpu
from jax.sharding import PartitionSpec as P

beta_one = 0.9
beta_two = 0.99
learn_rate = 0.01
adam_eps = 1e-15

LANES = 128
RUN = 32
VMEM_LIMIT = 16 << 20
f32, bf16, i32 = jnp.float32, jnp.bfloat16, jnp.int32


def iota(shape, axis):
    return lax.broadcasted_iota(i32, shape, axis)


def lane_blocks(pieces):
    lane = iota(pieces[0].shape, 1)
    for width in (2 * RUN, RUN):
        low = (lane & width) == 0
        step = width // RUN
        results = list(pieces)
        for one in range(4):
            if not one & step:
                x, y = pieces[one], pieces[one + step]
                results[one] = jnp.where(low, x, pltpu.roll(y, width, 1))
                results[one + step] = jnp.where(low, pltpu.roll(x, LANES - width, 1), y)
        pieces = results
    return pieces


def tile_blocks(value):
    shift = (iota((8, LANES), 0) // 2 - iota((8, LANES), 1) // RUN) & 3
    result = value
    for d in range(1, 4):
        moved = pltpu.roll(pltpu.roll(value, 2 * d, 0), LANES - RUN * d, 1)
        result = jnp.where(shift == d, moved, result)
    return result


def start_all(sources, targets, sems):
    copies = [pltpu.make_async_copy(x, y, sems.at[n]) for n, (x, y) in enumerate(zip(sources, targets))]
    for copy in copies:
        copy.start()
    return copies


def wait_all(copies):
    for copy in copies:
        copy.wait()


def pack_kernel(slot_hbm, corners_hbm, fractions_hbm, cot_hbm, out_ref, slot_ref, corners_ref, fractions_ref, cot_ref, sems):
    wait_all(
        start_all(
            (slot_hbm, corners_hbm, fractions_hbm, cot_hbm), (slot_ref, corners_ref, fractions_ref, cot_ref), sems
        )
    )
    groups = [corners_ref[0].astype(f32), corners_ref[1].astype(f32)]
    for level in range(2):
        rows = [slot_ref[level : level + 1, :].astype(f32)]
        rows += [fractions_ref[d, level : level + 1, :] for d in range(3)]
        rows += [cot_ref[level]]
        groups.append(jnp.concatenate(rows, axis=0))
    for v in range(4):
        lanes = slice(v * LANES, (v + 1) * LANES)
        for p, value in enumerate(lane_blocks([g[:, lanes] for g in groups])):
            for t in range(8):
                out_ref[16 * t + 4 * v + p] = value


def gather_lanes(value, index):
    return jnp.take_along_axis(value, index, axis=1, mode="promise_in_bounds")


def owner_kernel(
    ids_hbm, recv_ref, table_ref, m1_hbm, m2_hbm,
    tnew_ref, m1new_ref, m2new_ref, out_ref,
    ids_ref, grad_ref, corner_ref, aux_ref, slots_ref, hat_ref, key_ref, column_ref, cot_ref,
    found_ref, result_ref, sems,
):
    loads = start_all((ids_hbm, m1_hbm, m2_hbm), (ids_ref, m1new_ref, m2new_ref), sems)
    mine = lax.axis_index("table")
    owner = mine * lax.axis_size("ray") + lax.axis_index("ray")
    sub = iota((8, LANES), 0)
    parity = sub // 4

    grad_ref[...] = jnp.zeros_like(grad_ref)
    result_ref[...] = jnp.zeros_like(result_ref)

    def unpack(t, carry):
        for v in range(4):
            rows = lane_blocks([recv_ref[t * 16 + 4 * v + p] for p in range(4)])
            corner_ref[t, v] = rows[0]
            corner_ref[8 + t, v] = rows[1]
            aux_ref[t, v] = rows[2]
            aux_ref[8 + t, v] = rows[3]
        return carry

    lax.fori_loop(0, 8, unpack, 0, unroll=8)

    first_slot = (mine * 64).astype(f32)
    hits = []
    for v in range(4):
        slot = jnp.concatenate([aux_ref[lt, v, 0:1, :] for lt in range(16)], axis=0)
        hits.append(jnp.where((slot >= first_slot) & (slot < first_slot + 64.0), 1.0, 0.0))
    row, column = iota((LANES, 2 * LANES), 0), iota((LANES, 2 * LANES), 1)
    upper = jnp.where(row <= column, 1.0, 0.0).astype(bf16)
    counts = jnp.dot(jnp.concatenate(hits, axis=0).astype(bf16), upper, preferred_element_type=f32).astype(i32)
    through = [counts[16 * v : 16 * v + 16, :LANES] for v in range(4)]
    totals = [counts[16 * v : 16 * v + 16, LANES:] for v in range(4)]
    before = [jnp.zeros_like(totals[0])]
    for v in range(4):
        before.append(before[v] + totals[v])
    passes = (jnp.max(before[4]) + (LANES - 1)) // LANES

    def locate(step):
        for v in range(4):
            rank = before[v] + through[v] - 1 - step * LANES
            inside = (hits[v] > 0.5) & (rank >= 0) & (rank < LANES)
            slots_ref[v] = jnp.where(inside, rank, -1)

    entries = [(iota((16, LANES), 0) + 16 * i).astype(f32).astype(bf16) for i in range(8)]
    owns = [((iota((16, LANES), 0) & 7) // 4 + 2 * i).astype(f32).astype(bf16) for i in range(8)]
    one = jnp.ones((16, LANES), bf16)
    none = jnp.zeros((16, LANES), bf16)

    def compact(lt, carry):
        high, low, chosen = [], [], []
        for v in range(4):
            piece = jnp.concatenate([corner_ref[lt, v], aux_ref[lt, v]], axis=0)
            high.append(piece.astype(bf16))
            low.append((piece - high[v].astype(f32)).astype(bf16))
            slot = jnp.broadcast_to(slots_ref[v, pl.ds(lt, 1), :].astype(f32), (16, LANES)).astype(bf16)
            chosen.append(jnp.concatenate([jnp.where(slot == entries[i], one, none) for i in range(8)], axis=0))
        rows = jnp.concatenate([jnp.concatenate(high, axis=1), jnp.concatenate(low, axis=1)], axis=0)
        both = lax.dot_general(
            rows, jnp.concatenate(chosen, axis=1), (((1,), (1,)), ((), ())), preferred_element_type=f32
        )
        corner, aux = both[:8] + both[16:24], both[8:16] + both[24:]
        hat = None
        for d in range(3):
            f = jnp.broadcast_to(aux[1 + d : 2 + d], (8, LANES))
            factor = jnp.where((sub >> d) & 1 == 1, f, 1.0 - f)
            hat = factor if hat is None else hat * factor
        entry = corner.astype(i32)
        hat_ref[lt] = hat
        key_ref[lt] = ((aux[0:1].astype(i32) & 3) * 4 + (entry >> 7)).astype(f32)
        column_ref[lt] = (entry & 127).astype(f32)
        cot_ref[lt] = jnp.where(sub < 4, pltpu.roll(aux, 4, 0), aux)
        return carry

    def hot_rows(lt):
        pieces = []
        for c in range(8):
            wanted = jnp.broadcast_to(column_ref[lt, c : c + 1, :], (16, LANES)).astype(bf16)
            pieces.append(jnp.concatenate([jnp.where(wanted == entries[i], one, none) for i in range(8)], axis=0))
        return jnp.concatenate(pieces, axis=1)

    def block_of(lt, slot):
        level, group = lt // 8, lt % 8
        return level * 64 + ids_ref[(group * 2 + level) * 4 + slot, owner]

    def accumulate(lt, carry):
        cot = cot_ref[lt]
        columns = []
        for c in range(8):
            value = cot * hat_ref[lt, c : c + 1, :]
            high = value.astype(bf16).astype(f32)
            both = jnp.concatenate([high, value - high], axis=0).astype(bf16)
            key = jnp.broadcast_to(key_ref[lt, c : c + 1, :], (16, LANES)).astype(bf16)
            columns.append(jnp.concatenate([jnp.where(key == owns[i], both, none) for i in range(8)], axis=0))
        sums = lax.dot_general(
            jnp.concatenate(columns, axis=1), hot_rows(lt), (((1,), (1,)), ((), ())), preferred_element_type=f32
        )
        for slot in range(4):
            block = block_of(lt, slot)
            for half in range(2):
                at = 32 * slot + 16 * half
                grad_ref[block, 8 * half : 8 * half + 8, :] += sums[at : at + 8] + sums[at + 8 : at + 16]
        return carry

    locate(0)
    lax.fori_loop(0, 16, compact, 0, unroll=4)
    loads[0].wait()
    lax.fori_loop(0, 16, accumulate, 0, unroll=4)

    def gather_pass(step, carry):
        locate(step)
        lax.fori_loop(0, 16, compact, 0)
        lax.fori_loop(0, 16, accumulate, 0)
        return carry

    lax.fori_loop(1, passes, gather_pass, 0)
    wait_all(loads[1:])

    def update(step, carry):
        at = pl.ds(step * 4, 4)
        grad = grad_ref[at]
        first = beta_one * m1new_ref[at] + (1.0 - beta_one) * grad
        second = beta_two * m2new_ref[at] + (1.0 - beta_two) * grad * grad
        m1new_ref[at] = first
        m2new_ref[at] = second
        tnew_ref[at] = table_ref[at] - learn_rate * first / (jnp.sqrt(second) + adam_eps)
        return carry

    lax.fori_loop(0, 32, update, 0)

    def look(lt, carry):
        rows = jnp.concatenate([tnew_ref[block_of(lt, slot)] for slot in range(4)], axis=0)
        high = rows.astype(bf16)
        low = (rows - high.astype(f32)).astype(bf16)
        hot = hot_rows(lt)
        seen = jnp.dot(
            jnp.concatenate([high, low], axis=1), jnp.concatenate([hot, hot], axis=0), preferred_element_type=f32
        )
        total = jnp.zeros((8, LANES), f32)
        for c in range(8):
            own = jnp.broadcast_to(key_ref[lt, c : c + 1, :], (8, LANES))
            picked = jnp.zeros((8, LANES), f32)
            for i in range(8):
                mask = own == (parity + 2 * i).astype(f32)
                picked = jnp.where(mask, seen[8 * i : 8 * i + 8, c * LANES : (c + 1) * LANES], picked)
            total = total + picked * hat_ref[lt, c : c + 1, :]
        found_ref[lt] = total + pltpu.roll(total, 4, 0)
        return carry

    def spread(t, carry):
        value = jnp.where(sub < 4, found_ref[t], found_ref[8 + t])
        for v in range(4):
            zero = jnp.broadcast_to(slots_ref[v, pl.ds(t, 1), :], (8, LANES))
            one = jnp.broadcast_to(slots_ref[v, pl.ds(8 + t, 1), :], (8, LANES))
            place = jnp.where(sub < 4, zero, one)
            taken = gather_lanes(value, jnp.maximum(place, 0))
            result_ref[t * 4 + v] += jnp.where(place >= 0, taken, 0.0)
        return carry

    def look_pass(step, carry):
        locate(step)
        lax.fori_loop(0, 16, compact, 0)
        lax.fori_loop(0, 16, look, 0)
        lax.fori_loop(0, 8, spread, 0)
        return carry

    @pl.when(passes > 1)
    def _():
        locate(0)
        lax.fori_loop(0, 16, compact, 0)

    lax.fori_loop(0, 16, look, 0, unroll=4)
    lax.fori_loop(0, 8, spread, 0, unroll=2)
    lax.fori_loop(1, passes, look_pass, 0)
    for m in range(32):
        out_ref[m] = tile_blocks(result_ref[m])


def network_kernel(recv_ref, win_ref, wout_ref, out_ref):
    columns = []
    for v in range(4):
        total = recv_ref[v]
        for t in range(1, 8):
            total = total + recv_ref[4 * t + v]
        columns.append(tile_blocks(total))
    encoded = jnp.concatenate(columns, axis=1)
    hidden = jnp.maximum(
        lax.dot_general(
            win_ref[...], encoded, (((0,), (0,)), ((), ())),
            precision=lax.Precision.HIGHEST, preferred_element_type=f32,
        ),
        0.0,
    )
    out_ref[...] = jnp.dot(wout_ref[...], hidden, precision=lax.Precision.HIGHEST, preferred_element_type=f32)


VMEM = pl.BlockSpec(memory_space=pltpu.VMEM)
HBM = pl.BlockSpec(memory_space=pltpu.HBM)


def call(kernel, outs, in_specs, scratch=(), out_specs=None, **extra):
    return pl.pallas_call(
        kernel,
        out_shape=[jax.ShapeDtypeStruct(*o) if isinstance(o, tuple) else o for o in outs],
        in_specs=in_specs,
        out_specs=[VMEM] * len(outs) if out_specs is None else out_specs,
        scratch_shapes=list(scratch),
        compiler_params=pltpu.CompilerParams(vmem_limit_bytes=VMEM_LIMIT),
        **extra,
    )


def in_hbm(*arrays):
    return [pltpu.with_memory_space_constraint(array, pltpu.HBM) for array in arrays]


def exchange(value):
    return lax.all_to_all(value, ("table", "ray"), split_axis=0, concat_axis=0, tiled=True)


def rows_of(array):
    levels, blocks = array.shape[:2]
    return array.reshape(levels, blocks, 4, 4, LANES).transpose(0, 1, 3, 2, 4).reshape(levels * blocks, 16, LANES)


def rows_back(array, shape):
    levels, blocks = shape[:2]
    return array.reshape(levels, blocks, 4, 4, LANES).transpose(0, 1, 3, 2, 4).reshape(shape)


def on_device(
    table,
    moment1,
    moment2,
    block_ids,
    sample_slot,
    corners,
    fractions,
    feat_cot,
    weight_in,
    weight_out,
):
    (packed,) = call(
        pack_kernel,
        [((128, 8, LANES), f32)],
        [HBM] * 4,
        [
            pltpu.VMEM((2, 512), i32),
            pltpu.VMEM((2, 8, 512), i32),
            pltpu.VMEM((3, 2, 512), f32),
            pltpu.VMEM((2, 4, 512), f32),
            pltpu.SemaphoreType.DMA((4,)),
        ],
    )(*in_hbm(sample_slot, corners, fractions.transpose(1, 0, 2), feat_cot))
    samples = exchange(packed)
    rows = (128, 16, LANES)
    ids = block_ids.transpose(0, 1, 3, 2).reshape(64, 128)
    tnew, m1new, m2new, found = call(
        owner_kernel,
        [pltpu.VMEM(rows, f32)] * 3 + [((32, 8, LANES), f32)],
        [HBM, VMEM, VMEM, HBM, HBM],
        [
            pltpu.SMEM((64, LANES), i32),
            pltpu.VMEM(rows, f32),
            pltpu.VMEM((16, 4, 8, LANES), f32),
            pltpu.VMEM((16, 4, 8, LANES), f32),
            pltpu.VMEM((4, 16, LANES), i32),
            pltpu.VMEM((16, 8, LANES), f32),
            pltpu.VMEM((16, 8, LANES), f32),
            pltpu.VMEM((16, 8, LANES), f32),
            pltpu.VMEM((16, 8, LANES), f32),
            pltpu.VMEM((16, 8, LANES), f32),
            pltpu.VMEM((32, 8, LANES), f32),
            pltpu.SemaphoreType.DMA((3,)),
        ],
    )(*in_hbm(ids), samples, rows_of(table), *in_hbm(rows_of(moment1), rows_of(moment2)))
    back = exchange(found.reshape(128, 2, LANES)).reshape(32, 8, LANES)
    (mlp_out,) = call(network_kernel, [((16, 512), f32)], [VMEM] * 3)(back, weight_in.T, weight_out)
    shape = table.shape
    return (rows_back(tnew, shape), rows_back(m1new, shape), rows_back(m2new, shape), mlp_out)


def solution(mesh):
    in_specs = (
        P(None, ("table", "ray"), None, None),
        P(None, ("table", "ray"), None, None),
        P(None, ("table", "ray"), None, None),
        P(),
        P(None, ("table", "ray")),
        P(None, None, ("table", "ray")),
        P(None, None, ("table", "ray")),
        P(None, None, ("table", "ray")),
        P(),
        P(),
    )
    out_specs = (
        P(None, ("table", "ray"), None, None),
        P(None, ("table", "ray"), None, None),
        P(None, ("table", "ray"), None, None),
        P(None, ("table", "ray")),
    )
    return jax.shard_map(
        on_device, mesh=mesh, in_specs=in_specs, out_specs=out_specs, check_vma=False
    )
```

```python
import jax
import jax.numpy as jnp
from jax import lax
from jax.experimental import pallas as pl
from jax.experimental.pallas import tpu as pltpu
from jax.sharding import PartitionSpec as P

beta_one = 0.9
beta_two = 0.99
learn_rate = 0.01
adam_eps = 1e-15

LANES = 128
RUN = 32
VMEM_LIMIT = 16 << 20
f32, bf16, i32 = jnp.float32, jnp.bfloat16, jnp.int32


def iota(shape, axis):
    return lax.broadcasted_iota(i32, shape, axis)


def lane_blocks(pieces):
    lane = iota(pieces[0].shape, 1)
    for width in (2 * RUN, RUN):
        low = (lane & width) == 0
        step = width // RUN
        results = list(pieces)
        for one in range(4):
            if not one & step:
                x, y = pieces[one], pieces[one + step]
                results[one] = jnp.where(low, x, pltpu.roll(y, width, 1))
                results[one + step] = jnp.where(low, pltpu.roll(x, LANES - width, 1), y)
        pieces = results
    return pieces


def tile_blocks(value):
    shift = (iota((8, LANES), 0) // 2 - iota((8, LANES), 1) // RUN) & 3
    result = value
    for d in range(1, 4):
        moved = pltpu.roll(pltpu.roll(value, 2 * d, 0), LANES - RUN * d, 1)
        result = jnp.where(shift == d, moved, result)
    return result


def start_all(sources, targets, sems):
    copies = [pltpu.make_async_copy(x, y, sems.at[n]) for n, (x, y) in enumerate(zip(sources, targets))]
    for copy in copies:
        copy.start()
    return copies


def wait_all(copies):
    for copy in copies:
        copy.wait()


def pack_kernel(slot_hbm, corners_hbm, fractions_hbm, cot_hbm, out_ref, slot_ref, corners_ref, fractions_ref, cot_ref, sems):
    wait_all(
        start_all(
            (slot_hbm, corners_hbm, fractions_hbm, cot_hbm), (slot_ref, corners_ref, fractions_ref, cot_ref), sems
        )
    )
    groups = [corners_ref[0].astype(f32), corners_ref[1].astype(f32)]
    for level in range(2):
        rows = [slot_ref[level : level + 1, :].astype(f32)]
        rows += [fractions_ref[d, level : level + 1, :] for d in range(3)]
        rows += [cot_ref[level]]
        groups.append(jnp.concatenate(rows, axis=0))
    for v in range(4):
        lanes = slice(v * LANES, (v + 1) * LANES)
        for p, value in enumerate(lane_blocks([g[:, lanes] for g in groups])):
            for t in range(4):
                out_ref[16 * t + 4 * v + p] = value


def gather_lanes(value, index):
    return jnp.take_along_axis(value, index, axis=1, mode="promise_in_bounds")


class Half:
    def __init__(self, recv_ref, corner_ref, aux_ref, slots_ref, hat_ref, key_ref, column_ref, cot_ref):
        self.recv_ref, self.corner_ref, self.aux_ref, self.slots_ref = recv_ref, corner_ref, aux_ref, slots_ref
        self.hat_ref, self.key_ref, self.column_ref, self.cot_ref = hat_ref, key_ref, column_ref, cot_ref
        self.entries = [(iota((16, LANES), 0) + 16 * i).astype(f32).astype(bf16) for i in range(8)]
        self.owns = [((iota((16, LANES), 0) & 7) // 4 + 2 * i).astype(f32).astype(bf16) for i in range(8)]
        self.one = jnp.ones((16, LANES), bf16)
        self.none = jnp.zeros((16, LANES), bf16)
        self.sub = iota((8, LANES), 0)

    def count(self, unroll):
        def unpack(t, carry):
            for v in range(4):
                rows = lane_blocks([self.recv_ref[t * 16 + 4 * v + p] for p in range(4)])
                self.corner_ref[t, v] = rows[0]
                self.corner_ref[4 + t, v] = rows[1]
                self.aux_ref[t, v] = rows[2]
                self.aux_ref[4 + t, v] = rows[3]
            return carry

        lax.fori_loop(0, 4, unpack, 0, unroll=unroll)
        first_slot = (lax.axis_index("table") * 64).astype(f32)
        self.hits = []
        for v in range(4):
            slot = jnp.concatenate([self.aux_ref[lt, v, 0:1, :] for lt in range(8)], axis=0)
            self.hits.append(jnp.where((slot >= first_slot) & (slot < first_slot + 64.0), 1.0, 0.0))
        row, column = iota((LANES, 2 * LANES), 0), iota((LANES, 2 * LANES), 1)
        upper = jnp.where(row <= column, 1.0, 0.0).astype(bf16)
        hits = jnp.concatenate(self.hits, axis=0).astype(bf16)
        counts = jnp.dot(hits, upper, preferred_element_type=f32).astype(i32)
        self.through = [counts[8 * v : 8 * v + 8, :LANES] for v in range(4)]
        self.before = [jnp.zeros((8, LANES), i32)]
        for v in range(4):
            self.before.append(self.before[v] + counts[8 * v : 8 * v + 8, LANES:])
        self.total = self.before[4]

    def gather(self, step, unroll):
        for v in range(4):
            rank = self.before[v] + self.through[v] - 1 - step * LANES
            inside = (self.hits[v] > 0.5) & (rank >= 0) & (rank < LANES)
            self.slots_ref[v] = jnp.where(inside, rank, -1)
        lax.fori_loop(0, 8, self.compact, 0, unroll=unroll)

    def compact(self, lt, carry):
        high, low, chosen = [], [], []
        for v in range(4):
            piece = jnp.concatenate([self.corner_ref[lt, v], self.aux_ref[lt, v]], axis=0)
            high.append(piece.astype(bf16))
            low.append((piece - high[v].astype(f32)).astype(bf16))
            slot = jnp.broadcast_to(self.slots_ref[v, pl.ds(lt, 1), :].astype(f32), (16, LANES)).astype(bf16)
            chosen.append(
                jnp.concatenate([jnp.where(slot == self.entries[i], self.one, self.none) for i in range(8)], axis=0)
            )
        rows = jnp.concatenate([jnp.concatenate(high, axis=1), jnp.concatenate(low, axis=1)], axis=0)
        both = lax.dot_general(
            rows, jnp.concatenate(chosen, axis=1), (((1,), (1,)), ((), ())), preferred_element_type=f32
        )
        corner, aux = both[:8] + both[16:24], both[8:16] + both[24:]
        hat = None
        for d in range(3):
            f = jnp.broadcast_to(aux[1 + d : 2 + d], (8, LANES))
            factor = jnp.where((self.sub >> d) & 1 == 1, f, 1.0 - f)
            hat = factor if hat is None else hat * factor
        entry = corner.astype(i32)
        self.hat_ref[lt] = hat
        self.key_ref[lt] = ((aux[0:1].astype(i32) & 3) * 4 + (entry >> 7)).astype(f32)
        self.column_ref[lt] = (entry & 127).astype(f32)
        self.cot_ref[lt] = jnp.where(self.sub < 4, pltpu.roll(aux, 4, 0), aux)
        return carry

    def hot_rows(self, lt):
        pieces = []
        for c in range(8):
            wanted = jnp.broadcast_to(self.column_ref[lt, c : c + 1, :], (16, LANES)).astype(bf16)
            pieces.append(
                jnp.concatenate([jnp.where(wanted == self.entries[i], self.one, self.none) for i in range(8)], axis=0)
            )
        return jnp.concatenate(pieces, axis=1)

    def accumulate(self, grad_ref, blocks):
        def one_group(lt, carry):
            cot = self.cot_ref[lt]
            columns = []
            for c in range(8):
                value = cot * self.hat_ref[lt, c : c + 1, :]
                high = value.astype(bf16).astype(f32)
                both = jnp.concatenate([high, value - high], axis=0).astype(bf16)
                key = jnp.broadcast_to(self.key_ref[lt, c : c + 1, :], (16, LANES)).astype(bf16)
                columns.append(
                    jnp.concatenate([jnp.where(key == self.owns[i], both, self.none) for i in range(8)], axis=0)
                )
            sums = lax.dot_general(
                jnp.concatenate(columns, axis=1), self.hot_rows(lt), (((1,), (1,)), ((), ())),
                preferred_element_type=f32,
            )
            for slot in range(4):
                block = blocks(lt, slot)
                for half in range(2):
                    at = 32 * slot + 16 * half
                    grad_ref[block, 8 * half : 8 * half + 8, :] += sums[at : at + 8] + sums[at + 8 : at + 16]
            return carry

        return one_group

    def look(self, table_ref, found_ref, blocks):
        parity = self.sub // 4

        def one_group(lt, carry):
            rows = jnp.concatenate([table_ref[blocks(lt, slot)] for slot in range(4)], axis=0)
            high = rows.astype(bf16)
            low = (rows - high.astype(f32)).astype(bf16)
            hot = self.hot_rows(lt)
            seen = jnp.dot(
                jnp.concatenate([high, low], axis=1), jnp.concatenate([hot, hot], axis=0), preferred_element_type=f32
            )
            total = jnp.zeros((8, LANES), f32)
            for c in range(8):
                own = jnp.broadcast_to(self.key_ref[lt, c : c + 1, :], (8, LANES))
                picked = jnp.zeros((8, LANES), f32)
                for i in range(8):
                    mask = own == (parity + 2 * i).astype(f32)
                    picked = jnp.where(mask, seen[8 * i : 8 * i + 8, c * LANES : (c + 1) * LANES], picked)
                total = total + picked * self.hat_ref[lt, c : c + 1, :]
            found_ref[lt] = total + pltpu.roll(total, 4, 0)
            return carry

        return one_group

    def spread(self, found_ref, result_ref):
        def one_group(t, carry):
            value = jnp.where(self.sub < 4, found_ref[t], found_ref[4 + t])
            for v in range(4):
                zero = jnp.broadcast_to(self.slots_ref[v, pl.ds(t, 1), :], (8, LANES))
                one = jnp.broadcast_to(self.slots_ref[v, pl.ds(4 + t, 1), :], (8, LANES))
                place = jnp.where(self.sub < 4, zero, one)
                taken = gather_lanes(value, jnp.maximum(place, 0))
                result_ref[t * 4 + v] += jnp.where(place >= 0, taken, 0.0)
            return carry

        return one_group


def passes_of(total):
    return (jnp.max(total) + (LANES - 1)) // LANES


def block_finder(ids_ref, other):
    mine = lax.axis_index("table")
    owner = mine * lax.axis_size("ray") + lax.axis_index("ray")
    parity = (mine + other) % 2

    def blocks(lt, slot):
        level, group = lt // 4, 2 * (lt % 4) + parity
        return level * 64 + ids_ref[(group * 2 + level) * 4 + slot, owner]

    return blocks


def gradients(half, grad_ref, blocks, ready):
    half.count(4)
    half.gather(0, 4)
    ready()
    step = half.accumulate(grad_ref, blocks)
    lax.fori_loop(0, 8, step, 0, unroll=4)
    passes = passes_of(half.total)

    def again(number, carry):
        half.gather(number, 1)
        return lax.fori_loop(0, 8, step, carry)

    lax.fori_loop(1, passes, again, 0)

    @pl.when(passes > 1)
    def _():
        half.gather(0, 1)

    return passes


def first_kernel(
    ids_hbm, recv_ref, m1_hbm, m2_hbm,
    grad_ref, slots_ref, hat_ref, key_ref, column_ref, total_ref, m1_ref, m2_ref,
    ids_ref, corner_ref, aux_ref, cot_ref, sems,
):
    loads = start_all((ids_hbm, m1_hbm, m2_hbm), (ids_ref, m1_ref, m2_ref), sems)
    grad_ref[...] = jnp.zeros_like(grad_ref)
    half = Half(recv_ref, corner_ref, aux_ref, slots_ref, hat_ref, key_ref, column_ref, cot_ref)
    gradients(half, grad_ref, block_finder(ids_ref, 0), loads[0].wait)
    total_ref[...] = half.total
    wait_all(loads[1:])


def second_kernel(
    ids_hbm, recv_ref, before_ref, table_ref, m1_ref, m2_ref,
    tnew_ref, m1new_ref, m2new_ref, out_ref,
    ids_ref, grad_ref, corner_ref, aux_ref, slots_ref, hat_ref, key_ref, column_ref, cot_ref,
    found_ref, result_ref, sem,
):
    (load,) = start_all((ids_hbm,), (ids_ref,), sem)
    grad_ref[...] = before_ref[...]
    result_ref[...] = jnp.zeros_like(result_ref)
    half = Half(recv_ref, corner_ref, aux_ref, slots_ref, hat_ref, key_ref, column_ref, cot_ref)
    blocks = block_finder(ids_ref, 1)
    passes = gradients(half, grad_ref, blocks, load.wait)

    def update(step, carry):
        at = pl.ds(step * 4, 4)
        grad = grad_ref[at]
        first = beta_one * m1_ref[at] + (1.0 - beta_one) * grad
        second = beta_two * m2_ref[at] + (1.0 - beta_two) * grad * grad
        m1new_ref[at] = first
        m2new_ref[at] = second
        tnew_ref[at] = table_ref[at] - learn_rate * first / (jnp.sqrt(second) + adam_eps)
        return carry

    lax.fori_loop(0, 32, update, 0)
    look, spread = half.look(tnew_ref, found_ref, blocks), half.spread(found_ref, result_ref)
    lax.fori_loop(0, 8, look, 0, unroll=4)
    lax.fori_loop(0, 4, spread, 0, unroll=2)

    def again(number, carry):
        half.gather(number, 1)
        lax.fori_loop(0, 8, look, 0)
        return lax.fori_loop(0, 4, spread, carry)

    lax.fori_loop(1, passes, again, 0)
    for m in range(16):
        out_ref[m] = tile_blocks(result_ref[m])


def third_kernel(
    ids_hbm, recv_ref, tnew_ref, slots_ref, hat_ref, key_ref, column_ref, total_ref,
    out_ref,
    ids_ref, corner_ref, aux_ref, slots_s, hat_s, key_s, column_s, cot_s, found_ref, result_ref, sem,
):
    (load,) = start_all((ids_hbm,), (ids_ref,), sem)
    result_ref[...] = jnp.zeros_like(result_ref)
    half = Half(recv_ref, corner_ref, aux_ref, slots_ref, hat_ref, key_ref, column_ref, cot_s)
    blocks = block_finder(ids_ref, 0)
    load.wait()
    lax.fori_loop(0, 8, half.look(tnew_ref, found_ref, blocks), 0, unroll=4)
    lax.fori_loop(0, 4, half.spread(found_ref, result_ref), 0, unroll=2)
    passes = passes_of(total_ref[...])

    @pl.when(passes > 1)
    def _():
        more = Half(recv_ref, corner_ref, aux_ref, slots_s, hat_s, key_s, column_s, cot_s)
        more.count(1)
        look, spread = more.look(tnew_ref, found_ref, blocks), more.spread(found_ref, result_ref)

        def again(number, carry):
            more.gather(number, 1)
            lax.fori_loop(0, 8, look, 0)
            return lax.fori_loop(0, 4, spread, carry)

        lax.fori_loop(1, passes, again, 0)

    for m in range(16):
        out_ref[m] = tile_blocks(result_ref[m])


def network_kernel(recv_ref, win_ref, wout_ref, out_ref):
    columns = []
    for v in range(4):
        total = recv_ref[v]
        for t in range(1, 4):
            total = total + recv_ref[4 * t + v]
        columns.append(tile_blocks(total))
    encoded = jnp.concatenate(columns, axis=1)
    hidden = jnp.maximum(
        lax.dot_general(
            win_ref[...], encoded, (((0,), (0,)), ((), ())),
            precision=lax.Precision.HIGHEST, preferred_element_type=f32,
        ),
        0.0,
    )
    out_ref[...] = jnp.dot(wout_ref[...], hidden, precision=lax.Precision.HIGHEST, preferred_element_type=f32)


VMEM = pl.BlockSpec(memory_space=pltpu.VMEM)
HBM = pl.BlockSpec(memory_space=pltpu.HBM)


def call(kernel, outs, in_specs, scratch=(), out_specs=None, **extra):
    return pl.pallas_call(
        kernel,
        out_shape=[jax.ShapeDtypeStruct(*o) if isinstance(o, tuple) else o for o in outs],
        in_specs=in_specs,
        out_specs=[VMEM] * len(outs) if out_specs is None else out_specs,
        scratch_shapes=list(scratch),
        compiler_params=pltpu.CompilerParams(vmem_limit_bytes=VMEM_LIMIT),
        **extra,
    )


def in_hbm(*arrays):
    return [pltpu.with_memory_space_constraint(array, pltpu.HBM) for array in arrays]


def exchange(value):
    tables, rays = lax.axis_size("table"), lax.axis_size("ray")
    groups = [[t * rays + r for t in range(core, tables, 2) for r in range(rays)] for core in range(2)]
    return lax.all_to_all(
        value, ("table", "ray"), split_axis=0, concat_axis=0, tiled=True, axis_index_groups=groups
    )


def swap_cores(value):
    return lax.ppermute(value, "table", [(t, t ^ 1) for t in range(lax.axis_size("table"))])


def rows_of(array):
    levels, blocks = array.shape[:2]
    return array.reshape(levels, blocks, 4, 4, LANES).transpose(0, 1, 3, 2, 4).reshape(levels * blocks, 16, LANES)


def rows_back(array, shape):
    levels, blocks = shape[:2]
    return array.reshape(levels, blocks, 4, 4, LANES).transpose(0, 1, 3, 2, 4).reshape(shape)


def on_device(
    table,
    moment1,
    moment2,
    block_ids,
    sample_slot,
    corners,
    fractions,
    feat_cot,
    weight_in,
    weight_out,
):
    (packed,) = call(
        pack_kernel,
        [((64, 8, LANES), f32)],
        [HBM] * 4,
        [
            pltpu.VMEM((2, 512), i32),
            pltpu.VMEM((2, 8, 512), i32),
            pltpu.VMEM((3, 2, 512), f32),
            pltpu.VMEM((2, 4, 512), f32),
            pltpu.SemaphoreType.DMA((4,)),
        ],
    )(*in_hbm(sample_slot, corners, fractions.transpose(1, 0, 2), feat_cot))
    samples = exchange(packed)
    others = swap_cores(samples)
    rows = (128, 16, LANES)
    (ids,) = in_hbm(block_ids.transpose(0, 1, 3, 2).reshape(64, 128))
    tile = pltpu.VMEM((8, 8, LANES), f32)
    lists = pltpu.VMEM((4, 8, LANES), i32)
    full = pltpu.VMEM(rows, f32)
    data = pltpu.VMEM((8, 4, 8, LANES), f32)
    wide = pltpu.VMEM((16, 8, LANES), f32)
    id_table = pltpu.SMEM((64, LANES), i32)
    grad, slots, hat, key, column, total, m1, m2 = call(
        first_kernel,
        [full, lists, tile, tile, tile, pltpu.VMEM((8, LANES), i32), full, full],
        [HBM, VMEM, HBM, HBM],
        [id_table, data, data, tile, pltpu.SemaphoreType.DMA((3,))],
        cost_estimate=pl.CostEstimate(flops=1 << 30, bytes_accessed=4 << 20, transcendentals=0),
    )(ids, samples, *in_hbm(rows_of(moment1), rows_of(moment2)))
    tnew, m1new, m2new, found_other = call(
        second_kernel,
        [full, full, full, ((16, 8, LANES), f32)],
        [HBM] + [VMEM] * 5,
        [id_table, full, data, data, lists, tile, tile, tile, tile, tile, wide, pltpu.SemaphoreType.DMA((1,))],
    )(ids, others, grad, rows_of(table), m1, m2)
    partner = swap_cores(found_other)
    (found_own,) = call(
        third_kernel,
        [((16, 8, LANES), f32)],
        [HBM] + [VMEM] * 7,
        [id_table, data, data, lists, tile, tile, tile, tile, tile, wide, pltpu.SemaphoreType.DMA((1,))],
        cost_estimate=pl.CostEstimate(flops=1 << 30, bytes_accessed=4 << 20, transcendentals=0),
    )(ids, samples, tnew, slots, hat, key, column, total)
    found = found_own + partner
    back = exchange(found.reshape(64, 2, LANES)).reshape(16, 8, LANES)
    (mlp_out,) = call(network_kernel, [((16, 512), f32)], [VMEM] * 3)(back, weight_in.T, weight_out)
    shape = table.shape
    return (rows_back(tnew, shape), rows_back(m1new, shape), rows_back(m2new, shape), mlp_out)


def solution(mesh):
    in_specs = (
        P(None, ("table", "ray"), None, None),
        P(None, ("table", "ray"), None, None),
        P(None, ("table", "ray"), None, None),
        P(),
        P(None, ("table", "ray")),
        P(None, None, ("table", "ray")),
        P(None, None, ("table", "ray")),
        P(None, None, ("table", "ray")),
        P(),
        P(),
    )
    out_specs = (
        P(None, ("table", "ray"), None, None),
        P(None, ("table", "ray"), None, None),
        P(None, ("table", "ray"), None, None),
        P(None, ("table", "ray")),
    )
    return jax.shard_map(
        on_device, mesh=mesh, in_specs=in_specs, out_specs=out_specs, check_vma=False
    )
```

```python
import jax
import jax.numpy as jnp
from jax import lax
from jax.experimental import pallas as pl
from jax.experimental.pallas import tpu as pltpu
from jax.sharding import PartitionSpec as P

beta_one = 0.9
beta_two = 0.99
learn_rate = 0.01
adam_eps = 1e-15

LANES = 128
RUN = 32
VMEM_LIMIT = 16 << 20
f32, bf16, i32 = jnp.float32, jnp.bfloat16, jnp.int32


def iota(shape, axis):
    return lax.broadcasted_iota(i32, shape, axis)


def lane_blocks(pieces):
    lane = iota(pieces[0].shape, 1)
    for width in (2 * RUN, RUN):
        low = (lane & width) == 0
        step = width // RUN
        results = list(pieces)
        for one in range(4):
            if not one & step:
                x, y = pieces[one], pieces[one + step]
                results[one] = jnp.where(low, x, pltpu.roll(y, width, 1))
                results[one + step] = jnp.where(low, pltpu.roll(x, LANES - width, 1), y)
        pieces = results
    return pieces


def tile_blocks(value):
    shift = (iota((8, LANES), 0) // 2 - iota((8, LANES), 1) // RUN) & 3
    result = value
    for d in range(1, 4):
        moved = pltpu.roll(pltpu.roll(value, 2 * d, 0), LANES - RUN * d, 1)
        result = jnp.where(shift == d, moved, result)
    return result


def start_all(sources, targets, sems):
    copies = [pltpu.make_async_copy(x, y, sems.at[n]) for n, (x, y) in enumerate(zip(sources, targets))]
    for copy in copies:
        copy.start()
    return copies


def wait_all(copies):
    for copy in copies:
        copy.wait()


def pack_kernel(slot_hbm, corners_hbm, fractions_hbm, cot_hbm, out_ref, slot_ref, corners_ref, fractions_ref, cot_ref, sems):
    wait_all(
        start_all(
            (slot_hbm, corners_hbm, fractions_hbm, cot_hbm), (slot_ref, corners_ref, fractions_ref, cot_ref), sems
        )
    )
    groups = [corners_ref[0].astype(f32), corners_ref[1].astype(f32)]
    for level in range(2):
        rows = [slot_ref[level : level + 1, :].astype(f32)]
        rows += [fractions_ref[d, level : level + 1, :] for d in range(3)]
        rows += [cot_ref[level]]
        groups.append(jnp.concatenate(rows, axis=0))
    for v in range(4):
        lanes = slice(v * LANES, (v + 1) * LANES)
        for p, value in enumerate(lane_blocks([g[:, lanes] for g in groups])):
            for t in range(4):
                out_ref[16 * t + 4 * v + p] = value


def gather_lanes(value, index):
    return jnp.take_along_axis(value, index, axis=1, mode="promise_in_bounds")


class Half:
    def __init__(self, recv_ref, corner_ref, aux_ref, slots_ref, hat_ref, key_ref, column_ref, cot_ref):
        self.recv_ref, self.corner_ref, self.aux_ref, self.slots_ref = recv_ref, corner_ref, aux_ref, slots_ref
        self.hat_ref, self.key_ref, self.column_ref, self.cot_ref = hat_ref, key_ref, column_ref, cot_ref
        self.entries = [(iota((16, LANES), 0) + 16 * i).astype(f32).astype(bf16) for i in range(8)]
        self.owns = [((iota((16, LANES), 0) & 7) // 4 + 2 * i).astype(f32).astype(bf16) for i in range(8)]
        self.one = jnp.ones((16, LANES), bf16)
        self.none = jnp.zeros((16, LANES), bf16)
        self.sub = iota((8, LANES), 0)

    def count(self, unroll):
        def unpack(t, carry):
            for v in range(4):
                rows = lane_blocks([self.recv_ref[t * 16 + 4 * v + p] for p in range(4)])
                self.corner_ref[t, v] = rows[0]
                self.corner_ref[4 + t, v] = rows[1]
                self.aux_ref[t, v] = rows[2]
                self.aux_ref[4 + t, v] = rows[3]
            return carry

        lax.fori_loop(0, 4, unpack, 0, unroll=unroll)
        first_slot = (lax.axis_index("table") * 64).astype(f32)
        self.hits = []
        for v in range(4):
            slot = jnp.concatenate([self.aux_ref[lt, v, 0:1, :] for lt in range(8)], axis=0)
            self.hits.append(jnp.where((slot >= first_slot) & (slot < first_slot + 64.0), 1.0, 0.0))
        row, column = iota((LANES, 2 * LANES), 0), iota((LANES, 2 * LANES), 1)
        upper = jnp.where(row <= column, 1.0, 0.0).astype(bf16)
        hits = jnp.concatenate(self.hits, axis=0).astype(bf16)
        counts = jnp.dot(hits, upper, preferred_element_type=f32).astype(i32)
        self.through = [counts[8 * v : 8 * v + 8, :LANES] for v in range(4)]
        self.before = [jnp.zeros((8, LANES), i32)]
        for v in range(4):
            self.before.append(self.before[v] + counts[8 * v : 8 * v + 8, LANES:])
        self.total = self.before[4]

    def gather(self, step, unroll):
        for v in range(4):
            rank = self.before[v] + self.through[v] - 1 - step * LANES
            inside = (self.hits[v] > 0.5) & (rank >= 0) & (rank < LANES)
            self.slots_ref[v] = jnp.where(inside, rank, -1)
        lax.fori_loop(0, 8, self.compact, 0, unroll=unroll)

    def compact(self, lt, carry):
        high, low, chosen = [], [], []
        for v in range(4):
            piece = jnp.concatenate([self.corner_ref[lt, v], self.aux_ref[lt, v]], axis=0)
            high.append(piece.astype(bf16))
            low.append((piece - high[v].astype(f32)).astype(bf16))
            slot = jnp.broadcast_to(self.slots_ref[v, pl.ds(lt, 1), :].astype(f32), (16, LANES)).astype(bf16)
            chosen.append(
                jnp.concatenate([jnp.where(slot == self.entries[i], self.one, self.none) for i in range(8)], axis=0)
            )
        rows = jnp.concatenate([jnp.concatenate(high, axis=1), jnp.concatenate(low, axis=1)], axis=0)
        both = lax.dot_general(
            rows, jnp.concatenate(chosen, axis=1), (((1,), (1,)), ((), ())), preferred_element_type=f32
        )
        corner, aux = both[:8] + both[16:24], both[8:16] + both[24:]
        hat = None
        for d in range(3):
            f = jnp.broadcast_to(aux[1 + d : 2 + d], (8, LANES))
            factor = jnp.where((self.sub >> d) & 1 == 1, f, 1.0 - f)
            hat = factor if hat is None else hat * factor
        entry = corner.astype(i32)
        self.hat_ref[lt] = hat
        self.key_ref[lt] = ((aux[0:1].astype(i32) & 3) * 4 + (entry >> 7)).astype(f32)
        self.column_ref[lt] = (entry & 127).astype(f32)
        self.cot_ref[lt] = jnp.where(self.sub < 4, pltpu.roll(aux, 4, 0), aux)
        return carry

    def hot_rows(self, lt):
        pieces = []
        for c in range(8):
            wanted = jnp.broadcast_to(self.column_ref[lt, c : c + 1, :], (16, LANES)).astype(bf16)
            pieces.append(
                jnp.concatenate([jnp.where(wanted == self.entries[i], self.one, self.none) for i in range(8)], axis=0)
            )
        return jnp.concatenate(pieces, axis=1)

    def accumulate(self, grad_ref, blocks):
        def one_group(lt, carry):
            cot = self.cot_ref[lt]
            columns = []
            for c in range(8):
                value = cot * self.hat_ref[lt, c : c + 1, :]
                high = value.astype(bf16).astype(f32)
                both = jnp.concatenate([high, value - high], axis=0).astype(bf16)
                key = jnp.broadcast_to(self.key_ref[lt, c : c + 1, :], (16, LANES)).astype(bf16)
                columns.append(
                    jnp.concatenate([jnp.where(key == self.owns[i], both, self.none) for i in range(8)], axis=0)
                )
            sums = lax.dot_general(
                jnp.concatenate(columns, axis=1), self.hot_rows(lt), (((1,), (1,)), ((), ())),
                preferred_element_type=f32,
            )
            for slot in range(4):
                block = blocks(lt, slot)
                for half in range(2):
                    at = 32 * slot + 16 * half
                    grad_ref[block, 8 * half : 8 * half + 8, :] += sums[at : at + 8] + sums[at + 8 : at + 16]
            return carry

        return one_group

    def look(self, table_ref, found_ref, blocks):
        parity = self.sub // 4

        def one_group(lt, carry):
            rows = jnp.concatenate([table_ref[blocks(lt, slot)] for slot in range(4)], axis=0)
            high = rows.astype(bf16)
            low = (rows - high.astype(f32)).astype(bf16)
            hot = self.hot_rows(lt)
            seen = jnp.dot(
                jnp.concatenate([high, low], axis=1), jnp.concatenate([hot, hot], axis=0), preferred_element_type=f32
            )
            total = jnp.zeros((8, LANES), f32)
            for c in range(8):
                own = jnp.broadcast_to(self.key_ref[lt, c : c + 1, :], (8, LANES))
                picked = jnp.zeros((8, LANES), f32)
                for i in range(8):
                    mask = own == (parity + 2 * i).astype(f32)
                    picked = jnp.where(mask, seen[8 * i : 8 * i + 8, c * LANES : (c + 1) * LANES], picked)
                total = total + picked * self.hat_ref[lt, c : c + 1, :]
            found_ref[lt] = total + pltpu.roll(total, 4, 0)
            return carry

        return one_group

    def spread(self, found_ref, result_ref):
        def one_group(t, carry):
            value = jnp.where(self.sub < 4, found_ref[t], found_ref[4 + t])
            for v in range(4):
                zero = jnp.broadcast_to(self.slots_ref[v, pl.ds(t, 1), :], (8, LANES))
                one = jnp.broadcast_to(self.slots_ref[v, pl.ds(4 + t, 1), :], (8, LANES))
                place = jnp.where(self.sub < 4, zero, one)
                taken = gather_lanes(value, jnp.maximum(place, 0))
                result_ref[t * 4 + v] += jnp.where(place >= 0, taken, 0.0)
            return carry

        return one_group


def passes_of(total):
    return (jnp.max(total) + (LANES - 1)) // LANES


def block_finder(ids_ref, other):
    mine = lax.axis_index("table")
    owner = mine * lax.axis_size("ray") + lax.axis_index("ray")
    parity = (mine + other) % 2

    def blocks(lt, slot):
        level, group = lt // 4, 2 * (lt % 4) + parity
        return level * 64 + ids_ref[(group * 2 + level) * 4 + slot, owner]

    return blocks


def gradients(half, grad_ref, blocks, ready):
    half.count(4)
    half.gather(0, 4)
    ready()
    step = half.accumulate(grad_ref, blocks)
    lax.fori_loop(0, 8, step, 0, unroll=4)
    passes = passes_of(half.total)

    def again(number, carry):
        half.gather(number, 1)
        return lax.fori_loop(0, 8, step, carry)

    lax.fori_loop(1, passes, again, 0)

    @pl.when(passes > 1)
    def _():
        half.gather(0, 1)

    return passes


def first_kernel(
    ids_hbm, recv_ref, m1_hbm, m2_hbm,
    grad_ref, slots_ref, hat_ref, key_ref, column_ref, total_ref, m1_ref, m2_ref,
    ids_ref, corner_ref, aux_ref, cot_ref, sems,
):
    loads = start_all((ids_hbm, m1_hbm, m2_hbm), (ids_ref, m1_ref, m2_ref), sems)
    grad_ref[...] = jnp.zeros_like(grad_ref)
    half = Half(recv_ref, corner_ref, aux_ref, slots_ref, hat_ref, key_ref, column_ref, cot_ref)
    gradients(half, grad_ref, block_finder(ids_ref, 0), loads[0].wait)
    total_ref[...] = half.total
    wait_all(loads[1:])


def second_kernel(
    ids_hbm, recv_ref, own_recv_ref, before_ref, table_ref, m1_ref, m2_ref,
    own_slots_ref, own_hat_ref, own_key_ref, own_column_ref, own_total_ref,
    tnew_ref, m1new_ref, m2new_ref, out_ref,
    ids_ref, grad_ref, corner_ref, aux_ref, slots_ref, hat_ref, key_ref, column_ref, cot_ref,
    found_ref, result_ref, sem,
):
    (load,) = start_all((ids_hbm,), (ids_ref,), sem)
    grad_ref[...] = before_ref[...]
    result_ref[...] = jnp.zeros_like(result_ref)
    spare = (corner_ref, aux_ref, slots_ref, hat_ref, key_ref, column_ref, cot_ref)
    half = Half(recv_ref, *spare)
    blocks, own_blocks = block_finder(ids_ref, 1), block_finder(ids_ref, 0)
    passes = gradients(half, grad_ref, blocks, load.wait)

    def update(step, carry):
        at = pl.ds(step * 4, 4)
        grad = grad_ref[at]
        first = beta_one * m1_ref[at] + (1.0 - beta_one) * grad
        second = beta_two * m2_ref[at] + (1.0 - beta_two) * grad * grad
        m1new_ref[at] = first
        m2new_ref[at] = second
        tnew_ref[at] = table_ref[at] - learn_rate * first / (jnp.sqrt(second) + adam_eps)
        return carry

    lax.fori_loop(0, 32, update, 0)
    own = Half(own_recv_ref, corner_ref, aux_ref, own_slots_ref, own_hat_ref, own_key_ref, own_column_ref, cot_ref)
    results = [result_ref.at[pl.ds(0, 16)], result_ref.at[pl.ds(16, 16)]]
    for part, finder, result in ((own, own_blocks, results[0]), (half, blocks, results[1])):
        lax.fori_loop(0, 8, part.look(tnew_ref, found_ref, finder), 0, unroll=4)
        lax.fori_loop(0, 4, part.spread(found_ref, result), 0, unroll=2)

    def more_passes(part, finder, result, count):
        look, spread = part.look(tnew_ref, found_ref, finder), part.spread(found_ref, result)

        def again(number, carry):
            part.gather(number, 1)
            lax.fori_loop(0, 8, look, 0)
            return lax.fori_loop(0, 4, spread, carry)

        lax.fori_loop(1, count, again, 0)

    more_passes(half, blocks, results[1], passes)
    own_passes = passes_of(own_total_ref[...])

    @pl.when(own_passes > 1)
    def _():
        again = Half(own_recv_ref, *spare)
        again.count(1)
        more_passes(again, own_blocks, results[0], own_passes)

    core = lax.axis_index("table") % 2
    for h in range(4):
        for v in range(4):
            out_ref[(2 * h + core) * 4 + v] = tile_blocks(result_ref[4 * h + v])
            out_ref[(2 * h + 1 - core) * 4 + v] = tile_blocks(result_ref[16 + 4 * h + v])


def network_kernel(recv_ref, win_ref, wout_ref, out_ref):
    columns = []
    for v in range(4):
        total = recv_ref[v]
        for t in range(1, 8):
            total = total + recv_ref[4 * t + v]
        columns.append(tile_blocks(total))
    encoded = jnp.concatenate(columns, axis=1)
    hidden = jnp.maximum(
        lax.dot_general(
            win_ref[...], encoded, (((0,), (0,)), ((), ())),
            precision=lax.Precision.HIGHEST, preferred_element_type=f32,
        ),
        0.0,
    )
    out_ref[...] = jnp.dot(wout_ref[...], hidden, precision=lax.Precision.HIGHEST, preferred_element_type=f32)


VMEM = pl.BlockSpec(memory_space=pltpu.VMEM)
HBM = pl.BlockSpec(memory_space=pltpu.HBM)


def call(kernel, outs, in_specs, scratch=(), out_specs=None, **extra):
    return pl.pallas_call(
        kernel,
        out_shape=[jax.ShapeDtypeStruct(*o) if isinstance(o, tuple) else o for o in outs],
        in_specs=in_specs,
        out_specs=[VMEM] * len(outs) if out_specs is None else out_specs,
        scratch_shapes=list(scratch),
        compiler_params=pltpu.CompilerParams(vmem_limit_bytes=VMEM_LIMIT),
        **extra,
    )


def in_hbm(*arrays):
    return [pltpu.with_memory_space_constraint(array, pltpu.HBM) for array in arrays]


def exchange(value, groups=None):
    return lax.all_to_all(
        value, ("table", "ray"), split_axis=0, concat_axis=0, tiled=True, axis_index_groups=groups
    )


def same_core():
    tables, rays = lax.axis_size("table"), lax.axis_size("ray")
    return [[t * rays + r for t in range(core, tables, 2) for r in range(rays)] for core in range(2)]


def swap_cores(value):
    return lax.ppermute(value, "table", [(t, t ^ 1) for t in range(lax.axis_size("table"))])


def rows_of(array):
    levels, blocks = array.shape[:2]
    return array.reshape(levels, blocks, 4, 4, LANES).transpose(0, 1, 3, 2, 4).reshape(levels * blocks, 16, LANES)


def rows_back(array, shape):
    levels, blocks = shape[:2]
    return array.reshape(levels, blocks, 4, 4, LANES).transpose(0, 1, 3, 2, 4).reshape(shape)


def on_device(
    table,
    moment1,
    moment2,
    block_ids,
    sample_slot,
    corners,
    fractions,
    feat_cot,
    weight_in,
    weight_out,
):
    (packed,) = call(
        pack_kernel,
        [((64, 8, LANES), f32)],
        [HBM] * 4,
        [
            pltpu.VMEM((2, 512), i32),
            pltpu.VMEM((2, 8, 512), i32),
            pltpu.VMEM((3, 2, 512), f32),
            pltpu.VMEM((2, 4, 512), f32),
            pltpu.SemaphoreType.DMA((4,)),
        ],
    )(*in_hbm(sample_slot, corners, fractions.transpose(1, 0, 2), feat_cot))
    samples = exchange(packed, same_core())
    others = swap_cores(samples)
    rows = (128, 16, LANES)
    (ids,) = in_hbm(block_ids.transpose(0, 1, 3, 2).reshape(64, 128))
    tile = pltpu.VMEM((8, 8, LANES), f32)
    lists = pltpu.VMEM((4, 8, LANES), i32)
    full = pltpu.VMEM(rows, f32)
    data = pltpu.VMEM((8, 4, 8, LANES), f32)
    id_table = pltpu.SMEM((64, LANES), i32)
    grad, slots, hat, key, column, total, m1, m2 = call(
        first_kernel,
        [full, lists, tile, tile, tile, pltpu.VMEM((8, LANES), i32), full, full],
        [HBM, VMEM, HBM, HBM],
        [id_table, data, data, tile, pltpu.SemaphoreType.DMA((3,))],
        cost_estimate=pl.CostEstimate(flops=1 << 30, bytes_accessed=4 << 20, transcendentals=0),
    )(ids, samples, *in_hbm(rows_of(moment1), rows_of(moment2)))
    tnew, m1new, m2new, found = call(
        second_kernel,
        [full, full, full, ((32, 8, LANES), f32)],
        [HBM] + [VMEM] * 11,
        [
            id_table, full, data, data, lists, tile, tile, tile, tile, tile,
            pltpu.VMEM((32, 8, LANES), f32),
            pltpu.SemaphoreType.DMA((1,)),
        ],
    )(ids, others, samples, grad, rows_of(table), m1, m2, slots, hat, key, column, total)
    back = exchange(found.reshape(128, 2, LANES)).reshape(32, 8, LANES)
    (mlp_out,) = call(network_kernel, [((16, 512), f32)], [VMEM] * 3)(back, weight_in.T, weight_out)
    shape = table.shape
    return (rows_back(tnew, shape), rows_back(m1new, shape), rows_back(m2new, shape), mlp_out)


def solution(mesh):
    in_specs = (
        P(None, ("table", "ray"), None, None),
        P(None, ("table", "ray"), None, None),
        P(None, ("table", "ray"), None, None),
        P(),
        P(None, ("table", "ray")),
        P(None, None, ("table", "ray")),
        P(None, None, ("table", "ray")),
        P(None, None, ("table", "ray")),
        P(),
        P(),
    )
    out_specs = (
        P(None, ("table", "ray"), None, None),
        P(None, ("table", "ray"), None, None),
        P(None, ("table", "ray"), None, None),
        P(None, ("table", "ray")),
    )
    return jax.shard_map(
        on_device, mesh=mesh, in_specs=in_specs, out_specs=out_specs, check_vma=False
    )
```

```python
import jax
import jax.numpy as jnp
from jax import lax
from jax.experimental import pallas as pl
from jax.experimental.pallas import tpu as pltpu
from jax.sharding import PartitionSpec as P

beta_one = 0.9
beta_two = 0.99
learn_rate = 0.01
adam_eps = 1e-15

LANES = 128
RUN = 32
VMEM_LIMIT = 16 << 20
DEEP = 4
f32, bf16, i32 = jnp.float32, jnp.bfloat16, jnp.int32


def iota(shape, axis):
    return lax.broadcasted_iota(i32, shape, axis)


def lane_blocks(pieces):
    lane = iota(pieces[0].shape, 1)
    for width in (2 * RUN, RUN):
        low = (lane & width) == 0
        step = width // RUN
        results = list(pieces)
        for one in range(4):
            if not one & step:
                x, y = pieces[one], pieces[one + step]
                results[one] = jnp.where(low, x, pltpu.roll(y, width, 1))
                results[one + step] = jnp.where(low, pltpu.roll(x, LANES - width, 1), y)
        pieces = results
    return pieces


def tile_blocks(value):
    shift = (iota((8, LANES), 0) // 2 - iota((8, LANES), 1) // RUN) & 3
    result = value
    for d in range(1, 4):
        moved = pltpu.roll(pltpu.roll(value, 2 * d, 0), LANES - RUN * d, 1)
        result = jnp.where(shift == d, moved, result)
    return result


def each(count, step):
    for number in range(count):
        step(number, 0)


def start_all(sources, targets, sems):
    copies = [pltpu.make_async_copy(x, y, sems.at[n]) for n, (x, y) in enumerate(zip(sources, targets))]
    for copy in copies:
        copy.start()
    return copies


def wait_all(copies):
    for copy in copies:
        copy.wait()


def pack_kernel(slot_hbm, corners_hbm, fractions_hbm, cot_hbm, out_ref, slot_ref, corners_ref, fractions_ref, cot_ref, sems):
    wait_all(
        start_all(
            (slot_hbm, corners_hbm, fractions_hbm, cot_hbm), (slot_ref, corners_ref, fractions_ref, cot_ref), sems
        )
    )
    groups = [corners_ref[0].astype(f32), corners_ref[1].astype(f32)]
    for level in range(2):
        rows = [slot_ref[level : level + 1, :].astype(f32)]
        rows += [fractions_ref[d, level : level + 1, :] for d in range(3)]
        rows += [cot_ref[level]]
        groups.append(jnp.concatenate(rows, axis=0))
    for v in range(4):
        lanes = slice(v * LANES, (v + 1) * LANES)
        for p, value in enumerate(lane_blocks([g[:, lanes] for g in groups])):
            for t in range(4):
                out_ref[16 * t + 4 * v + p] = value


def gather_lanes(value, index):
    return jnp.take_along_axis(value, index, axis=1, mode="promise_in_bounds")


class Half:
    def __init__(self, recv_ref, corner_ref, aux_ref, slots_ref, hat_ref, key_ref, column_ref, cot_ref):
        self.recv_ref, self.corner_ref, self.aux_ref, self.slots_ref = recv_ref, corner_ref, aux_ref, slots_ref
        self.hat_ref, self.key_ref, self.column_ref, self.cot_ref = hat_ref, key_ref, column_ref, cot_ref
        self.entries = [(iota((16, LANES), 0) + 16 * i).astype(f32).astype(bf16) for i in range(8)]
        self.owns = [((iota((16, LANES), 0) & 7) // 4 + 2 * i).astype(f32).astype(bf16) for i in range(8)]
        self.one = jnp.ones((16, LANES), bf16)
        self.none = jnp.zeros((16, LANES), bf16)
        self.sub = iota((8, LANES), 0)

    def count(self, unroll):
        def unpack(t, carry):
            for v in range(4):
                rows = lane_blocks([self.recv_ref[t * 16 + 4 * v + p] for p in range(4)])
                self.corner_ref[t, v] = rows[0]
                self.corner_ref[4 + t, v] = rows[1]
                self.aux_ref[t, v] = rows[2]
                self.aux_ref[4 + t, v] = rows[3]
            return carry

        if unroll:
            each(4, unpack)
        else:
            lax.fori_loop(0, 4, unpack, 0)
        first_slot = (lax.axis_index("table") * 64).astype(f32)
        self.hits = []
        for v in range(4):
            slot = jnp.concatenate([self.aux_ref[lt, v, 0:1, :] for lt in range(8)], axis=0)
            self.hits.append(jnp.where((slot >= first_slot) & (slot < first_slot + 64.0), 1.0, 0.0))
        row, column = iota((LANES, 2 * LANES), 0), iota((LANES, 2 * LANES), 1)
        upper = jnp.where(row <= column, 1.0, 0.0).astype(bf16)
        hits = jnp.concatenate(self.hits, axis=0).astype(bf16)
        counts = jnp.dot(hits, upper, preferred_element_type=f32).astype(i32)
        self.through = [counts[8 * v : 8 * v + 8, :LANES] for v in range(4)]
        self.before = [jnp.zeros((8, LANES), i32)]
        for v in range(4):
            self.before.append(self.before[v] + counts[8 * v : 8 * v + 8, LANES:])
        self.total = self.before[4]

    def gather(self, step, unroll):
        for v in range(4):
            rank = self.before[v] + self.through[v] - 1 - step * LANES
            inside = (self.hits[v] > 0.5) & (rank >= 0) & (rank < LANES)
            self.slots_ref[v] = jnp.where(inside, rank, -1)
        if unroll:
            each(8, self.compact)
        else:
            lax.fori_loop(0, 8, self.compact, 0)

    def compact(self, lt, carry):
        high, low, chosen = [], [], []
        for v in range(4):
            piece = jnp.concatenate([self.corner_ref[lt, v], self.aux_ref[lt, v]], axis=0)
            high.append(piece.astype(bf16))
            low.append((piece - high[v].astype(f32)).astype(bf16))
            slot = jnp.broadcast_to(self.slots_ref[v, pl.ds(lt, 1), :].astype(f32), (16, LANES)).astype(bf16)
            chosen.append(
                jnp.concatenate([jnp.where(slot == self.entries[i], self.one, self.none) for i in range(8)], axis=0)
            )
        rows = jnp.concatenate([jnp.concatenate(high, axis=1), jnp.concatenate(low, axis=1)], axis=0)
        both = lax.dot_general(
            rows, jnp.concatenate(chosen, axis=1), (((1,), (1,)), ((), ())), preferred_element_type=f32
        )
        corner, aux = both[:8] + both[16:24], both[8:16] + both[24:]
        hat = None
        for d in range(3):
            f = jnp.broadcast_to(aux[1 + d : 2 + d], (8, LANES))
            factor = jnp.where((self.sub >> d) & 1 == 1, f, 1.0 - f)
            hat = factor if hat is None else hat * factor
        entry = corner.astype(i32)
        self.hat_ref[lt] = hat
        self.key_ref[lt] = ((aux[0:1].astype(i32) & 3) * 4 + (entry >> 7)).astype(f32)
        self.column_ref[lt] = (entry & 127).astype(f32)
        self.cot_ref[lt] = jnp.where(self.sub < 4, pltpu.roll(aux, 4, 0), aux)
        return carry

    def hot_rows(self, lt, corners=range(8)):
        pieces = []
        for c in corners:
            wanted = jnp.broadcast_to(self.column_ref[lt, c : c + 1, :], (16, LANES)).astype(bf16)
            pieces.append(
                jnp.concatenate([jnp.where(wanted == self.entries[i], self.one, self.none) for i in range(8)], axis=0)
            )
        return jnp.concatenate(pieces, axis=1)

    def accumulate(self, grad_ref, blocks):
        def one_group(lt, carry):
            cot = self.cot_ref[lt]
            columns = []
            for c in range(8):
                value = cot * self.hat_ref[lt, c : c + 1, :]
                high = value.astype(bf16).astype(f32)
                both = jnp.concatenate([high, value - high], axis=0).astype(bf16)
                key = jnp.broadcast_to(self.key_ref[lt, c : c + 1, :], (16, LANES)).astype(bf16)
                columns.append(
                    jnp.concatenate([jnp.where(key == self.owns[i], both, self.none) for i in range(8)], axis=0)
                )
            sums = lax.dot_general(
                jnp.concatenate(columns, axis=1), self.hot_rows(lt), (((1,), (1,)), ((), ())),
                preferred_element_type=f32,
            )
            for slot in range(4):
                block = blocks(lt, slot)
                for half in range(2):
                    at = 32 * slot + 16 * half
                    grad_ref[block, 8 * half : 8 * half + 8, :] += sums[at : at + 8] + sums[at + 8 : at + 16]
            return carry

        return one_group

    def look(self, table_ref, found_ref, blocks):
        parity = self.sub // 4

        def one_group(lt, carry):
            rows = jnp.concatenate([table_ref[blocks(lt, slot)] for slot in range(4)], axis=0)
            high = rows.astype(bf16)
            low = (rows - high.astype(f32)).astype(bf16)
            deep, tall = self.hot_rows(lt, range(DEEP)), self.hot_rows(lt, range(DEEP, 8))
            seen = jnp.dot(
                jnp.concatenate([high, low], axis=1), jnp.concatenate([deep, deep], axis=0), preferred_element_type=f32
            )
            both = jnp.dot(jnp.concatenate([high, low], axis=0), tall, preferred_element_type=f32)
            seen = jnp.concatenate([seen, both[:64] + both[64:]], axis=1)
            total = jnp.zeros((8, LANES), f32)
            for c in range(8):
                own = jnp.broadcast_to(self.key_ref[lt, c : c + 1, :], (8, LANES))
                picked = jnp.zeros((8, LANES), f32)
                for i in range(8):
                    mask = own == (parity + 2 * i).astype(f32)
                    picked = jnp.where(mask, seen[8 * i : 8 * i + 8, c * LANES : (c + 1) * LANES], picked)
                total = total + picked * self.hat_ref[lt, c : c + 1, :]
            found_ref[lt] = total + pltpu.roll(total, 4, 0)
            return carry

        return one_group

    def spread(self, found_ref, result_ref):
        def one_group(t, carry):
            value = jnp.where(self.sub < 4, found_ref[t], found_ref[4 + t])
            for v in range(4):
                zero = jnp.broadcast_to(self.slots_ref[v, pl.ds(t, 1), :], (8, LANES))
                one = jnp.broadcast_to(self.slots_ref[v, pl.ds(4 + t, 1), :], (8, LANES))
                place = jnp.where(self.sub < 4, zero, one)
                taken = gather_lanes(value, jnp.maximum(place, 0))
                result_ref[t * 4 + v] += jnp.where(place >= 0, taken, 0.0)
            return carry

        return one_group


def passes_of(total):
    return (jnp.max(total) + (LANES - 1)) // LANES


def block_finder(ids_ref, other):
    mine = lax.axis_index("table")
    owner = mine * lax.axis_size("ray") + lax.axis_index("ray")
    parity = (mine + other) % 2

    def blocks(lt, slot):
        level, group = lt // 4, 2 * (lt % 4) + parity
        return level * 64 + ids_ref[(group * 2 + level) * 4 + slot, owner]

    return blocks


def gradients(half, grad_ref, blocks, ready):
    half.count(True)
    half.gather(0, True)
    ready()
    step = half.accumulate(grad_ref, blocks)
    each(8, step)
    passes = passes_of(half.total)

    def again(number, carry):
        half.gather(number, False)
        return lax.fori_loop(0, 8, step, carry)

    lax.fori_loop(1, passes, again, 0)

    @pl.when(passes > 1)
    def _():
        half.gather(0, False)

    return passes


def first_kernel(
    ids_hbm, recv_ref, m1_hbm, m2_hbm,
    grad_ref, slots_ref, hat_ref, key_ref, column_ref, total_ref, m1_ref, m2_ref,
    ids_ref, corner_ref, aux_ref, cot_ref, sems,
):
    loads = start_all((ids_hbm, m1_hbm, m2_hbm), (ids_ref, m1_ref, m2_ref), sems)
    grad_ref[...] = jnp.zeros_like(grad_ref)
    half = Half(recv_ref, corner_ref, aux_ref, slots_ref, hat_ref, key_ref, column_ref, cot_ref)
    gradients(half, grad_ref, block_finder(ids_ref, 0), loads[0].wait)
    total_ref[...] = half.total
    wait_all(loads[1:])


def second_kernel(
    ids_hbm, recv_ref, own_recv_ref, before_ref, table_ref, m1_ref, m2_ref,
    own_slots_ref, own_hat_ref, own_key_ref, own_column_ref, own_total_ref,
    tnew_ref, m1new_ref, m2new_ref, out_ref,
    ids_ref, grad_ref, corner_ref, aux_ref, slots_ref, hat_ref, key_ref, column_ref, cot_ref,
    found_ref, result_ref, sem,
):
    (load,) = start_all((ids_hbm,), (ids_ref,), sem)
    grad_ref[...] = before_ref[...]
    result_ref[...] = jnp.zeros_like(result_ref)
    spare = (corner_ref, aux_ref, slots_ref, hat_ref, key_ref, column_ref, cot_ref)
    half = Half(recv_ref, *spare)
    blocks, own_blocks = block_finder(ids_ref, 1), block_finder(ids_ref, 0)
    passes = gradients(half, grad_ref, blocks, load.wait)

    def update(step, carry):
        at = pl.ds(step * 4, 4)
        grad = grad_ref[at]
        first = beta_one * m1_ref[at] + (1.0 - beta_one) * grad
        second = beta_two * m2_ref[at] + (1.0 - beta_two) * grad * grad
        m1new_ref[at] = first
        m2new_ref[at] = second
        tnew_ref[at] = table_ref[at] - learn_rate * first / (jnp.sqrt(second) + adam_eps)
        return carry

    lax.fori_loop(0, 32, update, 0)
    own = Half(own_recv_ref, corner_ref, aux_ref, own_slots_ref, own_hat_ref, own_key_ref, own_column_ref, cot_ref)
    results = [result_ref.at[pl.ds(0, 16)], result_ref.at[pl.ds(16, 16)]]
    for part, finder, result in ((own, own_blocks, results[0]), (half, blocks, results[1])):
        each(8, part.look(tnew_ref, found_ref, finder))
        each(4, part.spread(found_ref, result))

    def more_passes(part, finder, result, count):
        look, spread = part.look(tnew_ref, found_ref, finder), part.spread(found_ref, result)

        def again(number, carry):
            part.gather(number, False)
            lax.fori_loop(0, 8, look, 0)
            return lax.fori_loop(0, 4, spread, carry)

        lax.fori_loop(1, count, again, 0)

    more_passes(half, blocks, results[1], passes)
    own_passes = passes_of(own_total_ref[...])

    @pl.when(own_passes > 1)
    def _():
        again = Half(own_recv_ref, *spare)
        again.count(False)
        more_passes(again, own_blocks, results[0], own_passes)

    core = lax.axis_index("table") % 2
    for h in range(4):
        for v in range(4):
            out_ref[(2 * h + core) * 4 + v] = tile_blocks(result_ref[4 * h + v])
            out_ref[(2 * h + 1 - core) * 4 + v] = tile_blocks(result_ref[16 + 4 * h + v])


def network_kernel(recv_ref, win_ref, wout_ref, out_ref):
    columns = []
    for v in range(4):
        total = recv_ref[v]
        for t in range(1, 8):
            total = total + recv_ref[4 * t + v]
        columns.append(tile_blocks(total))
    encoded = jnp.concatenate(columns, axis=1)
    hidden = jnp.maximum(
        lax.dot_general(
            win_ref[...], encoded, (((0,), (0,)), ((), ())),
            precision=lax.Precision.HIGHEST, preferred_element_type=f32,
        ),
        0.0,
    )
    out_ref[...] = jnp.dot(wout_ref[...], hidden, precision=lax.Precision.HIGHEST, preferred_element_type=f32)


VMEM = pl.BlockSpec(memory_space=pltpu.VMEM)
HBM = pl.BlockSpec(memory_space=pltpu.HBM)


def call(kernel, outs, in_specs, scratch=(), out_specs=None, **extra):
    return pl.pallas_call(
        kernel,
        out_shape=[jax.ShapeDtypeStruct(*o) if isinstance(o, tuple) else o for o in outs],
        in_specs=in_specs,
        out_specs=[VMEM] * len(outs) if out_specs is None else out_specs,
        scratch_shapes=list(scratch),
        compiler_params=pltpu.CompilerParams(vmem_limit_bytes=VMEM_LIMIT),
        **extra,
    )


def in_hbm(*arrays):
    return [pltpu.with_memory_space_constraint(array, pltpu.HBM) for array in arrays]


def exchange(value, groups=None):
    return lax.all_to_all(
        value, ("table", "ray"), split_axis=0, concat_axis=0, tiled=True, axis_index_groups=groups
    )


def same_core():
    tables, rays = lax.axis_size("table"), lax.axis_size("ray")
    return [[t * rays + r for t in range(core, tables, 2) for r in range(rays)] for core in range(2)]


def swap_cores(value):
    return lax.ppermute(value, "table", [(t, t ^ 1) for t in range(lax.axis_size("table"))])


def rows_of(array):
    levels, blocks = array.shape[:2]
    return array.reshape(levels, blocks, 4, 4, LANES).transpose(0, 1, 3, 2, 4).reshape(levels * blocks, 16, LANES)


def rows_back(array, shape):
    levels, blocks = shape[:2]
    return array.reshape(levels, blocks, 4, 4, LANES).transpose(0, 1, 3, 2, 4).reshape(shape)


def on_device(
    table,
    moment1,
    moment2,
    block_ids,
    sample_slot,
    corners,
    fractions,
    feat_cot,
    weight_in,
    weight_out,
):
    (packed,) = call(
        pack_kernel,
        [((64, 8, LANES), f32)],
        [HBM] * 4,
        [
            pltpu.VMEM((2, 512), i32),
            pltpu.VMEM((2, 8, 512), i32),
            pltpu.VMEM((3, 2, 512), f32),
            pltpu.VMEM((2, 4, 512), f32),
            pltpu.SemaphoreType.DMA((4,)),
        ],
    )(*in_hbm(sample_slot, corners, fractions.transpose(1, 0, 2), feat_cot))
    samples = exchange(packed, same_core())
    others = swap_cores(samples)
    rows = (128, 16, LANES)
    (ids,) = in_hbm(block_ids.transpose(0, 1, 3, 2).reshape(64, 128))
    tile = pltpu.VMEM((8, 8, LANES), f32)
    lists = pltpu.VMEM((4, 8, LANES), i32)
    full = pltpu.VMEM(rows, f32)
    data = pltpu.VMEM((8, 4, 8, LANES), f32)
    id_table = pltpu.SMEM((64, LANES), i32)
    grad, slots, hat, key, column, total, m1, m2 = call(
        first_kernel,
        [full, lists, tile, tile, tile, pltpu.VMEM((8, LANES), i32), full, full],
        [HBM, VMEM, HBM, HBM],
        [id_table, data, data, tile, pltpu.SemaphoreType.DMA((3,))],
        cost_estimate=pl.CostEstimate(flops=1 << 30, bytes_accessed=4 << 20, transcendentals=0),
    )(ids, samples, *in_hbm(rows_of(moment1), rows_of(moment2)))
    tnew, m1new, m2new, found = call(
        second_kernel,
        [full, full, full, ((32, 8, LANES), f32)],
        [HBM] + [VMEM] * 11,
        [
            id_table, full, data, data, lists, tile, tile, tile, tile, tile,
            pltpu.VMEM((32, 8, LANES), f32),
            pltpu.SemaphoreType.DMA((1,)),
        ],
    )(ids, others, samples, grad, rows_of(table), m1, m2, slots, hat, key, column, total)
    back = exchange(found.reshape(128, 2, LANES)).reshape(32, 8, LANES)
    (mlp_out,) = call(network_kernel, [((16, 512), f32)], [VMEM] * 3)(back, weight_in.T, weight_out)
    shape = table.shape
    return (rows_back(tnew, shape), rows_back(m1new, shape), rows_back(m2new, shape), mlp_out)


def solution(mesh):
    in_specs = (
        P(None, ("table", "ray"), None, None),
        P(None, ("table", "ray"), None, None),
        P(None, ("table", "ray"), None, None),
        P(),
        P(None, ("table", "ray")),
        P(None, None, ("table", "ray")),
        P(None, None, ("table", "ray")),
        P(None, None, ("table", "ray")),
        P(),
        P(),
    )
    out_specs = (
        P(None, ("table", "ray"), None, None),
        P(None, ("table", "ray"), None, None),
        P(None, ("table", "ray"), None, None),
        P(None, ("table", "ray")),
    )
    return jax.shard_map(
        on_device, mesh=mesh, in_specs=in_specs, out_specs=out_specs, check_vma=False
    )
```

```python
import jax
import jax.numpy as jnp
from jax import lax
from jax.experimental import pallas as pl
from jax.experimental.pallas import tpu as pltpu
from jax.sharding import PartitionSpec as P

beta_one = 0.9
beta_two = 0.99
learn_rate = 0.01
adam_eps = 1e-15

LANES = 128
RUN = 32
VMEM_LIMIT = 16 << 20
DEEP = 4
f32, bf16, i32 = jnp.float32, jnp.bfloat16, jnp.int32


def iota(shape, axis):
    return lax.broadcasted_iota(i32, shape, axis)


def lane_blocks(pieces):
    lane = iota(pieces[0].shape, 1)
    for width in (2 * RUN, RUN):
        low = (lane & width) == 0
        step = width // RUN
        results = list(pieces)
        for one in range(4):
            if not one & step:
                x, y = pieces[one], pieces[one + step]
                results[one] = jnp.where(low, x, pltpu.roll(y, width, 1))
                results[one + step] = jnp.where(low, pltpu.roll(x, LANES - width, 1), y)
        pieces = results
    return pieces


def tile_blocks(value):
    shift = (iota((8, LANES), 0) // 2 - iota((8, LANES), 1) // RUN) & 3
    result = value
    for d in range(1, 4):
        moved = pltpu.roll(pltpu.roll(value, 2 * d, 0), LANES - RUN * d, 1)
        result = jnp.where(shift == d, moved, result)
    return result


def split_two(value):
    high = value.astype(bf16).astype(f32)
    return high, value - high


def each(count, step):
    for number in range(count):
        step(number, 0)


def start_all(sources, targets, sems):
    copies = [pltpu.make_async_copy(x, y, sems.at[n]) for n, (x, y) in enumerate(zip(sources, targets))]
    for copy in copies:
        copy.start()
    return copies


def wait_all(copies):
    for copy in copies:
        copy.wait()


def pack_kernel(slot_hbm, corners_hbm, fractions_hbm, cot_hbm, out_ref, slot_ref, corners_ref, fractions_ref, cot_ref, sems):
    wait_all(
        start_all(
            (slot_hbm, corners_hbm, fractions_hbm, cot_hbm), (slot_ref, corners_ref, fractions_ref, cot_ref), sems
        )
    )
    groups = [corners_ref[0].astype(f32), corners_ref[1].astype(f32)]
    for level in range(2):
        rows = [slot_ref[level : level + 1, :].astype(f32)]
        rows += [fractions_ref[d, level : level + 1, :] for d in range(3)]
        rows += [cot_ref[level]]
        groups.append(jnp.concatenate(rows, axis=0))
    for v in range(4):
        lanes = slice(v * LANES, (v + 1) * LANES)
        for p, value in enumerate(lane_blocks([g[:, lanes] for g in groups])):
            for t in range(4):
                out_ref[16 * t + 4 * v + p] = value


def gather_lanes(value, index):
    return jnp.take_along_axis(value, index, axis=1, mode="promise_in_bounds")


class Half:
    def __init__(self, recv_ref, corner_ref, aux_ref, slots_ref, hat_ref, key_ref, column_ref, cot_ref):
        self.recv_ref, self.corner_ref, self.aux_ref, self.slots_ref = recv_ref, corner_ref, aux_ref, slots_ref
        self.hat_ref, self.key_ref, self.column_ref, self.cot_ref = hat_ref, key_ref, column_ref, cot_ref
        self.entries = [(iota((16, LANES), 0) + 16 * i).astype(f32).astype(bf16) for i in range(8)]
        self.owns = [((iota((16, LANES), 0) & 7) // 4 + 2 * i).astype(f32).astype(bf16) for i in range(8)]
        self.one = jnp.ones((16, LANES), bf16)
        self.none = jnp.zeros((16, LANES), bf16)
        self.sub = iota((8, LANES), 0)

    def count(self, unroll):
        def unpack(t, carry):
            for v in range(4):
                rows = lane_blocks([self.recv_ref[t * 16 + 4 * v + p] for p in range(4)])
                self.corner_ref[t, v] = rows[0]
                self.corner_ref[4 + t, v] = rows[1]
                self.aux_ref[t, v] = rows[2]
                self.aux_ref[4 + t, v] = rows[3]
            return carry

        if unroll:
            each(4, unpack)
        else:
            lax.fori_loop(0, 4, unpack, 0)
        first_slot = (lax.axis_index("table") * 64).astype(f32)
        self.hits = []
        for v in range(4):
            slot = jnp.concatenate([self.aux_ref[lt, v, 0:1, :] for lt in range(8)], axis=0)
            self.hits.append(jnp.where((slot >= first_slot) & (slot < first_slot + 64.0), 1.0, 0.0))
        row, column = iota((LANES, 2 * LANES), 0), iota((LANES, 2 * LANES), 1)
        upper = jnp.where(row <= column, 1.0, 0.0).astype(bf16)
        hits = jnp.concatenate(self.hits, axis=0).astype(bf16)
        counts = jnp.dot(hits, upper, preferred_element_type=f32).astype(i32)
        self.through = [counts[8 * v : 8 * v + 8, :LANES] for v in range(4)]
        self.before = [jnp.zeros((8, LANES), i32)]
        for v in range(4):
            self.before.append(self.before[v] + counts[8 * v : 8 * v + 8, LANES:])
        self.total = self.before[4]

    def gather(self, step, unroll):
        for v in range(4):
            rank = self.before[v] + self.through[v] - 1 - step * LANES
            inside = (self.hits[v] > 0.5) & (rank >= 0) & (rank < LANES)
            self.slots_ref[v] = jnp.where(inside, rank, -1)
        if unroll:
            each(8, self.compact)
        else:
            lax.fori_loop(0, 8, self.compact, 0)

    def compact(self, lt, carry):
        high, low, chosen = [], [], []
        for v in range(4):
            piece = jnp.concatenate([self.corner_ref[lt, v], self.aux_ref[lt, v]], axis=0)
            high.append(piece.astype(bf16))
            low.append((piece - high[v].astype(f32)).astype(bf16))
            slot = jnp.broadcast_to(self.slots_ref[v, pl.ds(lt, 1), :].astype(f32), (16, LANES)).astype(bf16)
            chosen.append(
                jnp.concatenate([jnp.where(slot == self.entries[i], self.one, self.none) for i in range(8)], axis=0)
            )
        rows = jnp.concatenate([jnp.concatenate(high, axis=1), jnp.concatenate(low, axis=1)], axis=0)
        both = lax.dot_general(
            rows, jnp.concatenate(chosen, axis=1), (((1,), (1,)), ((), ())), preferred_element_type=f32
        )
        corner, aux = both[:8] + both[16:24], both[8:16] + both[24:]
        hat = None
        for d in range(3):
            f = jnp.broadcast_to(aux[1 + d : 2 + d], (8, LANES))
            factor = jnp.where((self.sub >> d) & 1 == 1, f, 1.0 - f)
            hat = factor if hat is None else hat * factor
        entry = corner.astype(i32)
        self.hat_ref[lt] = hat
        self.key_ref[lt] = ((aux[0:1].astype(i32) & 3) * 4 + (entry >> 7)).astype(f32)
        self.column_ref[lt] = (entry & 127).astype(f32)
        self.cot_ref[lt] = jnp.where(self.sub < 4, pltpu.roll(aux, 4, 0), aux)
        return carry

    def hot_rows(self, lt, corners=range(8)):
        pieces = []
        for c in corners:
            wanted = jnp.broadcast_to(self.column_ref[lt, c : c + 1, :], (16, LANES)).astype(bf16)
            pieces.append(
                jnp.concatenate([jnp.where(wanted == self.entries[i], self.one, self.none) for i in range(8)], axis=0)
            )
        return jnp.concatenate(pieces, axis=1)

    def accumulate(self, grad_ref, blocks):
        def one_group(lt, carry):
            cot = self.cot_ref[lt]
            columns = []
            for c in range(8):
                value = cot * self.hat_ref[lt, c : c + 1, :]
                high = value.astype(bf16).astype(f32)
                both = jnp.concatenate([high, value - high], axis=0).astype(bf16)
                key = jnp.broadcast_to(self.key_ref[lt, c : c + 1, :], (16, LANES)).astype(bf16)
                columns.append(
                    jnp.concatenate([jnp.where(key == self.owns[i], both, self.none) for i in range(8)], axis=0)
                )
            sums = lax.dot_general(
                jnp.concatenate(columns, axis=1), self.hot_rows(lt), (((1,), (1,)), ((), ())),
                preferred_element_type=f32,
            )
            for slot in range(4):
                block = blocks(lt, slot)
                for half in range(2):
                    at = 32 * slot + 16 * half
                    grad_ref[block, 8 * half : 8 * half + 8, :] += sums[at : at + 8] + sums[at + 8 : at + 16]
            return carry

        return one_group

    def look(self, table_ref, found_ref, blocks):
        parity = self.sub // 4

        def one_group(lt, carry):
            rows = jnp.concatenate([table_ref[blocks(lt, slot)] for slot in range(4)], axis=0)
            high = rows.astype(bf16)
            low = (rows - high.astype(f32)).astype(bf16)
            deep, tall = self.hot_rows(lt, range(DEEP)), self.hot_rows(lt, range(DEEP, 8))
            seen = jnp.dot(
                jnp.concatenate([high, low], axis=1), jnp.concatenate([deep, deep], axis=0), preferred_element_type=f32
            )
            both = jnp.dot(jnp.concatenate([high, low], axis=0), tall, preferred_element_type=f32)
            seen = jnp.concatenate([seen, both[:64] + both[64:]], axis=1)
            total = jnp.zeros((8, LANES), f32)
            for c in range(8):
                own = jnp.broadcast_to(self.key_ref[lt, c : c + 1, :], (8, LANES))
                picked = jnp.zeros((8, LANES), f32)
                for i in range(8):
                    mask = own == (parity + 2 * i).astype(f32)
                    picked = jnp.where(mask, seen[8 * i : 8 * i + 8, c * LANES : (c + 1) * LANES], picked)
                total = total + picked * self.hat_ref[lt, c : c + 1, :]
            found_ref[lt] = total + pltpu.roll(total, 4, 0)
            return carry

        return one_group

    def spread(self, found_ref, result_ref):
        def one_group(t, carry):
            value = jnp.where(self.sub < 4, found_ref[t], found_ref[4 + t])
            for v in range(4):
                zero = jnp.broadcast_to(self.slots_ref[v, pl.ds(t, 1), :], (8, LANES))
                one = jnp.broadcast_to(self.slots_ref[v, pl.ds(4 + t, 1), :], (8, LANES))
                place = jnp.where(self.sub < 4, zero, one)
                taken = gather_lanes(value, jnp.maximum(place, 0))
                result_ref[t * 4 + v] += jnp.where(place >= 0, taken, 0.0)
            return carry

        return one_group


def passes_of(total):
    return (jnp.max(total) + (LANES - 1)) // LANES


def block_finder(ids_ref, other):
    mine = lax.axis_index("table")
    owner = mine * lax.axis_size("ray") + lax.axis_index("ray")
    parity = (mine + other) % 2

    def blocks(lt, slot):
        level, group = lt // 4, 2 * (lt % 4) + parity
        return level * 64 + ids_ref[(group * 2 + level) * 4 + slot, owner]

    return blocks


def gradients(half, grad_ref, blocks, ready):
    half.count(True)
    half.gather(0, True)
    ready()
    step = half.accumulate(grad_ref, blocks)
    each(8, step)
    passes = passes_of(half.total)

    def again(number, carry):
        half.gather(number, False)
        return lax.fori_loop(0, 8, step, carry)

    lax.fori_loop(1, passes, again, 0)

    @pl.when(passes > 1)
    def _():
        half.gather(0, False)

    return passes


def first_kernel(
    ids_hbm, recv_ref, m1_hbm,
    grad_ref, slots_ref, hat_ref, key_ref, column_ref, total_ref, m1_ref,
    ids_ref, corner_ref, aux_ref, cot_ref, sems,
):
    loads = start_all((ids_hbm, m1_hbm), (ids_ref, m1_ref), sems)
    grad_ref[...] = jnp.zeros_like(grad_ref)
    half = Half(recv_ref, corner_ref, aux_ref, slots_ref, hat_ref, key_ref, column_ref, cot_ref)
    gradients(half, grad_ref, block_finder(ids_ref, 0), loads[0].wait)
    total_ref[...] = half.total
    wait_all(loads[1:])


def second_kernel(
    ids_hbm, m2_hbm, recv_ref, own_recv_ref, before_ref, table_ref, m1_ref,
    own_slots_ref, own_hat_ref, own_key_ref, own_column_ref, own_total_ref,
    tnew_ref, m1new_ref, m2new_ref, out_ref,
    ids_ref, grad_ref, corner_ref, aux_ref, slots_ref, hat_ref, key_ref, column_ref, cot_ref,
    found_ref, result_ref, sems,
):
    loads = start_all((ids_hbm, m2_hbm), (ids_ref, m2new_ref), sems)
    grad_ref[...] = before_ref[...]
    result_ref[...] = jnp.zeros_like(result_ref)
    spare = (corner_ref, aux_ref, slots_ref, hat_ref, key_ref, column_ref, cot_ref)
    half = Half(recv_ref, *spare)
    blocks, own_blocks = block_finder(ids_ref, 1), block_finder(ids_ref, 0)
    passes = gradients(half, grad_ref, blocks, loads[0].wait)
    loads[1].wait()

    def update(step, carry):
        at = pl.ds(step * 4, 4)
        grad = grad_ref[at]
        first = beta_one * m1_ref[at] + (1.0 - beta_one) * grad
        second = beta_two * m2new_ref[at] + (1.0 - beta_two) * grad * grad
        m1new_ref[at] = first
        m2new_ref[at] = second
        tnew_ref[at] = table_ref[at] - learn_rate * first / (jnp.sqrt(second) + adam_eps)
        return carry

    lax.fori_loop(0, 32, update, 0)
    own = Half(own_recv_ref, corner_ref, aux_ref, own_slots_ref, own_hat_ref, own_key_ref, own_column_ref, cot_ref)
    results = [result_ref.at[pl.ds(0, 16)], result_ref.at[pl.ds(16, 16)]]
    for part, finder, result in ((own, own_blocks, results[0]), (half, blocks, results[1])):
        each(8, part.look(tnew_ref, found_ref, finder))
        each(4, part.spread(found_ref, result))

    def more_passes(part, finder, result, count):
        look, spread = part.look(tnew_ref, found_ref, finder), part.spread(found_ref, result)

        def again(number, carry):
            part.gather(number, False)
            lax.fori_loop(0, 8, look, 0)
            return lax.fori_loop(0, 4, spread, carry)

        lax.fori_loop(1, count, again, 0)

    more_passes(half, blocks, results[1], passes)
    own_passes = passes_of(own_total_ref[...])

    @pl.when(own_passes > 1)
    def _():
        again = Half(own_recv_ref, *spare)
        again.count(False)
        more_passes(again, own_blocks, results[0], own_passes)

    core = lax.axis_index("table") % 2
    for h in range(4):
        for v in range(4):
            out_ref[(2 * h + core) * 4 + v] = tile_blocks(result_ref[4 * h + v])
            out_ref[(2 * h + 1 - core) * 4 + v] = tile_blocks(result_ref[16 + 4 * h + v])


def network_kernel(recv_ref, win_ref, wout_ref, out_ref):
    columns = []
    for v in range(4):
        total = recv_ref[v]
        for t in range(1, 8):
            total = total + recv_ref[4 * t + v]
        columns.append(tile_blocks(total))
    encoded = jnp.concatenate(columns, axis=1)
    w_high, w_low = split_two(win_ref[...])
    e_high, e_low = split_two(encoded)
    hidden = lax.dot_general(
        jnp.concatenate([w_high, w_low, w_high], axis=0).astype(bf16),
        jnp.concatenate([e_high, e_high, e_low], axis=0).astype(bf16),
        (((0,), (0,)), ((), ())), preferred_element_type=f32,
    )
    h_high, h_low = split_two(jnp.maximum(hidden, 0.0))
    w_high, w_low = split_two(wout_ref[...])
    both = jnp.dot(
        jnp.concatenate([w_high, w_low], axis=0).astype(bf16), h_high.astype(bf16), preferred_element_type=f32
    )
    rest = jnp.dot(w_high.astype(bf16), h_low.astype(bf16), preferred_element_type=f32)
    out_ref[...] = both[:16] + both[16:] + rest


VMEM = pl.BlockSpec(memory_space=pltpu.VMEM)
HBM = pl.BlockSpec(memory_space=pltpu.HBM)


def call(kernel, outs, in_specs, scratch=(), out_specs=None, **extra):
    return pl.pallas_call(
        kernel,
        out_shape=[jax.ShapeDtypeStruct(*o) if isinstance(o, tuple) else o for o in outs],
        in_specs=in_specs,
        out_specs=[VMEM] * len(outs) if out_specs is None else out_specs,
        scratch_shapes=list(scratch),
        compiler_params=pltpu.CompilerParams(vmem_limit_bytes=VMEM_LIMIT),
        **extra,
    )


def in_hbm(*arrays):
    return [pltpu.with_memory_space_constraint(array, pltpu.HBM) for array in arrays]


def exchange(value, groups=None):
    return lax.all_to_all(
        value, ("table", "ray"), split_axis=0, concat_axis=0, tiled=True, axis_index_groups=groups
    )


def same_core():
    tables, rays = lax.axis_size("table"), lax.axis_size("ray")
    return [[t * rays + r for t in range(core, tables, 2) for r in range(rays)] for core in range(2)]


def swap_cores(value):
    return lax.ppermute(value, "table", [(t, t ^ 1) for t in range(lax.axis_size("table"))])


def rows_of(array):
    levels, blocks = array.shape[:2]
    return array.reshape(levels, blocks, 4, 4, LANES).transpose(0, 1, 3, 2, 4).reshape(levels * blocks, 16, LANES)


def rows_back(array, shape):
    levels, blocks = shape[:2]
    return array.reshape(levels, blocks, 4, 4, LANES).transpose(0, 1, 3, 2, 4).reshape(shape)


def on_device(
    table,
    moment1,
    moment2,
    block_ids,
    sample_slot,
    corners,
    fractions,
    feat_cot,
    weight_in,
    weight_out,
):
    (packed,) = call(
        pack_kernel,
        [((64, 8, LANES), f32)],
        [HBM] * 4,
        [
            pltpu.VMEM((2, 512), i32),
            pltpu.VMEM((2, 8, 512), i32),
            pltpu.VMEM((3, 2, 512), f32),
            pltpu.VMEM((2, 4, 512), f32),
            pltpu.SemaphoreType.DMA((4,)),
        ],
    )(*in_hbm(sample_slot, corners, fractions.transpose(1, 0, 2), feat_cot))
    samples = exchange(packed, same_core())
    others = swap_cores(samples)
    rows = (128, 16, LANES)
    (ids,) = in_hbm(block_ids.transpose(0, 1, 3, 2).reshape(64, 128))
    tile = pltpu.VMEM((8, 8, LANES), f32)
    lists = pltpu.VMEM((4, 8, LANES), i32)
    full = pltpu.VMEM(rows, f32)
    data = pltpu.VMEM((8, 4, 8, LANES), f32)
    id_table = pltpu.SMEM((64, LANES), i32)
    grad, slots, hat, key, column, total, m1 = call(
        first_kernel,
        [full, lists, tile, tile, tile, pltpu.VMEM((8, LANES), i32), full],
        [HBM, VMEM, HBM],
        [id_table, data, data, tile, pltpu.SemaphoreType.DMA((2,))],
        cost_estimate=pl.CostEstimate(flops=1 << 30, bytes_accessed=4 << 20, transcendentals=0),
    )(ids, samples, *in_hbm(rows_of(moment1)))
    tnew, m1new, m2new, found = call(
        second_kernel,
        [full, full, full, ((32, 8, LANES), f32)],
        [HBM, HBM] + [VMEM] * 10,
        [
            id_table, full, data, data, lists, tile, tile, tile, tile, tile,
            pltpu.VMEM((32, 8, LANES), f32),
            pltpu.SemaphoreType.DMA((2,)),
        ],
    )(ids, *in_hbm(rows_of(moment2)), others, samples, grad, rows_of(table), m1, slots, hat, key, column, total)
    back = exchange(found.reshape(128, 2, LANES)).reshape(32, 8, LANES)
    (mlp_out,) = call(network_kernel, [((16, 512), f32)], [VMEM] * 3)(back, weight_in.T, weight_out)
    shape = table.shape
    return (rows_back(tnew, shape), rows_back(m1new, shape), rows_back(m2new, shape), mlp_out)


def solution(mesh):
    in_specs = (
        P(None, ("table", "ray"), None, None),
        P(None, ("table", "ray"), None, None),
        P(None, ("table", "ray"), None, None),
        P(),
        P(None, ("table", "ray")),
        P(None, None, ("table", "ray")),
        P(None, None, ("table", "ray")),
        P(None, None, ("table", "ray")),
        P(),
        P(),
    )
    out_specs = (
        P(None, ("table", "ray"), None, None),
        P(None, ("table", "ray"), None, None),
        P(None, ("table", "ray"), None, None),
        P(None, ("table", "ray")),
    )
    return jax.shard_map(
        on_device, mesh=mesh, in_specs=in_specs, out_specs=out_specs, check_vma=False
    )
```

```python
import jax
import jax.numpy as jnp
from jax import lax
from jax.experimental import pallas as pl
from jax.experimental.pallas import tpu as pltpu
from jax.sharding import PartitionSpec as P

beta_one = 0.9
beta_two = 0.99
learn_rate = 0.01
adam_eps = 1e-15

LANES = 128
RUN = 32
VMEM_LIMIT = 16 << 20
DEEP = 4
f32, bf16, i32 = jnp.float32, jnp.bfloat16, jnp.int32


def iota(shape, axis):
    return lax.broadcasted_iota(i32, shape, axis)


def lane_blocks(pieces):
    lane = iota(pieces[0].shape, 1)
    for width in (2 * RUN, RUN):
        low = (lane & width) == 0
        step = width // RUN
        results = list(pieces)
        for one in range(4):
            if not one & step:
                x, y = pieces[one], pieces[one + step]
                results[one] = jnp.where(low, x, pltpu.roll(y, width, 1))
                results[one + step] = jnp.where(low, pltpu.roll(x, LANES - width, 1), y)
        pieces = results
    return pieces


def tile_blocks(value):
    shift = (iota((8, LANES), 0) // 2 - iota((8, LANES), 1) // RUN) & 3
    result = value
    for d in range(1, 4):
        moved = pltpu.roll(pltpu.roll(value, 2 * d, 0), LANES - RUN * d, 1)
        result = jnp.where(shift == d, moved, result)
    return result


def split_two(value):
    high = value.astype(bf16).astype(f32)
    return high, value - high


def each(count, step):
    for number in range(count):
        step(number, 0)


def start_all(sources, targets, sems):
    copies = [pltpu.make_async_copy(x, y, sems.at[n]) for n, (x, y) in enumerate(zip(sources, targets))]
    for copy in copies:
        copy.start()
    return copies


def wait_all(copies):
    for copy in copies:
        copy.wait()


def pack_kernel(slot_hbm, corners_hbm, fractions_hbm, cot_hbm, out_ref, slot_ref, corners_ref, fractions_ref, cot_ref, sems):
    wait_all(
        start_all(
            (slot_hbm, corners_hbm, fractions_hbm, cot_hbm), (slot_ref, corners_ref, fractions_ref, cot_ref), sems
        )
    )
    groups = [corners_ref[0].astype(f32), corners_ref[1].astype(f32)]
    for level in range(2):
        rows = [slot_ref[level : level + 1, :].astype(f32)]
        rows += [fractions_ref[d, level : level + 1, :] for d in range(3)]
        rows += [cot_ref[level]]
        groups.append(jnp.concatenate(rows, axis=0))
    for v in range(4):
        lanes = slice(v * LANES, (v + 1) * LANES)
        for p, value in enumerate(lane_blocks([g[:, lanes] for g in groups])):
            for t in range(4):
                out_ref[16 * t + 4 * v + p] = value


def gather_lanes(value, index):
    return jnp.take_along_axis(value, index, axis=1, mode="promise_in_bounds")


class Half:
    def __init__(self, recv_ref, corner_ref, aux_ref, slots_ref, hat_ref, key_ref, column_ref, cot_ref):
        self.recv_ref, self.corner_ref, self.aux_ref, self.slots_ref = recv_ref, corner_ref, aux_ref, slots_ref
        self.hat_ref, self.key_ref, self.column_ref, self.cot_ref = hat_ref, key_ref, column_ref, cot_ref
        self.entries = [(iota((16, LANES), 0) + 16 * i).astype(f32).astype(bf16) for i in range(8)]
        self.owns = [((iota((16, LANES), 0) & 7) // 4 + 2 * i).astype(f32).astype(bf16) for i in range(8)]
        self.one = jnp.ones((16, LANES), bf16)
        self.none = jnp.zeros((16, LANES), bf16)
        self.sub = iota((8, LANES), 0)

    def count(self, unroll):
        def unpack(t, carry):
            for v in range(4):
                rows = lane_blocks([self.recv_ref[t * 16 + 4 * v + p] for p in range(4)])
                self.corner_ref[t, v] = rows[0]
                self.corner_ref[4 + t, v] = rows[1]
                self.aux_ref[t, v] = rows[2]
                self.aux_ref[4 + t, v] = rows[3]
            return carry

        if unroll:
            each(4, unpack)
        else:
            lax.fori_loop(0, 4, unpack, 0)
        first_slot = (lax.axis_index("table") * 64).astype(f32)
        self.hits = []
        for v in range(4):
            slot = jnp.concatenate([self.aux_ref[lt, v, 0:1, :] for lt in range(8)], axis=0)
            self.hits.append(jnp.where((slot >= first_slot) & (slot < first_slot + 64.0), 1.0, 0.0))
        row, column = iota((LANES, 2 * LANES), 0), iota((LANES, 2 * LANES), 1)
        upper = jnp.where(row <= column, 1.0, 0.0).astype(bf16)
        hits = jnp.concatenate(self.hits, axis=0).astype(bf16)
        counts = jnp.dot(hits, upper, preferred_element_type=f32).astype(i32)
        self.through = [counts[8 * v : 8 * v + 8, :LANES] for v in range(4)]
        self.before = [jnp.zeros((8, LANES), i32)]
        for v in range(4):
            self.before.append(self.before[v] + counts[8 * v : 8 * v + 8, LANES:])
        self.total = self.before[4]

    def gather(self, step, unroll):
        for v in range(4):
            rank = self.before[v] + self.through[v] - 1 - step * LANES
            inside = (self.hits[v] > 0.5) & (rank >= 0) & (rank < LANES)
            self.slots_ref[v] = jnp.where(inside, rank, -1)
        if unroll:
            each(8, self.compact)
        else:
            lax.fori_loop(0, 8, self.compact, 0)

    def compact(self, lt, carry):
        high, low, chosen = [], [], []
        for v in range(4):
            piece = jnp.concatenate([self.corner_ref[lt, v], self.aux_ref[lt, v]], axis=0)
            high.append(piece.astype(bf16))
            low.append((piece - high[v].astype(f32)).astype(bf16))
            slot = jnp.broadcast_to(self.slots_ref[v, pl.ds(lt, 1), :].astype(f32), (16, LANES)).astype(bf16)
            chosen.append(
                jnp.concatenate([jnp.where(slot == self.entries[i], self.one, self.none) for i in range(8)], axis=0)
            )
        rows = jnp.concatenate([jnp.concatenate(high, axis=1), jnp.concatenate(low, axis=1)], axis=0)
        both = lax.dot_general(
            rows, jnp.concatenate(chosen, axis=1), (((1,), (1,)), ((), ())), preferred_element_type=f32
        )
        corner, aux = both[:8] + both[16:24], both[8:16] + both[24:]
        hat = None
        for d in range(3):
            f = jnp.broadcast_to(aux[1 + d : 2 + d], (8, LANES))
            factor = jnp.where((self.sub >> d) & 1 == 1, f, 1.0 - f)
            hat = factor if hat is None else hat * factor
        entry = corner.astype(i32)
        self.hat_ref[lt] = hat
        self.key_ref[lt] = ((aux[0:1].astype(i32) & 3) * 4 + (entry >> 7)).astype(f32)
        self.column_ref[lt] = (entry & 127).astype(f32)
        self.cot_ref[lt] = jnp.where(self.sub < 4, pltpu.roll(aux, 4, 0), aux)
        return carry

    def hot_rows(self, lt, corners=range(8)):
        pieces = []
        for c in corners:
            wanted = jnp.broadcast_to(self.column_ref[lt, c : c + 1, :], (16, LANES)).astype(bf16)
            pieces.append(
                jnp.concatenate([jnp.where(wanted == self.entries[i], self.one, self.none) for i in range(8)], axis=0)
            )
        return jnp.concatenate(pieces, axis=1)

    def accumulate(self, grad_ref, blocks):
        def one_group(lt, carry):
            cot = self.cot_ref[lt]
            columns = []
            for c in range(8):
                value = cot * self.hat_ref[lt, c : c + 1, :]
                high = value.astype(bf16).astype(f32)
                both = jnp.concatenate([high, value - high], axis=0).astype(bf16)
                key = jnp.broadcast_to(self.key_ref[lt, c : c + 1, :], (16, LANES)).astype(bf16)
                columns.append(
                    jnp.concatenate([jnp.where(key == self.owns[i], both, self.none) for i in range(8)], axis=0)
                )
            sums = lax.dot_general(
                jnp.concatenate(columns, axis=1), self.hot_rows(lt), (((1,), (1,)), ((), ())),
                preferred_element_type=f32,
            )
            for slot in range(4):
                block = blocks(lt, slot)
                for half in range(2):
                    at = 32 * slot + 16 * half
                    grad_ref[block, 8 * half : 8 * half + 8, :] += sums[at : at + 8] + sums[at + 8 : at + 16]
            return carry

        return one_group

    def look(self, rows_at, found_ref, blocks):
        parity = self.sub // 4

        def one_group(lt, carry):
            rows = jnp.concatenate([rows_at(blocks(lt, slot)) for slot in range(4)], axis=0)
            high = rows.astype(bf16)
            low = (rows - high.astype(f32)).astype(bf16)
            deep, tall = self.hot_rows(lt, range(DEEP)), self.hot_rows(lt, range(DEEP, 8))
            seen = jnp.dot(
                jnp.concatenate([high, low], axis=1), jnp.concatenate([deep, deep], axis=0), preferred_element_type=f32
            )
            both = jnp.dot(jnp.concatenate([high, low], axis=0), tall, preferred_element_type=f32)
            seen = jnp.concatenate([seen, both[:64] + both[64:]], axis=1)
            total = jnp.zeros((8, LANES), f32)
            for c in range(8):
                own = jnp.broadcast_to(self.key_ref[lt, c : c + 1, :], (8, LANES))
                picked = jnp.zeros((8, LANES), f32)
                for i in range(8):
                    mask = own == (parity + 2 * i).astype(f32)
                    picked = jnp.where(mask, seen[8 * i : 8 * i + 8, c * LANES : (c + 1) * LANES], picked)
                total = total + picked * self.hat_ref[lt, c : c + 1, :]
            found_ref[lt] = total + pltpu.roll(total, 4, 0)
            return carry

        return one_group

    def spread(self, found_ref, result_ref):
        def one_group(t, carry):
            value = jnp.where(self.sub < 4, found_ref[t], found_ref[4 + t])
            for v in range(4):
                zero = jnp.broadcast_to(self.slots_ref[v, pl.ds(t, 1), :], (8, LANES))
                one = jnp.broadcast_to(self.slots_ref[v, pl.ds(4 + t, 1), :], (8, LANES))
                place = jnp.where(self.sub < 4, zero, one)
                taken = gather_lanes(value, jnp.maximum(place, 0))
                result_ref[t * 4 + v] += jnp.where(place >= 0, taken, 0.0)
            return carry

        return one_group


def passes_of(total):
    return (jnp.max(total) + (LANES - 1)) // LANES


def block_finder(ids_ref, other):
    mine = lax.axis_index("table")
    owner = mine * lax.axis_size("ray") + lax.axis_index("ray")
    parity = (mine + other) % 2

    def blocks(lt, slot):
        level, group = lt // 4, 2 * (lt % 4) + parity
        return level * 64 + ids_ref[(group * 2 + level) * 4 + slot, owner]

    return blocks


def gradients(half, grad_ref, blocks, ready):
    half.count(True)
    half.gather(0, True)
    ready()
    step = half.accumulate(grad_ref, blocks)
    each(8, step)
    passes = passes_of(half.total)

    def again(number, carry):
        half.gather(number, False)
        return lax.fori_loop(0, 8, step, carry)

    lax.fori_loop(1, passes, again, 0)

    @pl.when(passes > 1)
    def _():
        half.gather(0, False)

    return passes


def first_kernel(
    ids_hbm, recv_ref, m1_hbm,
    grad_ref, slots_ref, hat_ref, key_ref, column_ref, total_ref, m1_ref,
    ids_ref, corner_ref, aux_ref, cot_ref, sems,
):
    loads = start_all((ids_hbm, m1_hbm), (ids_ref, m1_ref), sems)
    grad_ref[...] = jnp.zeros_like(grad_ref)
    half = Half(recv_ref, corner_ref, aux_ref, slots_ref, hat_ref, key_ref, column_ref, cot_ref)
    gradients(half, grad_ref, block_finder(ids_ref, 0), loads[0].wait)
    total_ref[...] = half.total
    wait_all(loads[1:])


def moments(grad, m1, m2):
    first = beta_one * m1 + (1.0 - beta_one) * grad
    second = beta_two * m2 + (1.0 - beta_two) * grad * grad
    return first, second


def stepped(table, first, second):
    return table - learn_rate * first / (jnp.sqrt(second) + adam_eps)


def second_kernel(
    ids_hbm, m2_hbm, recv_ref, own_recv_ref, before_ref, table_ref, m1_ref,
    own_slots_ref, own_hat_ref, own_key_ref, own_column_ref, own_total_ref,
    grad_ref, m2_ref, out_ref,
    ids_ref, corner_ref, aux_ref, slots_ref, hat_ref, key_ref, column_ref, cot_ref,
    found_ref, result_ref, sems,
):
    loads = start_all((ids_hbm, m2_hbm), (ids_ref, m2_ref), sems)
    grad_ref[...] = before_ref[...]
    result_ref[...] = jnp.zeros_like(result_ref)
    spare = (corner_ref, aux_ref, slots_ref, hat_ref, key_ref, column_ref, cot_ref)
    half = Half(recv_ref, *spare)
    blocks, own_blocks = block_finder(ids_ref, 1), block_finder(ids_ref, 0)
    passes = gradients(half, grad_ref, blocks, loads[0].wait)
    loads[1].wait()

    def rows_at(block):
        first, second = moments(grad_ref[block], m1_ref[block], m2_ref[block])
        return stepped(table_ref[block], first, second)

    own = Half(own_recv_ref, corner_ref, aux_ref, own_slots_ref, own_hat_ref, own_key_ref, own_column_ref, cot_ref)
    results = [result_ref.at[pl.ds(0, 16)], result_ref.at[pl.ds(16, 16)]]
    for part, finder, result in ((own, own_blocks, results[0]), (half, blocks, results[1])):
        each(8, part.look(rows_at, found_ref, finder))
        each(4, part.spread(found_ref, result))

    def more_passes(part, finder, result, count):
        look, spread = part.look(rows_at, found_ref, finder), part.spread(found_ref, result)

        def again(number, carry):
            part.gather(number, False)
            lax.fori_loop(0, 8, look, 0)
            return lax.fori_loop(0, 4, spread, carry)

        lax.fori_loop(1, count, again, 0)

    more_passes(half, blocks, results[1], passes)
    own_passes = passes_of(own_total_ref[...])

    @pl.when(own_passes > 1)
    def _():
        again = Half(own_recv_ref, *spare)
        again.count(False)
        more_passes(again, own_blocks, results[0], own_passes)

    core = lax.axis_index("table") % 2
    for h in range(4):
        for v in range(4):
            out_ref[(2 * h + core) * 4 + v] = tile_blocks(result_ref[4 * h + v])
            out_ref[(2 * h + 1 - core) * 4 + v] = tile_blocks(result_ref[16 + 4 * h + v])


def third_kernel(grad_ref, m2_ref, m1_hbm, table_hbm, tnew_hbm, m1new_hbm, m2new_hbm, table_ref, m1_ref, m2new_ref, loads, stores):
    chunks = [pl.ds(32 * n, 32) for n in range(4)]
    arriving = []
    for n, chunk in enumerate(chunks):
        sources = [ref.at[chunk] for ref in (m1_hbm, table_hbm)]
        arriving.append(start_all(sources, [ref.at[chunk] for ref in (m1_ref, table_ref)], loads.at[n]))
    leaving = []
    for n, chunk in enumerate(chunks):
        wait_all(arriving[n])

        def update(step, carry):
            at = pl.ds(32 * n + step * 4, 4)
            first, second = moments(grad_ref[at], m1_ref[at], m2_ref[at])
            m1_ref[at] = first
            m2new_ref[at] = second
            table_ref[at] = stepped(table_ref[at], first, second)
            return carry

        lax.fori_loop(0, 8, update, 0)
        leaving += start_all(
            [ref.at[chunk] for ref in (table_ref, m1_ref, m2new_ref)],
            [ref.at[chunk] for ref in (tnew_hbm, m1new_hbm, m2new_hbm)],
            stores.at[n],
        )
    wait_all(leaving)


def network_kernel(recv_ref, win_ref, wout_ref, out_ref):
    columns = []
    for v in range(4):
        total = recv_ref[v]
        for t in range(1, 8):
            total = total + recv_ref[4 * t + v]
        columns.append(tile_blocks(total))
    encoded = jnp.concatenate(columns, axis=1)
    w_high, w_low = split_two(win_ref[...])
    e_high, e_low = split_two(encoded)
    hidden = lax.dot_general(
        jnp.concatenate([w_high, w_low, w_high], axis=0).astype(bf16),
        jnp.concatenate([e_high, e_high, e_low], axis=0).astype(bf16),
        (((0,), (0,)), ((), ())), preferred_element_type=f32,
    )
    h_high, h_low = split_two(jnp.maximum(hidden, 0.0))
    w_high, w_low = split_two(wout_ref[...])
    both = jnp.dot(
        jnp.concatenate([w_high, w_low], axis=0).astype(bf16), h_high.astype(bf16), preferred_element_type=f32
    )
    rest = jnp.dot(w_high.astype(bf16), h_low.astype(bf16), preferred_element_type=f32)
    out_ref[...] = both[:16] + both[16:] + rest


VMEM = pl.BlockSpec(memory_space=pltpu.VMEM)
HBM = pl.BlockSpec(memory_space=pltpu.HBM)


def call(kernel, outs, in_specs, scratch=(), out_specs=None, **extra):
    return pl.pallas_call(
        kernel,
        out_shape=[jax.ShapeDtypeStruct(*o) if isinstance(o, tuple) else o for o in outs],
        in_specs=in_specs,
        out_specs=[VMEM] * len(outs) if out_specs is None else out_specs,
        scratch_shapes=list(scratch),
        compiler_params=pltpu.CompilerParams(vmem_limit_bytes=VMEM_LIMIT),
        **extra,
    )


def in_hbm(*arrays):
    return [pltpu.with_memory_space_constraint(array, pltpu.HBM) for array in arrays]


def exchange(value, groups=None):
    return lax.all_to_all(
        value, ("table", "ray"), split_axis=0, concat_axis=0, tiled=True, axis_index_groups=groups
    )


def same_core():
    tables, rays = lax.axis_size("table"), lax.axis_size("ray")
    return [[t * rays + r for t in range(core, tables, 2) for r in range(rays)] for core in range(2)]


def swap_cores(value):
    return lax.ppermute(value, "table", [(t, t ^ 1) for t in range(lax.axis_size("table"))])


def rows_of(array):
    levels, blocks = array.shape[:2]
    return array.reshape(levels, blocks, 4, 4, LANES).transpose(0, 1, 3, 2, 4).reshape(levels * blocks, 16, LANES)


def rows_back(array, shape):
    levels, blocks = shape[:2]
    return array.reshape(levels, blocks, 4, 4, LANES).transpose(0, 1, 3, 2, 4).reshape(shape)


def on_device(
    table,
    moment1,
    moment2,
    block_ids,
    sample_slot,
    corners,
    fractions,
    feat_cot,
    weight_in,
    weight_out,
):
    (packed,) = call(
        pack_kernel,
        [((64, 8, LANES), f32)],
        [HBM] * 4,
        [
            pltpu.VMEM((2, 512), i32),
            pltpu.VMEM((2, 8, 512), i32),
            pltpu.VMEM((3, 2, 512), f32),
            pltpu.VMEM((2, 4, 512), f32),
            pltpu.SemaphoreType.DMA((4,)),
        ],
    )(*in_hbm(sample_slot, corners, fractions.transpose(1, 0, 2), feat_cot))
    samples = exchange(packed, same_core())
    others = swap_cores(samples)
    rows = (128, 16, LANES)
    (ids,) = in_hbm(block_ids.transpose(0, 1, 3, 2).reshape(64, 128))
    tile = pltpu.VMEM((8, 8, LANES), f32)
    lists = pltpu.VMEM((4, 8, LANES), i32)
    full = pltpu.VMEM(rows, f32)
    data = pltpu.VMEM((8, 4, 8, LANES), f32)
    id_table = pltpu.SMEM((64, LANES), i32)
    grad, slots, hat, key, column, total, m1 = call(
        first_kernel,
        [full, lists, tile, tile, tile, pltpu.VMEM((8, LANES), i32), full],
        [HBM, VMEM, HBM],
        [id_table, data, data, tile, pltpu.SemaphoreType.DMA((2,))],
        cost_estimate=pl.CostEstimate(flops=1 << 30, bytes_accessed=4 << 20, transcendentals=0),
    )(ids, samples, *in_hbm(rows_of(moment1)))
    grad, m2, found = call(
        second_kernel,
        [full, full, ((32, 8, LANES), f32)],
        [HBM, HBM] + [VMEM] * 10,
        [
            id_table, data, data, lists, tile, tile, tile, tile, tile,
            pltpu.VMEM((32, 8, LANES), f32),
            pltpu.SemaphoreType.DMA((2,)),
        ],
    )(ids, *in_hbm(rows_of(moment2)), others, samples, grad, rows_of(table), m1, slots, hat, key, column, total)
    back = exchange(found.reshape(128, 2, LANES)).reshape(32, 8, LANES)
    tnew, m1new, m2new = call(
        third_kernel,
        [(rows, f32)] * 3,
        [VMEM] * 2 + [HBM] * 2,
        [full, full, full, pltpu.SemaphoreType.DMA((4, 2)), pltpu.SemaphoreType.DMA((4, 3))],
        [HBM] * 3,
        cost_estimate=pl.CostEstimate(flops=20 << 20, bytes_accessed=7 << 20, transcendentals=0),
    )(grad, m2, *in_hbm(rows_of(moment1), rows_of(table)))
    (mlp_out,) = call(network_kernel, [((16, 512), f32)], [VMEM] * 3)(back, weight_in.T, weight_out)
    shape = table.shape
    return (rows_back(tnew, shape), rows_back(m1new, shape), rows_back(m2new, shape), mlp_out)


def solution(mesh):
    in_specs = (
        P(None, ("table", "ray"), None, None),
        P(None, ("table", "ray"), None, None),
        P(None, ("table", "ray"), None, None),
        P(),
        P(None, ("table", "ray")),
        P(None, None, ("table", "ray")),
        P(None, None, ("table", "ray")),
        P(None, None, ("table", "ray")),
        P(),
        P(),
    )
    out_specs = (
        P(None, ("table", "ray"), None, None),
        P(None, ("table", "ray"), None, None),
        P(None, ("table", "ray"), None, None),
        P(None, ("table", "ray")),
    )
    return jax.shard_map(
        on_device, mesh=mesh, in_specs=in_specs, out_specs=out_specs, check_vma=False
    )
```

```python
import jax
import jax.numpy as jnp
from jax import lax
from jax.experimental import pallas as pl
from jax.experimental.pallas import tpu as pltpu
from jax.sharding import PartitionSpec as P

beta_one = 0.9
beta_two = 0.99
learn_rate = 0.01
adam_eps = 1e-15

LANES = 128
RUN = 32
VMEM_LIMIT = 16 << 20
DEEP = 4
f32, bf16, i32 = jnp.float32, jnp.bfloat16, jnp.int32


def iota(shape, axis):
    return lax.broadcasted_iota(i32, shape, axis)


def lane_blocks(pieces):
    lane = iota(pieces[0].shape, 1)
    for width in (2 * RUN, RUN):
        low = (lane & width) == 0
        step = width // RUN
        results = list(pieces)
        for one in range(4):
            if not one & step:
                x, y = pieces[one], pieces[one + step]
                results[one] = jnp.where(low, x, pltpu.roll(y, width, 1))
                results[one + step] = jnp.where(low, pltpu.roll(x, LANES - width, 1), y)
        pieces = results
    return pieces


def tile_blocks(value):
    shift = (iota((8, LANES), 0) // 2 - iota((8, LANES), 1) // RUN) & 3
    result = value
    for d in range(1, 4):
        moved = pltpu.roll(pltpu.roll(value, 2 * d, 0), LANES - RUN * d, 1)
        result = jnp.where(shift == d, moved, result)
    return result


def split_two(value):
    high = value.astype(bf16).astype(f32)
    return high, value - high


def each(count, step):
    for number in range(count):
        step(number, 0)


def start_all(sources, targets, sems):
    copies = [pltpu.make_async_copy(x, y, sems.at[n]) for n, (x, y) in enumerate(zip(sources, targets))]
    for copy in copies:
        copy.start()
    return copies


def wait_all(copies):
    for copy in copies:
        copy.wait()


def pack_kernel(slot_hbm, corners_hbm, fractions_hbm, cot_hbm, out_ref, slot_ref, corners_ref, fractions_ref, cot_ref, sems):
    wait_all(
        start_all(
            (slot_hbm, corners_hbm, fractions_hbm, cot_hbm), (slot_ref, corners_ref, fractions_ref, cot_ref), sems
        )
    )
    groups = [corners_ref[0].astype(f32), corners_ref[1].astype(f32)]
    for level in range(2):
        rows = [slot_ref[level : level + 1, :].astype(f32)]
        rows += [fractions_ref[d, level : level + 1, :] for d in range(3)]
        rows += [cot_ref[level]]
        groups.append(jnp.concatenate(rows, axis=0))
    for v in range(4):
        lanes = slice(v * LANES, (v + 1) * LANES)
        for p, value in enumerate(lane_blocks([g[:, lanes] for g in groups])):
            for t in range(4):
                out_ref[16 * t + 4 * v + p] = value


def gather_lanes(value, index):
    return jnp.take_along_axis(value, index, axis=1, mode="promise_in_bounds")


class Half:
    def __init__(self, recv_ref, corner_ref, aux_ref, slots_ref, hat_ref, key_ref, column_ref, cot_ref):
        self.recv_ref, self.corner_ref, self.aux_ref, self.slots_ref = recv_ref, corner_ref, aux_ref, slots_ref
        self.hat_ref, self.key_ref, self.column_ref, self.cot_ref = hat_ref, key_ref, column_ref, cot_ref
        self.entries = [(iota((16, LANES), 0) + 16 * i).astype(f32).astype(bf16) for i in range(8)]
        self.owns = [((iota((16, LANES), 0) & 7) // 4 + 2 * i).astype(f32).astype(bf16) for i in range(8)]
        self.one = jnp.ones((16, LANES), bf16)
        self.none = jnp.zeros((16, LANES), bf16)
        self.sub = iota((8, LANES), 0)

    def count(self, unroll):
        def unpack(t, carry):
            for v in range(4):
                rows = lane_blocks([self.recv_ref[t * 16 + 4 * v + p] for p in range(4)])
                self.corner_ref[t, v] = rows[0]
                self.corner_ref[4 + t, v] = rows[1]
                self.aux_ref[t, v] = rows[2]
                self.aux_ref[4 + t, v] = rows[3]
            return carry

        if unroll:
            each(4, unpack)
        else:
            lax.fori_loop(0, 4, unpack, 0)
        first_slot = (lax.axis_index("table") * 64).astype(f32)
        self.hits = []
        for v in range(4):
            slot = jnp.concatenate([self.aux_ref[lt, v, 0:1, :] for lt in range(8)], axis=0)
            self.hits.append(jnp.where((slot >= first_slot) & (slot < first_slot + 64.0), 1.0, 0.0))
        row, column = iota((LANES, 2 * LANES), 0), iota((LANES, 2 * LANES), 1)
        upper = jnp.where(row <= column, 1.0, 0.0).astype(bf16)
        hits = jnp.concatenate(self.hits, axis=0).astype(bf16)
        counts = jnp.dot(hits, upper, preferred_element_type=f32).astype(i32)
        self.through = [counts[8 * v : 8 * v + 8, :LANES] for v in range(4)]
        self.before = [jnp.zeros((8, LANES), i32)]
        for v in range(4):
            self.before.append(self.before[v] + counts[8 * v : 8 * v + 8, LANES:])
        self.total = self.before[4]

    def gather(self, step, unroll):
        for v in range(4):
            rank = self.before[v] + self.through[v] - 1 - step * LANES
            inside = (self.hits[v] > 0.5) & (rank >= 0) & (rank < LANES)
            self.slots_ref[v] = jnp.where(inside, rank, -1)
        if unroll:
            each(8, self.compact)
        else:
            lax.fori_loop(0, 8, self.compact, 0)

    def compact(self, lt, carry):
        high, low, chosen = [], [], []
        for v in range(4):
            piece = jnp.concatenate([self.corner_ref[lt, v], self.aux_ref[lt, v]], axis=0)
            high.append(piece.astype(bf16))
            low.append((piece - high[v].astype(f32)).astype(bf16))
            slot = jnp.broadcast_to(self.slots_ref[v, pl.ds(lt, 1), :].astype(f32), (16, LANES)).astype(bf16)
            chosen.append(
                jnp.concatenate([jnp.where(slot == self.entries[i], self.one, self.none) for i in range(8)], axis=0)
            )
        rows = jnp.concatenate([jnp.concatenate(high, axis=1), jnp.concatenate(low, axis=1)], axis=0)
        both = lax.dot_general(
            rows, jnp.concatenate(chosen, axis=1), (((1,), (1,)), ((), ())), preferred_element_type=f32
        )
        corner, aux = both[:8] + both[16:24], both[8:16] + both[24:]
        hat = None
        for d in range(3):
            f = jnp.broadcast_to(aux[1 + d : 2 + d], (8, LANES))
            factor = jnp.where((self.sub >> d) & 1 == 1, f, 1.0 - f)
            hat = factor if hat is None else hat * factor
        entry = corner.astype(i32)
        self.hat_ref[lt] = hat
        self.key_ref[lt] = ((aux[0:1].astype(i32) & 3) * 4 + (entry >> 7)).astype(f32)
        self.column_ref[lt] = (entry & 127).astype(f32)
        self.cot_ref[lt] = jnp.where(self.sub < 4, pltpu.roll(aux, 4, 0), aux)
        return carry

    def hot_rows(self, lt, corners=range(8)):
        pieces = []
        for c in corners:
            wanted = jnp.broadcast_to(self.column_ref[lt, c : c + 1, :], (16, LANES)).astype(bf16)
            pieces.append(
                jnp.concatenate([jnp.where(wanted == self.entries[i], self.one, self.none) for i in range(8)], axis=0)
            )
        return jnp.concatenate(pieces, axis=1)

    def accumulate(self, grad_ref, blocks):
        def one_group(lt, carry):
            cot = self.cot_ref[lt]
            columns = []
            for c in range(8):
                value = cot * self.hat_ref[lt, c : c + 1, :]
                high = value.astype(bf16).astype(f32)
                both = jnp.concatenate([high, value - high], axis=0).astype(bf16)
                key = jnp.broadcast_to(self.key_ref[lt, c : c + 1, :], (16, LANES)).astype(bf16)
                columns.append(
                    jnp.concatenate([jnp.where(key == self.owns[i], both, self.none) for i in range(8)], axis=0)
                )
            sums = lax.dot_general(
                jnp.concatenate(columns, axis=1), self.hot_rows(lt), (((1,), (1,)), ((), ())),
                preferred_element_type=f32,
            )
            for slot in range(4):
                block = blocks(lt, slot)
                for half in range(2):
                    at = 32 * slot + 16 * half
                    grad_ref[block, 8 * half : 8 * half + 8, :] += sums[at : at + 8] + sums[at + 8 : at + 16]
            return carry

        return one_group

    def look(self, rows_at, found_ref, blocks):
        parity = self.sub // 4

        def one_group(lt, carry):
            rows = jnp.concatenate([rows_at(blocks(lt, slot)) for slot in range(4)], axis=0)
            high = rows.astype(bf16)
            low = (rows - high.astype(f32)).astype(bf16)
            deep, tall = self.hot_rows(lt, range(DEEP)), self.hot_rows(lt, range(DEEP, 8))
            seen = jnp.dot(
                jnp.concatenate([high, low], axis=1), jnp.concatenate([deep, deep], axis=0), preferred_element_type=f32
            )
            both = jnp.dot(jnp.concatenate([high, low], axis=0), tall, preferred_element_type=f32)
            seen = jnp.concatenate([seen, both[:64] + both[64:]], axis=1)
            total = jnp.zeros((8, LANES), f32)
            for c in range(8):
                own = jnp.broadcast_to(self.key_ref[lt, c : c + 1, :], (8, LANES))
                picked = jnp.zeros((8, LANES), f32)
                for i in range(8):
                    mask = own == (parity + 2 * i).astype(f32)
                    picked = jnp.where(mask, seen[8 * i : 8 * i + 8, c * LANES : (c + 1) * LANES], picked)
                total = total + picked * self.hat_ref[lt, c : c + 1, :]
            found_ref[lt] = total + pltpu.roll(total, 4, 0)
            return carry

        return one_group

    def spread(self, found_ref, result_ref):
        def one_group(t, carry):
            value = jnp.where(self.sub < 4, found_ref[t], found_ref[4 + t])
            for v in range(4):
                zero = jnp.broadcast_to(self.slots_ref[v, pl.ds(t, 1), :], (8, LANES))
                one = jnp.broadcast_to(self.slots_ref[v, pl.ds(4 + t, 1), :], (8, LANES))
                place = jnp.where(self.sub < 4, zero, one)
                taken = gather_lanes(value, jnp.maximum(place, 0))
                result_ref[t * 4 + v] += jnp.where(place >= 0, taken, 0.0)
            return carry

        return one_group


def passes_of(total):
    return (jnp.max(total) + (LANES - 1)) // LANES


def block_finder(ids_ref, other):
    mine = lax.axis_index("table")
    owner = mine * lax.axis_size("ray") + lax.axis_index("ray")
    parity = (mine + other) % 2

    def blocks(lt, slot):
        level, group = lt // 4, 2 * (lt % 4) + parity
        return level * 64 + ids_ref[(group * 2 + level) * 4 + slot, owner]

    return blocks


def gradients(half, grad_ref, blocks, ready):
    half.count(True)
    half.gather(0, True)
    ready()
    step = half.accumulate(grad_ref, blocks)
    each(8, step)
    passes = passes_of(half.total)

    def again(number, carry):
        half.gather(number, False)
        return lax.fori_loop(0, 8, step, carry)

    lax.fori_loop(1, passes, again, 0)

    @pl.when(passes > 1)
    def _():
        half.gather(0, False)

    return passes


def first_kernel(
    ids_hbm, recv_ref, m1_hbm,
    grad_ref, slots_ref, hat_ref, key_ref, column_ref, total_ref, m1_ref,
    ids_ref, corner_ref, aux_ref, cot_ref, sems,
):
    loads = start_all((ids_hbm, m1_hbm.at[pl.ds(0, 64)]), (ids_ref, m1_ref), sems)
    grad_ref[...] = jnp.zeros_like(grad_ref)
    half = Half(recv_ref, corner_ref, aux_ref, slots_ref, hat_ref, key_ref, column_ref, cot_ref)
    gradients(half, grad_ref, block_finder(ids_ref, 0), loads[0].wait)
    total_ref[...] = half.total
    wait_all(loads[1:])


def moments(grad, m1, m2):
    first = beta_one * m1 + (1.0 - beta_one) * grad
    second = beta_two * m2 + (1.0 - beta_two) * grad * grad
    return first, second


def stepped(table, first, second):
    return table - learn_rate * first / (jnp.sqrt(second) + adam_eps)


def second_kernel(
    ids_hbm, m1_hbm, m2_hbm, recv_ref, own_recv_ref, before_ref, table_ref, m1_zero_ref,
    own_slots_ref, own_hat_ref, own_key_ref, own_column_ref, own_total_ref,
    grad_ref, m2_ref, out_ref,
    ids_ref, m1_ref, corner_ref, aux_ref, slots_ref, hat_ref, key_ref, column_ref, cot_ref,
    found_ref, result_ref, sems,
):
    low, high = pl.ds(0, 64), pl.ds(64, 64)
    sources = (ids_hbm, m1_hbm.at[high], m2_hbm, m1_zero_ref)
    loads = start_all(sources, (ids_ref, m1_ref.at[high], m2_ref, m1_ref.at[low]), sems)
    grad_ref[...] = before_ref[...]
    result_ref[...] = jnp.zeros_like(result_ref)
    spare = (corner_ref, aux_ref, slots_ref, hat_ref, key_ref, column_ref, cot_ref)
    half = Half(recv_ref, *spare)
    blocks, own_blocks = block_finder(ids_ref, 1), block_finder(ids_ref, 0)
    passes = gradients(half, grad_ref, blocks, loads[0].wait)
    wait_all(loads[1:])

    def rows_at(block):
        first, second = moments(grad_ref[block], m1_ref[block], m2_ref[block])
        return stepped(table_ref[block], first, second)

    own = Half(own_recv_ref, corner_ref, aux_ref, own_slots_ref, own_hat_ref, own_key_ref, own_column_ref, cot_ref)
    results = [result_ref.at[pl.ds(0, 16)], result_ref.at[pl.ds(16, 16)]]
    for part, finder, result in ((own, own_blocks, results[0]), (half, blocks, results[1])):
        each(8, part.look(rows_at, found_ref, finder))
        each(4, part.spread(found_ref, result))

    def more_passes(part, finder, result, count):
        look, spread = part.look(rows_at, found_ref, finder), part.spread(found_ref, result)

        def again(number, carry):
            part.gather(number, False)
            lax.fori_loop(0, 8, look, 0)
            return lax.fori_loop(0, 4, spread, carry)

        lax.fori_loop(1, count, again, 0)

    more_passes(half, blocks, results[1], passes)
    own_passes = passes_of(own_total_ref[...])

    @pl.when(own_passes > 1)
    def _():
        again = Half(own_recv_ref, *spare)
        again.count(False)
        more_passes(again, own_blocks, results[0], own_passes)

    core = lax.axis_index("table") % 2
    for h in range(4):
        for v in range(4):
            out_ref[(2 * h + core) * 4 + v] = tile_blocks(result_ref[4 * h + v])
            out_ref[(2 * h + 1 - core) * 4 + v] = tile_blocks(result_ref[16 + 4 * h + v])


def third_kernel(grad_ref, m2_ref, m1_hbm, table_hbm, tnew_hbm, m1new_hbm, m2new_hbm, table_ref, m1_ref, m2new_ref, loads, stores):
    chunks = [pl.ds(32 * n, 32) for n in range(4)]
    arriving = []
    for n, chunk in enumerate(chunks):
        sources = [ref.at[chunk] for ref in (m1_hbm, table_hbm)]
        arriving.append(start_all(sources, [ref.at[chunk] for ref in (m1_ref, table_ref)], loads.at[n]))
    leaving = []
    for n, chunk in enumerate(chunks):
        wait_all(arriving[n])

        def update(step, carry):
            at = pl.ds(32 * n + step * 4, 4)
            first, second = moments(grad_ref[at], m1_ref[at], m2_ref[at])
            m1_ref[at] = first
            m2new_ref[at] = second
            table_ref[at] = stepped(table_ref[at], first, second)
            return carry

        lax.fori_loop(0, 8, update, 0)
        leaving += start_all(
            [ref.at[chunk] for ref in (table_ref, m1_ref, m2new_ref)],
            [ref.at[chunk] for ref in (tnew_hbm, m1new_hbm, m2new_hbm)],
            stores.at[n],
        )
    wait_all(leaving)


def network_kernel(recv_ref, win_ref, wout_ref, out_ref):
    columns = []
    for v in range(4):
        total = recv_ref[v]
        for t in range(1, 8):
            total = total + recv_ref[4 * t + v]
        columns.append(tile_blocks(total))
    encoded = jnp.concatenate(columns, axis=1)
    w_high, w_low = split_two(win_ref[...])
    e_high, e_low = split_two(encoded)
    hidden = lax.dot_general(
        jnp.concatenate([w_high, w_low, w_high], axis=0).astype(bf16),
        jnp.concatenate([e_high, e_high, e_low], axis=0).astype(bf16),
        (((0,), (0,)), ((), ())), preferred_element_type=f32,
    )
    h_high, h_low = split_two(jnp.maximum(hidden, 0.0))
    w_high, w_low = split_two(wout_ref[...])
    both = jnp.dot(
        jnp.concatenate([w_high, w_low], axis=0).astype(bf16), h_high.astype(bf16), preferred_element_type=f32
    )
    rest = jnp.dot(w_high.astype(bf16), h_low.astype(bf16), preferred_element_type=f32)
    out_ref[...] = both[:16] + both[16:] + rest


VMEM = pl.BlockSpec(memory_space=pltpu.VMEM)
HBM = pl.BlockSpec(memory_space=pltpu.HBM)


def call(kernel, outs, in_specs, scratch=(), out_specs=None, **extra):
    return pl.pallas_call(
        kernel,
        out_shape=[jax.ShapeDtypeStruct(*o) if isinstance(o, tuple) else o for o in outs],
        in_specs=in_specs,
        out_specs=[VMEM] * len(outs) if out_specs is None else out_specs,
        scratch_shapes=list(scratch),
        compiler_params=pltpu.CompilerParams(vmem_limit_bytes=VMEM_LIMIT),
        **extra,
    )


def in_hbm(*arrays):
    return [pltpu.with_memory_space_constraint(array, pltpu.HBM) for array in arrays]


def exchange(value, groups=None):
    return lax.all_to_all(
        value, ("table", "ray"), split_axis=0, concat_axis=0, tiled=True, axis_index_groups=groups
    )


def same_core():
    tables, rays = lax.axis_size("table"), lax.axis_size("ray")
    return [[t * rays + r for t in range(core, tables, 2) for r in range(rays)] for core in range(2)]


def swap_cores(value):
    return lax.ppermute(value, "table", [(t, t ^ 1) for t in range(lax.axis_size("table"))])


def rows_of(array):
    levels, blocks = array.shape[:2]
    return array.reshape(levels, blocks, 4, 4, LANES).transpose(0, 1, 3, 2, 4).reshape(levels * blocks, 16, LANES)


def rows_back(array, shape):
    levels, blocks = shape[:2]
    return array.reshape(levels, blocks, 4, 4, LANES).transpose(0, 1, 3, 2, 4).reshape(shape)


def on_device(
    table,
    moment1,
    moment2,
    block_ids,
    sample_slot,
    corners,
    fractions,
    feat_cot,
    weight_in,
    weight_out,
):
    (packed,) = call(
        pack_kernel,
        [((64, 8, LANES), f32)],
        [HBM] * 4,
        [
            pltpu.VMEM((2, 512), i32),
            pltpu.VMEM((2, 8, 512), i32),
            pltpu.VMEM((3, 2, 512), f32),
            pltpu.VMEM((2, 4, 512), f32),
            pltpu.SemaphoreType.DMA((4,)),
        ],
    )(*in_hbm(sample_slot, corners, fractions.transpose(1, 0, 2), feat_cot))
    samples = exchange(packed, same_core())
    others = swap_cores(samples)
    rows = (128, 16, LANES)
    (ids,) = in_hbm(block_ids.transpose(0, 1, 3, 2).reshape(64, 128))
    tile = pltpu.VMEM((8, 8, LANES), f32)
    lists = pltpu.VMEM((4, 8, LANES), i32)
    full = pltpu.VMEM(rows, f32)
    data = pltpu.VMEM((8, 4, 8, LANES), f32)
    id_table = pltpu.SMEM((64, LANES), i32)
    grad, slots, hat, key, column, total, m1 = call(
        first_kernel,
        [full, lists, tile, tile, tile, pltpu.VMEM((8, LANES), i32), pltpu.VMEM((64, 16, LANES), f32)],
        [HBM, VMEM, HBM],
        [id_table, data, data, tile, pltpu.SemaphoreType.DMA((2,))],
        cost_estimate=pl.CostEstimate(flops=1 << 30, bytes_accessed=4 << 20, transcendentals=0),
    )(ids, samples, *in_hbm(rows_of(moment1)))
    grad, m2, found = call(
        second_kernel,
        [full, full, ((32, 8, LANES), f32)],
        [HBM] * 3 + [VMEM] * 10,
        [
            id_table, full, data, data, lists, tile, tile, tile, tile, tile,
            pltpu.VMEM((32, 8, LANES), f32),
            pltpu.SemaphoreType.DMA((4,)),
        ],
    )(ids, *in_hbm(rows_of(moment1), rows_of(moment2)), others, samples, grad, rows_of(table), m1, slots, hat, key, column, total)
    back = exchange(found.reshape(128, 2, LANES)).reshape(32, 8, LANES)
    tnew, m1new, m2new = call(
        third_kernel,
        [(rows, f32)] * 3,
        [VMEM] * 2 + [HBM] * 2,
        [full, full, full, pltpu.SemaphoreType.DMA((4, 2)), pltpu.SemaphoreType.DMA((4, 3))],
        [HBM] * 3,
        cost_estimate=pl.CostEstimate(flops=20 << 20, bytes_accessed=7 << 20, transcendentals=0),
    )(grad, m2, *in_hbm(rows_of(moment1), rows_of(table)))
    (mlp_out,) = call(network_kernel, [((16, 512), f32)], [VMEM] * 3)(back, weight_in.T, weight_out)
    shape = table.shape
    return (rows_back(tnew, shape), rows_back(m1new, shape), rows_back(m2new, shape), mlp_out)


def solution(mesh):
    in_specs = (
        P(None, ("table", "ray"), None, None),
        P(None, ("table", "ray"), None, None),
        P(None, ("table", "ray"), None, None),
        P(),
        P(None, ("table", "ray")),
        P(None, None, ("table", "ray")),
        P(None, None, ("table", "ray")),
        P(None, None, ("table", "ray")),
        P(),
        P(),
    )
    out_specs = (
        P(None, ("table", "ray"), None, None),
        P(None, ("table", "ray"), None, None),
        P(None, ("table", "ray"), None, None),
        P(None, ("table", "ray")),
    )
    return jax.shard_map(
        on_device, mesh=mesh, in_specs=in_specs, out_specs=out_specs, check_vma=False
    )
```
